256 devices in a mesh: filt: 2 (over core), row: 4 (over x), col: 32 (over z, y).
Axes of the slice: x: 4, y: 4, z: 8, core: 2. Of those that a mesh axis runs over, the one named last changes fastest.
Arguments:
- particles: bfloat16 [24576, 256], P(('filt', 'row', 'col')), parts along dimension 0, may hold values from -6 to 6
- cotangent: bfloat16 [24576, 256], P(('filt', 'row', 'col')), parts along dimension 0, may hold values from -3 to 3
- row_potential: bfloat16 [24576], P(('filt', 'row', 'col')), parts along dimension 0, may hold values from -0.099609375 to 0.099609375
- col_potential: bfloat16 [24576], P(('filt', 'row', 'col')), parts along dimension 0, may hold values from -0.099609375 to 0.099609375
- weights: bfloat16 [24576], P(('filt', 'row', 'col')), parts along dimension 0, may hold values from 0.5 to 18
Outputs:
- grad_particles: bfloat16 [24576, 256], P(('filt', 'row', 'col')), parts along dimension 0
- grad_weights: float32 [24576], P(('filt', 'row', 'col')), parts along dimension 0
The draws below stay inside these ranges and needn't reach their ends.
There are 2 independent parts, one for each index of `filt`. The reference program is written for one: setup_inputs(seed, part) draws one part's arguments, and reference() takes and returns one part's arrays. A program takes and returns all parts, laid end to end along the dimension named above; each array names one. Nothing has to cross between parts.
All inputs are finite; a program needn't handle non-finite values.
Results may differ from the reference program's by a relative error of at most 0.02.
Values may be sent and summed in bfloat16 or wider, within the bound.
No kernel may reach another device: no remote copies, remote signals or barrier semaphores. Data moves between devices by JAX's collectives and lax.ppermute only.
A program may use at most 64 MiB of HBM per device.

```python
import math
import jax
import jax.numpy as jnp
from jax import lax

D = 256
ITERS = 4
PARTICLES = 12288


def draw_particles(key, part):
    groups = max(PARTICLES // 64, 1)
    key_member = jax.random.fold_in(key, 11)
    key_spot = jax.random.fold_in(key, 12)
    key_freq = jax.random.fold_in(key, 13)
    key_phase = jax.random.fold_in(key, 14)
    key_centre = jax.random.fold_in(key, 15)
    key_jitter = jax.random.fold_in(key, 16)
    member = jax.random.randint(key_member, (PARTICLES,), 0, groups)
    spot = jax.random.randint(key_spot, (PARTICLES,), 0, 32).astype(jnp.float32)
    freq = jax.random.uniform(key_freq, (groups, D), jnp.float32, 0.15, 0.42)
    phase = jax.random.uniform(key_phase, (groups, D), jnp.float32, -math.pi, math.pi)
    centre = jax.random.normal(key_centre, (groups, D), jnp.float32)
    jitter = jax.random.normal(key_jitter, (PARTICLES, D), jnp.float32)
    values = 0.8 * centre[member] + 1.2 * jnp.sin(freq[member] * spot[:, None] + phase[member]) + 0.15 * jitter
    return jnp.clip(values, -6.0, 6.0).astype(jnp.bfloat16)


def draw_weights(key, part):
    uniform_draw = jax.random.uniform(key, (PARTICLES,), jnp.float32, 0.0, 1.0)
    ramp = jnp.arange(PARTICLES, dtype=jnp.float32) / max(PARTICLES - 1, 1)
    values = jnp.exp(jnp.log(0.5) + uniform_draw * jnp.log(4.0)) * (1.0 + 2.0 * ramp)
    return values.astype(jnp.bfloat16)


def level_of(stream_key, extent, split, smallest, high):
    loudness = 1.0
    for axis_at, blocks in split:
        heights = jax.random.uniform(jax.random.fold_in(jax.random.fold_in(stream_key, 6), axis_at), (blocks,), jnp.float32, smallest / len(split), high / len(split))
        loudness = loudness * jnp.repeat(jnp.exp(heights), extent[axis_at] // blocks).reshape((-1,) + (1,) * (len(extent) - 1 - axis_at))
    return loudness


def normal_values(rng, dims, deviation, reach, split=(), kind=jnp.bfloat16):
    factor_of = level_of(rng, dims, split, -0.22, 0.18) if split else 1.0
    result = jax.random.normal(rng, dims, jnp.float32) * deviation * factor_of
    return jnp.minimum(jnp.maximum(result, -reach), reach).astype(kind)


def setup_inputs(seed: int = 0, part: int = 0) -> dict:
    streams_of = jax.random.split(jax.random.key(seed), 6)
    part_splits = jax.random.split(jax.random.fold_in(streams_of[5], part), 6)
    return {
        "particles": draw_particles(jax.random.fold_in(jax.random.fold_in(streams_of[5], part), 71), part),
        "cotangent": normal_values(part_splits[1], (PARTICLES, D), 0.5, 3.0, ((0, 128),)),
        "row_potential": jnp.clip(jax.random.uniform(part_splits[2], (PARTICLES,), jnp.float32, -0.099609375, 0.099609375) * level_of(part_splits[2], (PARTICLES,), ((0, 128),), -0.4, 0.0), -0.099609375, 0.099609375).astype(jnp.bfloat16),
        "col_potential": jnp.clip(jax.random.uniform(part_splits[3], (PARTICLES,), jnp.float32, -0.099609375, 0.099609375) * level_of(part_splits[3], (PARTICLES,), ((0, 128),), -0.4, 0.0), -0.099609375, 0.099609375).astype(jnp.bfloat16),
        "weights": draw_weights(jax.random.fold_in(jax.random.fold_in(streams_of[5], part), 71), part),
    }


EPS = 0.09


def plan_rows(part_blk, pot_blk, sq_blk, particles, sq_all, col_pot):
    cross = jnp.dot(part_blk, particles.T, preferred_element_type=jnp.float32)
    cost = (sq_blk[:, None] + sq_all[None, :] - 2.0 * cross) / (2.0 * D)
    return jnp.exp((pot_blk[:, None] + col_pot[None, :] - cost) / EPS)


def reference(particles, cotangent, row_potential, col_potential, weights):
    rsize = math.gcd(PARTICLES, 512)
    nblocks = PARTICLES // rsize
    pfloat = particles.astype(jnp.float32)
    sq_all = jnp.sum(pfloat * pfloat, axis=1)
    fpot = row_potential.astype(jnp.float32)
    gpot = col_potential.astype(jnp.float32)
    items = (particles.reshape(nblocks, rsize, D), fpot.reshape(nblocks, rsize), sq_all.reshape(nblocks, rsize))

    def first(carry, item):
        part_blk, pot_blk, sq_blk = item
        plan = plan_rows(part_blk, pot_blk, sq_blk, particles, sq_all, gpot)
        grads = jnp.dot(part_blk, cotangent.T, preferred_element_type=jnp.float32)
        weighted = plan * grads
        return (carry[0] + jnp.sum(plan, axis=0), carry[1] + jnp.sum(weighted, axis=0)), (jnp.sum(plan, axis=1), jnp.sum(weighted, axis=1))

    zeros_n = jnp.zeros((PARTICLES,), jnp.float32)
    (colmass, colph), (rowmass, rowph) = lax.scan(first, (zeros_n, zeros_n), items)
    psi = zeros_n
    phi = jnp.zeros((nblocks, rsize), jnp.float32)
    for step in range(ITERS):
        def sweep(acc, item):
            part_blk, pot_blk, sq_blk, mass_blk, ph_blk = item
            plan = plan_rows(part_blk, pot_blk, sq_blk, particles, sq_all, gpot)
            phi_blk = -(ph_blk + jnp.dot(plan, psi, precision=lax.Precision.HIGHEST)) / mass_blk
            return acc + jnp.dot(phi_blk, plan, precision=lax.Precision.HIGHEST), phi_blk

        accum, phi = lax.scan(sweep, zeros_n, items + (rowmass, rowph))
        psi = -(colph + accum) / colmass

    def last(acc, item):
        part_blk, pot_blk, sq_blk, phi_blk = item
        plan = plan_rows(part_blk, pot_blk, sq_blk, particles, sq_all, gpot)
        grads = jnp.dot(part_blk, cotangent.T, preferred_element_type=jnp.float32)
        mixed = plan * (grads + phi_blk[:, None] + psi[None, :])
        qrow = jnp.sum(mixed, axis=1)
        plan_bf = plan.astype(jnp.bfloat16)
        mixed_bf = mixed.astype(jnp.bfloat16)
        rowterm = jnp.dot(plan_bf, cotangent, preferred_element_type=jnp.float32)
        rowterm = rowterm + (jnp.dot(mixed_bf, particles, preferred_element_type=jnp.float32) - qrow[:, None] * part_blk.astype(jnp.float32)) / (D * EPS)
        return acc + jnp.dot(mixed_bf.T, part_blk, preferred_element_type=jnp.float32), rowterm

    colacc, rowterms = lax.scan(last, jnp.zeros((PARTICLES, D), jnp.float32), items + (phi,))
    grad_particles = (rowterms.reshape(PARTICLES, D) + colacc / (D * EPS)).astype(jnp.bfloat16)
    phi_flat = phi.reshape(PARTICLES)
    wfloat = weights.astype(jnp.float32)
    total = jnp.sum(wfloat)
    wphi = jnp.sum(wfloat * phi_flat)
    grad_weights = -(PARTICLES / total) * (phi_flat - wphi / total)
    return grad_particles, grad_weights
```

```python
import functools

import jax
import jax.numpy as jnp
from jax import lax
from jax.experimental import pallas as pl
from jax.experimental.pallas import tpu as pltpu
from jax.sharding import Mesh
from jax.sharding import PartitionSpec as P

ITERS = 4


EPS = 0.09

LANES = 128
AUX = 16
F32 = jnp.float32
BF16 = jnp.bfloat16


def params():
    return pltpu.CompilerParams(vmem_limit_bytes=40 << 20)


def whole(n):
    return [pl.BlockSpec(memory_space=pltpu.VMEM)] * n


def eye(own):
    rows = lax.broadcasted_iota(jnp.int32, (own, LANES), 0)
    lanes = lax.broadcasted_iota(jnp.int32, (own, LANES), 1)
    return rows == lanes


def to_row(col, own):
    return jnp.sum(jnp.where(eye(own), col, 0.0), axis=0, keepdims=True)


def to_col(row, own):
    return jnp.sum(jnp.where(eye(own), row, 0.0), axis=1, keepdims=True)


def lanes_of(col):
    out = []
    for k in range(col.shape[0] // LANES):
        out.append(to_row(col[k * LANES : (k + 1) * LANES], LANES))
    return jnp.concatenate(out, axis=1)


def fold(block):
    return jnp.sum(block.reshape(block.shape[0] // 8, 8, block.shape[1]), axis=0)


def put_lanes(ref, slots, base, row):
    for k in range(row.shape[1] // LANES):
        piece = row[:, k * LANES : (k + 1) * LANES]
        for s in range(slots):
            ref[s, base + k : base + k + 1, :] = piece


def build(own, width, isrc, jsrc, pi_ref, pj_ref, plan_ref, xi_ref, xj_ref, gj_ref, w_ref, mass_ref, col_ref):
    cols = jsrc * own
    scale = 1.0 / (2.0 * width * EPS)
    bias = []
    for s in range(jsrc):
        part = pj_ref[s, 0:own, :]
        xj_ref[s * own : (s + 1) * own, :] = part
        gj_ref[s * own : (s + 1) * own, :] = pj_ref[s, own : 2 * own, :]
        pf = part.astype(F32)
        sq = jnp.sum(pf * pf, axis=1, keepdims=True)
        pot = to_col(pj_ref[s, 2 * own : 2 * own + AUX, :].astype(F32)[0:1, 0:LANES], own)
        bias.append(pot / EPS - sq * scale)
    jbias = lanes_of(jnp.concatenate(bias, axis=0))
    xj = xj_ref[...]
    gj = gj_ref[...]

    def step(s, acc):
        part = pi_ref[s, 0:own, :]
        xi_ref[pl.ds(pl.multiple_of(s * own, own), own), :] = part
        aux = pi_ref[s, own : own + AUX, :].astype(F32)
        w_ref[pl.ds(s, 1), :] = aux[1:2, 0:LANES]
        pf = part.astype(F32)
        sq = jnp.sum(pf * pf, axis=1, keepdims=True)
        ibias = to_col(aux[0:1, 0:LANES], own) / EPS - sq * scale
        dims = (((1,), (1,)), ((), ()))
        cross = lax.dot_general(part, xj, dims, preferred_element_type=F32)
        inner = lax.dot_general(part, gj, dims, preferred_element_type=F32)
        plan = jnp.exp(cross * (2.0 * scale) + jbias + ibias)
        plan_ref[pl.ds(pl.multiple_of(s * own, own), own), :] = plan
        weighted = plan * inner
        mass = to_row(jnp.sum(plan, axis=1, keepdims=True), own)
        ph = to_row(jnp.sum(weighted, axis=1, keepdims=True), own)
        mass_ref[0, pl.ds(s, 1), :] = mass
        mass_ref[0, pl.ds(isrc + s, 1), :] = ph
        return acc[0] + fold(plan), acc[1] + fold(weighted)

    zero = jnp.zeros((8, cols), F32)
    cmass, cph = lax.fori_loop(0, isrc, step, (zero, zero))
    for s in range(1, isrc):
        mass_ref[s] = mass_ref[0]
    col_ref[...] = jnp.zeros_like(col_ref)
    cmass = jnp.sum(cmass, axis=0, keepdims=True)
    cph = jnp.sum(cph, axis=0, keepdims=True)
    for k in range(cols // LANES):
        col_ref[k : k + 1, :] = cmass[:, k * LANES : (k + 1) * LANES]
        col_ref[8 + k : 9 + k, :] = cph[:, k * LANES : (k + 1) * LANES]


def apply_cols(own, isrc, phi_ref, plan_ref):
    cols = plan_ref.shape[1]

    def step(s, acc):
        col = to_col(phi_ref[pl.ds(s, 1), :], own)
        block = plan_ref[pl.ds(pl.multiple_of(s * own, own), own), :]
        return acc + fold(block * col)

    acc = lax.fori_loop(0, isrc, step, jnp.zeros((8, cols), F32))
    return jnp.sum(acc, axis=0, keepdims=True)


def valid(own, value):
    lanes = lax.broadcasted_iota(jnp.int32, value.shape, 1)
    return jnp.where(lanes < own, value, 0.0)


def phi_first(own, isrc, jsrc, got_ref, col_ref, plan_ref, mass_ref, phi_ref, send_ref):
    total = jnp.sum(got_ref[...], axis=0)
    mass_ref[...] = total
    phi_ref[...] = valid(own, -total[isrc:] / total[:isrc])
    applied = apply_cols(own, isrc, phi_ref, plan_ref)
    for s in range(jsrc):
        send_ref[s, 0:16, :] = col_ref[...]
        send_ref[s, 16:24, :] = jnp.zeros((8, LANES), F32)
    put_lanes(send_ref, jsrc, 16, applied)


def phi_next(own, isrc, jsrc, got_ref, mass_ref, w_ref, plan_ref, phi_ref, send_ref):
    total = jnp.sum(got_ref[...], axis=0)
    mass = mass_ref[...]
    phi = valid(own, -(mass[isrc:] + total) / mass[:isrc])
    phi_ref[...] = phi
    applied = apply_cols(own, isrc, phi_ref, plan_ref)
    wts = valid(own, w_ref[...])
    wsum = jnp.sum(wts, axis=0, keepdims=True)
    wphi = jnp.sum(wts * phi, axis=0, keepdims=True)
    for s in range(jsrc):
        send_ref[s, 6:7, :] = wsum
        send_ref[s, 7:8, :] = wphi
    put_lanes(send_ref, jsrc, 0, applied)


def row_of(value, count):
    return jnp.concatenate([value[k : k + 1, :] for k in range(count)], axis=1)


def apply_rows(own, isrc, psi, plan_ref, send_ref):
    def step(s, carry):
        block = plan_ref[pl.ds(pl.multiple_of(s * own, own), own), :]
        col = jnp.sum(block * psi, axis=1, keepdims=True)
        send_ref[0, pl.ds(s, 1), :] = to_row(col, own)
        return carry

    lax.fori_loop(0, isrc, step, 0)
    for s in range(1, isrc):
        send_ref[s] = send_ref[0]


def psi_first(own, isrc, got_ref, plan_ref, col_ref, send_ref):
    total = jnp.sum(got_ref[...], axis=0)
    col_ref[...] = total[:16]
    count = plan_ref.shape[1] // LANES
    psi = row_of(-(total[8:16] + total[16:24]) / total[0:8], count)
    apply_rows(own, isrc, psi, plan_ref, send_ref)


def psi_next(own, isrc, got_ref, col_ref, plan_ref, send_ref):
    total = jnp.sum(got_ref[...], axis=0)
    count = plan_ref.shape[1] // LANES
    psi = row_of(-(col_ref[8:16] + total) / col_ref[0:8], count)
    apply_rows(own, isrc, psi, plan_ref, send_ref)


def finish(own, width, isrc, jsrc, every, got_ref, col_ref, phi_ref, plan_ref, xi_ref, xj_ref, gj_ref, row_ref, out_ref, gw_ref, acc_ref):
    total = jnp.sum(got_ref[...], axis=0)
    count = plan_ref.shape[1] // LANES
    psi = row_of(-(col_ref[8:16] + total) / col_ref[0:8], count)
    wsum = jnp.sum(total[6:7], axis=1, keepdims=True)
    wphi = jnp.sum(total[7:8], axis=1, keepdims=True)
    gw_ref[...] = -(every / wsum) * (phi_ref[...] - wphi / wsum)
    xj = xj_ref[...]
    gj = gj_ref[...]
    scale = 1.0 / (width * EPS)
    acc_ref[...] = jnp.zeros_like(acc_ref)

    def step(s, carry):
        part = xi_ref[pl.ds(pl.multiple_of(s * own, own), own), :]
        plan = plan_ref[pl.ds(pl.multiple_of(s * own, own), own), :]
        col = to_col(phi_ref[pl.ds(s, 1), :], own)
        inner = lax.dot_general(part, gj, (((1,), (1,)), ((), ())), preferred_element_type=F32)
        mixed = plan * (inner + (col + psi))
        qrow = jnp.sum(mixed, axis=1, keepdims=True)
        mixed_bf = mixed.astype(BF16)
        term = jnp.dot(plan.astype(BF16), gj, preferred_element_type=F32)
        term += (jnp.dot(mixed_bf, xj, preferred_element_type=F32) - qrow * part.astype(F32)) * scale
        row_ref[s] = term.astype(BF16)
        acc_ref[...] += lax.dot_general(mixed_bf, part, (((0,), (0,)), ((), ())), preferred_element_type=F32)
        return carry

    lax.fori_loop(0, isrc, step, 0)
    for s in range(jsrc):
        out_ref[s] = (acc_ref[s * own : (s + 1) * own, :] * scale).astype(BF16)


def local(particles, cotangent, row_potential, col_potential, weights):
    own, width = particles.shape
    iaxes, jaxes = ("row", "y"), ("z",)
    isrc = lax.axis_size("row") * lax.axis_size("y")
    jsrc = lax.axis_size("z")
    rows, cols = isrc * own, jsrc * own

    def swap(value, axes):
        return lax.all_to_all(value, axes, 0, 0, tiled=True)

    def aux(*vectors):
        block = jnp.stack([jnp.pad(v, (0, width - own)) for v in vectors])
        return jnp.pad(block, ((0, AUX - len(vectors)), (0, 0)))

    ipack = jnp.concatenate([particles, aux(row_potential, weights)], axis=0)
    jpack = jnp.concatenate([particles, cotangent, aux(col_potential)], axis=0)
    igot = swap(jnp.broadcast_to(ipack, (isrc,) + ipack.shape), iaxes)
    jgot = swap(jnp.broadcast_to(jpack, (jsrc,) + jpack.shape), jaxes)

    def call(body, outs, *args, scratch=()):
        return pl.pallas_call(
            body,
            out_shape=[jax.ShapeDtypeStruct(s, d) for s, d in outs],
            in_specs=whole(len(args)),
            out_specs=whole(len(outs)),
            scratch_shapes=list(scratch),
            compiler_params=params(),
        )(*args)

    plan, xi, xj, gj, wts, mass_send, col_part = call(
        functools.partial(build, own, width, isrc, jsrc),
        [
            ((rows, cols), F32),
            ((rows, width), BF16),
            ((cols, width), BF16),
            ((cols, width), BF16),
            ((isrc, LANES), F32),
            ((isrc, 2 * isrc, LANES), F32),
            ((16, LANES), F32),
        ],
        igot,
        jgot,
    )
    got = swap(mass_send, iaxes)
    mass, phi, send = call(
        functools.partial(phi_first, own, isrc, jsrc),
        [((2 * isrc, LANES), F32), ((isrc, LANES), F32), ((jsrc, 24, LANES), F32)],
        got,
        col_part,
        plan,
    )
    got = swap(send, jaxes)
    col, send = call(
        functools.partial(psi_first, own, isrc),
        [((16, LANES), F32), ((isrc, isrc, LANES), F32)],
        got,
        plan,
    )
    for step in range(1, ITERS):
        got = swap(send, iaxes)
        phi, send = call(
            functools.partial(phi_next, own, isrc, jsrc),
            [((isrc, LANES), F32), ((jsrc, 8, LANES), F32)],
            got,
            mass,
            wts,
            plan,
        )
        got = swap(send, jaxes)
        if step < ITERS - 1:
            (send,) = call(
                functools.partial(psi_next, own, isrc),
                [((isrc, isrc, LANES), F32)],
                got,
                col,
                plan,
            )
    row_send, col_send, gw = call(
        functools.partial(finish, own, width, isrc, jsrc, float(isrc * jsrc * own)),
        [
            ((isrc, own, width), BF16),
            ((jsrc, own, width), BF16),
            ((isrc, LANES), F32),
        ],
        got,
        col,
        phi,
        plan,
        xi,
        xj,
        gj,
        scratch=[pltpu.VMEM((cols, width), F32)],
    )
    row_got = swap(row_send, iaxes)
    col_got = swap(col_send, jaxes)
    grad = jnp.sum(row_got.astype(F32), axis=0) + jnp.sum(col_got.astype(F32), axis=0)
    mine = lax.axis_index("row") * lax.axis_size("y") + lax.axis_index("y")
    grad_weights = lax.dynamic_slice(gw, (mine, 0), (1, own)).reshape(own)
    return (grad.astype(BF16), grad_weights)


def solution(mesh):
    filt, row, col = mesh.devices.shape
    split = Mesh(mesh.devices.reshape(filt, row, 8, col // 8), ("filt", "row", "z", "y"))
    spec = ("filt", "row", "z", "y")
    return jax.shard_map(
        local,
        mesh=split,
        in_specs=(P(spec, None), P(spec, None), P(spec), P(spec), P(spec)),
        out_specs=(P(spec, None), P(spec)),
        check_vma=False,
    )
```

```python
import functools

import jax
import jax.numpy as jnp
from jax import lax
from jax.experimental import pallas as pl
from jax.experimental.pallas import tpu as pltpu
from jax.sharding import Mesh
from jax.sharding import PartitionSpec as P

ITERS = 4


EPS = 0.09

LANES = 128
AUX = 16
F32 = jnp.float32
BF16 = jnp.bfloat16


def params():
    return pltpu.CompilerParams(vmem_limit_bytes=4 << 20)


def whole(n):
    return [pl.BlockSpec(memory_space=pltpu.VMEM)] * n


def eye(own):
    rows = lax.broadcasted_iota(jnp.int32, (own, LANES), 0)
    lanes = lax.broadcasted_iota(jnp.int32, (own, LANES), 1)
    return rows == lanes


def to_row(col, own):
    return jnp.sum(jnp.where(eye(own), col, 0.0), axis=0, keepdims=True)


def to_col(row, own):
    return jnp.sum(jnp.where(eye(own), row, 0.0), axis=1, keepdims=True)


def lanes_of(col):
    out = []
    for k in range(col.shape[0] // LANES):
        out.append(to_row(col[k * LANES : (k + 1) * LANES], LANES))
    return jnp.concatenate(out, axis=1)


def slots_of(value, own, count):
    return jnp.concatenate([to_row(value[k * own : (k + 1) * own], own) for k in range(count)], axis=0)


def column_of(value, own, count):
    return jnp.concatenate([to_col(value[k : k + 1], own) for k in range(count)], axis=0)


def fold(block):
    return jnp.sum(block.reshape(block.shape[0] // 8, 8, block.shape[1]), axis=0)


def put_lanes(ref, slots, base, row):
    for k in range(row.shape[1] // LANES):
        piece = row[:, k * LANES : (k + 1) * LANES]
        for s in range(slots):
            ref[s, base + k : base + k + 1, :] = piece


def pack(own, width, isrc, x_ref, gy_ref, f_ref, g_ref, w_ref, ipack_ref, jpack_ref, line_ref):
    line_ref[...] = jnp.zeros_like(line_ref)
    line_ref[0:1, 0:own] = f_ref[...].astype(F32)
    line_ref[1:2, 0:own] = w_ref[...].astype(F32)
    x = x_ref[...]
    lines = line_ref[...].astype(BF16)
    for s in range(isrc):
        ipack_ref[s, 0:own, :] = x
        ipack_ref[s, own : own + AUX, :] = lines
    jpack_ref[0:own, :] = x
    jpack_ref[own : 2 * own, :] = gy_ref[...]
    line_ref[0:1, 0:own] = g_ref[...].astype(F32)
    jpack_ref[2 * own : 2 * own + AUX, :] = line_ref[...].astype(BF16)


GROUP = 4
NT = (((1,), (1,)), ((), ()))
TN = (((0,), (0,)), ((), ()))


def behind(k, count):
    me = lax.axis_index("z")
    return lax.rem(me + count - k, count)


def ahead(k, count):
    return lax.rem(lax.axis_index("z") + k, count)


def build(own, width, isrc, jsrc, *refs):
    pi_ref, pj_refs = refs[0], refs[1 : 1 + jsrc]
    plan_ref, xi_ref, xj_ref, gj_ref, w_ref, mass_ref, col_ref, bias_ref = refs[1 + jsrc :]
    cols = jsrc * own
    scale = 1.0 / (2.0 * width * EPS)
    for k in range(jsrc):
        src = pj_refs[k]
        place = pl.ds(pl.multiple_of(behind(k, jsrc) * own, own), own)
        part = src[0:own, :]
        xj_ref[place, :] = part
        gj_ref[place, :] = src[own : 2 * own, :]
        pf = part.astype(F32)
        sq = jnp.sum(pf * pf, axis=1, keepdims=True)
        pot = to_col(src[2 * own : 2 * own + AUX, :].astype(F32)[0:1, 0:LANES], own)
        bias_ref[place, :] = pot / EPS - sq * scale
    jbias = lanes_of(bias_ref[...])
    xj = xj_ref[...]
    gj = gj_ref[...]
    span = GROUP * own

    def step(t, acc):
        base = pl.multiple_of(t * span, span)
        ibias = []
        for k in range(GROUP):
            s = t * GROUP + k
            part = pi_ref[s, 0:own, :]
            xi_ref[pl.ds(pl.multiple_of(base + k * own, own), own), :] = part
            aux = pi_ref[s, own : own + AUX, :].astype(F32)
            w_ref[pl.ds(s, 1), :] = aux[1:2, 0:LANES]
            pf = part.astype(F32)
            sq = jnp.sum(pf * pf, axis=1, keepdims=True)
            ibias.append(to_col(aux[0:1, 0:LANES], own) / EPS - sq * scale)
        ibias = jnp.concatenate(ibias, axis=0)
        part = xi_ref[pl.ds(base, span), :]
        cross = lax.dot_general(part, xj, NT, preferred_element_type=F32)
        plan = jnp.exp(cross * (2.0 * scale) + jbias + ibias)
        plan_ref[pl.ds(base, span), :] = plan
        weighted = plan * lax.dot_general(part, gj, NT, preferred_element_type=F32)
        mass = slots_of(jnp.sum(plan, axis=1, keepdims=True), own, GROUP)
        ph = slots_of(jnp.sum(weighted, axis=1, keepdims=True), own, GROUP)
        for k in range(GROUP):
            mass_ref[0, pl.ds(t * GROUP + k, 1), :] = mass[k : k + 1]
            mass_ref[0, pl.ds(isrc + t * GROUP + k, 1), :] = ph[k : k + 1]
        return acc[0] + fold(plan), acc[1] + fold(weighted)

    zero = jnp.zeros((8, cols), F32)
    cmass, cph = lax.fori_loop(0, isrc // GROUP, step, (zero, zero))
    for s in range(1, isrc):
        mass_ref[s] = mass_ref[0]
    col_ref[...] = jnp.zeros_like(col_ref)
    cmass = jnp.sum(cmass, axis=0, keepdims=True)
    cph = jnp.sum(cph, axis=0, keepdims=True)
    for k in range(cols // LANES):
        col_ref[k : k + 1, :] = cmass[:, k * LANES : (k + 1) * LANES]
        col_ref[8 + k : 9 + k, :] = cph[:, k * LANES : (k + 1) * LANES]


def prepare(own, isrc, plan_ref, xi_ref, gj_ref, base_ref, inner_ref):
    gj = gj_ref[...]
    span = GROUP * own

    def step(t, carry):
        at = pl.ds(pl.multiple_of(t * span, span), span)
        inner_ref[at, :] = lax.dot_general(xi_ref[at, :], gj, NT, preferred_element_type=F32)
        base_ref[at, :] = jnp.dot(plan_ref[at, :].astype(BF16), gj, preferred_element_type=F32)
        return carry

    lax.fori_loop(0, isrc // GROUP, step, 0)


def apply_cols(own, isrc, phi, plan_ref):
    span = GROUP * own
    acc = None
    for t in range(isrc // GROUP):
        col = column_of(phi[t * GROUP : (t + 1) * GROUP], own, GROUP)
        part = fold(plan_ref[t * span : (t + 1) * span, :] * col)
        acc = part if acc is None else acc + part
    return jnp.sum(acc, axis=0, keepdims=True)


def valid(own, value):
    lanes = lax.broadcasted_iota(jnp.int32, value.shape, 1)
    return jnp.where(lanes < own, value, 0.0)


def phi_first(own, isrc, jsrc, got_ref, col_ref, plan_ref, mass_ref, send_ref):
    total = jnp.sum(got_ref[...], axis=0)
    mass_ref[...] = total
    phi = valid(own, -total[isrc:] / total[:isrc])
    applied = apply_cols(own, isrc, phi, plan_ref)
    for s in range(jsrc):
        send_ref[s, 0:16, :] = col_ref[...]
        send_ref[s, 16:24, :] = jnp.zeros((8, LANES), F32)
    put_lanes(send_ref, jsrc, 16, applied)


def phi_next(own, isrc, jsrc, got_ref, mass_ref, w_ref, plan_ref, phi_ref, send_ref):
    total = jnp.sum(got_ref[...], axis=0)
    mass = mass_ref[...]
    phi = valid(own, -(mass[isrc:] + total) / mass[:isrc])
    phi_ref[...] = phi
    applied = apply_cols(own, isrc, phi, plan_ref)
    wts = valid(own, w_ref[...])
    wsum = jnp.sum(wts, axis=0, keepdims=True)
    wphi = jnp.sum(wts * phi, axis=0, keepdims=True)
    for s in range(jsrc):
        send_ref[s, 6:7, :] = wsum
        send_ref[s, 7:8, :] = wphi
    put_lanes(send_ref, jsrc, 0, applied)


def row_of(value, count):
    return jnp.concatenate([value[k : k + 1, :] for k in range(count)], axis=1)


def apply_rows(own, isrc, psi, plan_ref, send_ref):
    span = GROUP * own
    for t in range(isrc // GROUP):
        col = jnp.sum(plan_ref[t * span : (t + 1) * span, :] * psi, axis=1, keepdims=True)
        part = slots_of(col, own, GROUP)
        for s in range(isrc):
            send_ref[s, t * GROUP : (t + 1) * GROUP, :] = part


def psi_first(own, isrc, got_ref, plan_ref, col_ref, send_ref):
    total = jnp.sum(got_ref[...], axis=0)
    col_ref[...] = total[:16]
    count = plan_ref.shape[1] // LANES
    psi = row_of(-(total[8:16] + total[16:24]) / total[0:8], count)
    apply_rows(own, isrc, psi, plan_ref, send_ref)


def psi_next(own, isrc, got_ref, col_ref, plan_ref, send_ref):
    total = jnp.sum(got_ref[...], axis=0)
    count = plan_ref.shape[1] // LANES
    psi = row_of(-(col_ref[8:16] + total) / col_ref[0:8], count)
    apply_rows(own, isrc, psi, plan_ref, send_ref)


def finish_cols(own, width, isrc, jsrc, every, *refs):
    got_ref, col_ref, phi_ref, plan_ref, inner_ref, xi_ref = refs[:6]
    mixed_ref, q_ref, gw_ref = refs[6:9]
    out_refs, acc_ref = refs[9 : 9 + jsrc], refs[9 + jsrc]
    total = jnp.sum(got_ref[...], axis=0)
    count = plan_ref.shape[1] // LANES
    psi = row_of(-(col_ref[8:16] + total) / col_ref[0:8], count)
    wsum = jnp.sum(total[6:7], axis=1, keepdims=True)
    wphi = jnp.sum(total[7:8], axis=1, keepdims=True)
    gw_ref[...] = -(every / wsum) * (phi_ref[...] - wphi / wsum)
    span = GROUP * own
    for t in range(isrc // GROUP):
        at = slice(t * span, (t + 1) * span)
        col = column_of(phi_ref[t * GROUP : (t + 1) * GROUP, :], own, GROUP)
        mixed = plan_ref[at, :] * (inner_ref[at, :] + (col + psi))
        q_ref[at, :] = jnp.sum(mixed, axis=1, keepdims=True)
        mixed = mixed.astype(BF16)
        mixed_ref[at, :] = mixed
        term = lax.dot_general(mixed, xi_ref[at, :], TN, preferred_element_type=F32)
        if t:
            term = acc_ref[...] + term
        acc_ref[...] = term
    scale = 1.0 / (width * EPS)
    for k in range(jsrc):
        place = pl.ds(pl.multiple_of(ahead(k, jsrc) * own, own), own)
        out_refs[k][...] = (acc_ref[place, :] * scale).astype(BF16)


def finish_rows(own, width, isrc, base_ref, mixed_ref, q_ref, xi_ref, xj_ref, row_ref):
    scale = 1.0 / (width * EPS)
    span = GROUP * own
    xj = xj_ref[...]
    for t in range(isrc // GROUP):
        at = slice(t * span, (t + 1) * span)
        term = jnp.dot(mixed_ref[at, :], xj, preferred_element_type=F32)
        term = base_ref[at, :] + (term - q_ref[at, :] * xi_ref[at, :].astype(F32)) * scale
        term = term.astype(BF16)
        for k in range(GROUP):
            row_ref[t * GROUP + k] = term[k * own : (k + 1) * own]


def total_up(jsrc, *refs):
    rows_ref, parts, out_ref = refs[0], refs[1 : 1 + jsrc], refs[1 + jsrc]
    acc = jnp.sum(rows_ref[...].astype(F32), axis=0)
    for part in parts:
        acc += part[...].astype(F32)
    out_ref[...] = acc.astype(BF16)


def local(particles, cotangent, row_potential, col_potential, weights):
    own, width = particles.shape
    iaxes, jaxes = ("row", "y"), ("z",)
    isrc = lax.axis_size("row") * lax.axis_size("y")
    jsrc = lax.axis_size("z")
    rows, cols = isrc * own, jsrc * own
    far = sorted(range(1, jsrc), key=lambda k: -min(k, jsrc - k))

    def swap(value, axes):
        return lax.all_to_all(value, axes, 0, 0, tiled=True)

    def shift(value, k):
        return lax.ppermute(value, "z", [(i, (i + k) % jsrc) for i in range(jsrc)])

    def call(body, micros, outs, *args, scratch=()):
        return pl.pallas_call(
            body,
            out_shape=[jax.ShapeDtypeStruct(s, d) for s, d in outs],
            in_specs=whole(len(args)),
            out_specs=whole(len(outs)),
            scratch_shapes=list(scratch),
            compiler_params=params(),
            cost_estimate=pl.CostEstimate(flops=int(micros * 1e9), bytes_accessed=1024, transcendentals=0),
        )(*args)

    ipack, jpack = call(
        functools.partial(pack, own, width, isrc),
        2,
        [((isrc, own + AUX, width), BF16), ((2 * own + AUX, width), BF16)],
        particles,
        cotangent,
        row_potential.reshape(1, own),
        col_potential.reshape(1, own),
        weights.reshape(1, own),
        scratch=[pltpu.VMEM((AUX, width), F32)],
    )
    jgot = {k: shift(jpack, k) for k in far}
    igot = swap(ipack, iaxes)
    plan, xi, xj, gj, wts, send, col_part = call(
        functools.partial(build, own, width, isrc, jsrc),
        8,
        [
            ((rows, cols), F32),
            ((rows, width), BF16),
            ((cols, width), BF16),
            ((cols, width), BF16),
            ((isrc, LANES), F32),
            ((isrc, 2 * isrc, LANES), F32),
            ((16, LANES), F32),
        ],
        igot,
        jpack,
        *[jgot[k] for k in range(1, jsrc)],
        scratch=[pltpu.VMEM((cols, 1), F32)],
    )
    got = swap(send, iaxes)
    base, inner = call(
        functools.partial(prepare, own, isrc),
        4,
        [((rows, width), F32), ((rows, cols), F32)],
        plan,
        xi,
        gj,
    )
    mass, send = call(
        functools.partial(phi_first, own, isrc, jsrc),
        2,
        [((2 * isrc, LANES), F32), ((jsrc, 24, LANES), F32)],
        got,
        col_part,
        plan,
    )
    got = swap(send, jaxes)
    col, send = call(
        functools.partial(psi_first, own, isrc),
        2,
        [((16, LANES), F32), ((isrc, isrc, LANES), F32)],
        got,
        plan,
    )
    for step in range(1, ITERS):
        got = swap(send, iaxes)
        phi, send = call(
            functools.partial(phi_next, own, isrc, jsrc),
            2,
            [((isrc, LANES), F32), ((jsrc, 8, LANES), F32)],
            got,
            mass,
            wts,
            plan,
        )
        got = swap(send, jaxes)
        if step < ITERS - 1:
            (send,) = call(
                functools.partial(psi_next, own, isrc),
                2,
                [((isrc, isrc, LANES), F32)],
                got,
                col,
                plan,
            )
    mixed, q, gw, *col_sends = call(
        functools.partial(finish_cols, own, width, isrc, jsrc, float(isrc * jsrc * own)),
        5,
        [((rows, cols), BF16), ((rows, 1), F32), ((isrc, LANES), F32)] + [((own, width), BF16)] * jsrc,
        got,
        col,
        phi,
        plan,
        inner,
        xi,
        scratch=[pltpu.VMEM((cols, width), F32)],
    )
    col_got = [col_sends[0]] + [shift(col_sends[k], k) for k in far]
    (row_send,) = call(
        functools.partial(finish_rows, own, width, isrc),
        3,
        [((isrc, own, width), BF16)],
        base,
        mixed,
        q,
        xi,
        xj,
    )
    row_got = swap(row_send, iaxes)
    (grad,) = call(functools.partial(total_up, jsrc), 1, [((own, width), BF16)], row_got, *col_got)
    mine = lax.axis_index("row") * lax.axis_size("y") + lax.axis_index("y")
    grad_weights = lax.dynamic_slice(gw, (mine, 0), (1, own)).reshape(own)
    return (grad, grad_weights)


def solution(mesh):
    filt, row, col = mesh.devices.shape
    split = Mesh(mesh.devices.reshape(filt, row, 8, col // 8), ("filt", "row", "z", "y"))
    spec = ("filt", "row", "z", "y")
    return jax.shard_map(
        local,
        mesh=split,
        in_specs=(P(spec, None), P(spec, None), P(spec), P(spec), P(spec)),
        out_specs=(P(spec, None), P(spec)),
        check_vma=False,
    )
```

```python
import functools

import jax
import jax.numpy as jnp
from jax import lax
from jax.experimental import pallas as pl
from jax.experimental.pallas import tpu as pltpu
from jax.sharding import Mesh
from jax.sharding import PartitionSpec as P

ITERS = 4


EPS = 0.09

LANES = 128
AUX = 16
F32 = jnp.float32
BF16 = jnp.bfloat16


def params():
    return pltpu.CompilerParams(vmem_limit_bytes=12 << 20)


def whole(n):
    return [pl.BlockSpec(memory_space=pltpu.VMEM)] * n


def eye(own):
    rows = lax.broadcasted_iota(jnp.int32, (own, LANES), 0)
    lanes = lax.broadcasted_iota(jnp.int32, (own, LANES), 1)
    return rows == lanes


def to_row(col, own):
    return jnp.sum(jnp.where(eye(own), col, 0.0), axis=0, keepdims=True)


def to_col(row, own):
    return jnp.sum(jnp.where(eye(own), row, 0.0), axis=1, keepdims=True)


def lanes_of(col):
    out = []
    for k in range(col.shape[0] // LANES):
        out.append(to_row(col[k * LANES : (k + 1) * LANES], LANES))
    return jnp.concatenate(out, axis=1)


def slots_of(value, own, count):
    return jnp.concatenate([to_row(value[k * own : (k + 1) * own], own) for k in range(count)], axis=0)


def column_of(value, own, count):
    return jnp.concatenate([to_col(value[k : k + 1], own) for k in range(count)], axis=0)


def fold(block):
    return jnp.sum(block.reshape(block.shape[0] // 8, 8, block.shape[1]), axis=0)


def put_lanes(ref, slots, base, row):
    for k in range(row.shape[1] // LANES):
        piece = row[:, k * LANES : (k + 1) * LANES]
        for s in range(slots):
            ref[s, base + k : base + k + 1, :] = piece


def pack(own, width, jsrc, x_ref, gy_ref, f_ref, g_ref, w_ref, ipack_ref, jpack_ref, block_ref, line_ref, vec_ref, in_sem, out_sem):
    copies = [
        pltpu.make_async_copy(f_ref, vec_ref.at[0], in_sem.at[2]),
        pltpu.make_async_copy(w_ref, vec_ref.at[1], in_sem.at[3]),
        pltpu.make_async_copy(g_ref, vec_ref.at[2], in_sem.at[4]),
        pltpu.make_async_copy(x_ref, block_ref.at[pl.ds(0, own)], in_sem.at[0]),
        pltpu.make_async_copy(gy_ref, block_ref.at[pl.ds(own, own)], in_sem.at[1]),
    ]
    for copy in copies:
        copy.start()
    line_ref[...] = jnp.zeros_like(line_ref)
    for copy in copies:
        copy.wait()
    line_ref[0, 0:1, 0:own] = vec_ref[0].astype(F32)
    line_ref[0, 1:2, 0:own] = vec_ref[1].astype(F32)
    line_ref[1, 0:1, 0:own] = vec_ref[2].astype(F32)
    block_ref[2 * own : 2 * own + AUX, :] = line_ref[1].astype(BF16)
    outs = [pltpu.make_async_copy(block_ref, jpack_ref.at[s], out_sem.at[s]) for s in range(jsrc)]
    for copy in outs:
        copy.start()
    ipack_ref[0:own, :] = block_ref[0:own, :]
    ipack_ref[own : own + AUX, :] = line_ref[0].astype(BF16)
    for copy in outs:
        copy.wait()


def stack(own, count, *refs):
    out_ref = refs[count]
    size = own + AUX
    for k in range(count):
        place = behind("row", k, count)
        out_ref[pl.ds(pl.multiple_of(place * size, size), size), :] = refs[k][...]


GROUP = 4
NT = (((1,), (1,)), ((), ()))
TN = (((0,), (0,)), ((), ()))


def behind(axis, k, count):
    return lax.rem(lax.axis_index(axis) + (count - k), count)


def build(own, width, isrc, jsrc, *refs):
    steps = isrc // GROUP
    pi_refs, pj_ref = refs[:steps], refs[steps]
    plan_ref, inner_ref, xi_ref, xj_ref, gj_ref, w_ref, mass_ref, col_ref = refs[steps + 1 :]
    cols = jsrc * own
    size = own + AUX
    scale = 1.0 / (2.0 * width * EPS)
    bias = []
    for k in range(jsrc):
        part = pj_ref[k, 0:own, :]
        xj_ref[k * own : (k + 1) * own, :] = part
        gj_ref[k * own : (k + 1) * own, :] = pj_ref[k, own : 2 * own, :]
        pf = part.astype(F32)
        sq = jnp.sum(pf * pf, axis=1, keepdims=True)
        pot = to_col(pj_ref[k, 2 * own : 2 * own + AUX, :].astype(F32)[0:1, 0:LANES], own)
        bias.append(pot / EPS - sq * scale)
    jbias = lanes_of(jnp.concatenate(bias, axis=0))
    xj = xj_ref[...]
    gj = gj_ref[...]
    span = GROUP * own
    cmass = cph = None
    for m in range(steps):
        src = pi_refs[m]
        t = behind("y", m, steps)
        base = pl.multiple_of(t * span, span)
        first = pl.multiple_of(t * GROUP, GROUP)
        ibias = []
        for k in range(GROUP):
            part = src[k * size : k * size + own, :]
            xi_ref[pl.ds(pl.multiple_of(base + k * own, own), own), :] = part
            aux = src[k * size + own : (k + 1) * size, :].astype(F32)
            w_ref[pl.ds(first + k, 1), :] = aux[1:2, 0:LANES]
            pf = part.astype(F32)
            sq = jnp.sum(pf * pf, axis=1, keepdims=True)
            ibias.append(to_col(aux[0:1, 0:LANES], own) / EPS - sq * scale)
        ibias = jnp.concatenate(ibias, axis=0)
        part = xi_ref[pl.ds(base, span), :]
        cross = lax.dot_general(part, xj, NT, preferred_element_type=F32)
        plan = jnp.exp(cross * (2.0 * scale) + jbias + ibias)
        plan_ref[pl.ds(base, span), :] = plan
        inner = lax.dot_general(part, gj, NT, preferred_element_type=F32)
        inner_ref[pl.ds(base, span), :] = inner
        weighted = plan * inner
        mass = slots_of(jnp.sum(plan, axis=1, keepdims=True), own, GROUP)
        ph = slots_of(jnp.sum(weighted, axis=1, keepdims=True), own, GROUP)
        for k in range(GROUP):
            mass_ref[0, pl.ds(first + k, 1), :] = mass[k : k + 1]
            mass_ref[0, pl.ds(isrc + first + k, 1), :] = ph[k : k + 1]
        plan, weighted = fold(plan), fold(weighted)
        cmass = plan if cmass is None else cmass + plan
        cph = weighted if cph is None else cph + weighted
    for s in range(1, isrc):
        mass_ref[s] = mass_ref[0]
    col_ref[...] = jnp.zeros_like(col_ref)
    cmass = jnp.sum(cmass, axis=0, keepdims=True)
    cph = jnp.sum(cph, axis=0, keepdims=True)
    for k in range(cols // LANES):
        col_ref[k : k + 1, :] = cmass[:, k * LANES : (k + 1) * LANES]
        col_ref[8 + k : 9 + k, :] = cph[:, k * LANES : (k + 1) * LANES]


def apply_cols(own, isrc, phi, plan_ref):
    span = GROUP * own
    acc = None
    for t in range(isrc // GROUP):
        col = column_of(phi[t * GROUP : (t + 1) * GROUP], own, GROUP)
        part = fold(plan_ref[t * span : (t + 1) * span, :] * col)
        acc = part if acc is None else acc + part
    return jnp.sum(acc, axis=0, keepdims=True)


def valid(own, value):
    lanes = lax.broadcasted_iota(jnp.int32, value.shape, 1)
    return jnp.where(lanes < own, value, 0.0)


def phi_first(own, isrc, jsrc, got_ref, col_ref, plan_ref, mass_ref, send_ref):
    total = jnp.sum(got_ref[...], axis=0)
    mass_ref[...] = total
    phi = valid(own, -total[isrc:] / total[:isrc])
    applied = apply_cols(own, isrc, phi, plan_ref)
    for s in range(jsrc):
        send_ref[s, 0:16, :] = col_ref[...]
        send_ref[s, 16:24, :] = jnp.zeros((8, LANES), F32)
    put_lanes(send_ref, jsrc, 16, applied)


def phi_next(own, isrc, jsrc, got_ref, mass_ref, w_ref, plan_ref, phi_ref, send_ref):
    total = jnp.sum(got_ref[...], axis=0)
    mass = mass_ref[...]
    phi = valid(own, -(mass[isrc:] + total) / mass[:isrc])
    phi_ref[...] = phi
    applied = apply_cols(own, isrc, phi, plan_ref)
    wts = valid(own, w_ref[...])
    wsum = jnp.sum(wts, axis=0, keepdims=True)
    wphi = jnp.sum(wts * phi, axis=0, keepdims=True)
    for s in range(jsrc):
        send_ref[s, 6:7, :] = wsum
        send_ref[s, 7:8, :] = wphi
    put_lanes(send_ref, jsrc, 0, applied)


def row_of(value, count):
    return jnp.concatenate([value[k : k + 1, :] for k in range(count)], axis=1)


def apply_rows(own, isrc, psi, plan_ref, send_ref):
    span = GROUP * own
    for t in range(isrc // GROUP):
        col = jnp.sum(plan_ref[t * span : (t + 1) * span, :] * psi, axis=1, keepdims=True)
        part = slots_of(col, own, GROUP)
        for s in range(isrc):
            send_ref[s, t * GROUP : (t + 1) * GROUP, :] = part


def psi_first(own, isrc, got_ref, plan_ref, col_ref, send_ref):
    total = jnp.sum(got_ref[...], axis=0)
    col_ref[...] = total[:16]
    count = plan_ref.shape[1] // LANES
    psi = row_of(-(total[8:16] + total[16:24]) / total[0:8], count)
    apply_rows(own, isrc, psi, plan_ref, send_ref)


def psi_next(own, isrc, got_ref, col_ref, plan_ref, send_ref):
    total = jnp.sum(got_ref[...], axis=0)
    count = plan_ref.shape[1] // LANES
    psi = row_of(-(col_ref[8:16] + total) / col_ref[0:8], count)
    apply_rows(own, isrc, psi, plan_ref, send_ref)


def bit_of(axis, bit):
    return lax.rem(lax.shift_right_logical(lax.axis_index(axis), bit), 2)


def finish_cols(own, width, isrc, jsrc, every, got_ref, col_ref, phi_ref, plan_ref, inner_ref, xi_ref, mixed_ref, q_ref, gw_ref, send_ref, keep_ref, acc_ref):
    total = jnp.sum(got_ref[...], axis=0)
    count = plan_ref.shape[1] // LANES
    psi = row_of(-(col_ref[8:16] + total) / col_ref[0:8], count)
    wsum = jnp.sum(total[6:7], axis=1, keepdims=True)
    wphi = jnp.sum(total[7:8], axis=1, keepdims=True)
    gw_ref[...] = -(every / wsum) * (phi_ref[...] - wphi / wsum)
    span = GROUP * own
    for t in range(isrc // GROUP):
        at = slice(t * span, (t + 1) * span)
        col = column_of(phi_ref[t * GROUP : (t + 1) * GROUP, :], own, GROUP)
        mixed = plan_ref[at, :] * (inner_ref[at, :] + (col + psi))
        q_ref[at, :] = jnp.sum(mixed, axis=1, keepdims=True)
        mixed = mixed.astype(BF16)
        mixed_ref[at, :] = mixed
        term = lax.dot_general(mixed, xi_ref[at, :], TN, preferred_element_type=F32)
        if t:
            term = acc_ref[...] + term
        acc_ref[...] = term
    scale = 1.0 / (width * EPS)
    mine = bit_of("z", 0)
    for m in range(jsrc // 2):
        keep = pl.ds(pl.multiple_of((2 * m + mine) * own, own), own)
        give = pl.ds(pl.multiple_of((2 * m + 1 - mine) * own, own), own)
        at = slice(m * own, (m + 1) * own)
        keep_ref[at, :] = acc_ref[keep, :] * scale
        send_ref[at, :] = (acc_ref[give, :] * scale).astype(BF16)


def halve(own, bit, keep_ref, got_ref, next_ref, send_ref):
    mine = bit_of("z", bit)
    for m in range(next_ref.shape[0] // own):
        keep = pl.ds(pl.multiple_of((2 * m + mine) * own, own), own)
        give = pl.ds(pl.multiple_of((2 * m + 1 - mine) * own, own), own)
        at = slice(m * own, (m + 1) * own)
        next_ref[at, :] = keep_ref[keep, :] + got_ref[keep, :].astype(F32)
        send_ref[at, :] = (keep_ref[give, :] + got_ref[give, :].astype(F32)).astype(BF16)


def finish_rows(own, width, isrc, plan_ref, mixed_ref, q_ref, xi_ref, xj_ref, gj_ref, row_ref):
    scale = 1.0 / (width * EPS)
    span = GROUP * own
    xj = xj_ref[...]
    gj = gj_ref[...]
    for t in range(isrc // GROUP):
        at = slice(t * span, (t + 1) * span)
        base = jnp.dot(plan_ref[at, :].astype(BF16), gj, preferred_element_type=F32)
        term = jnp.dot(mixed_ref[at, :], xj, preferred_element_type=F32)
        term = base + (term - q_ref[at, :] * xi_ref[at, :].astype(F32)) * scale
        term = term.astype(BF16)
        for k in range(GROUP):
            row_ref[t * GROUP + k] = term[k * own : (k + 1) * own]


def total_up(rows_ref, keep_ref, got_ref, out_ref):
    acc = jnp.sum(rows_ref[...].astype(F32), axis=0)
    out_ref[...] = (acc + (keep_ref[...] + got_ref[...].astype(F32))).astype(BF16)


def local(particles, cotangent, row_potential, col_potential, weights):
    own, width = particles.shape
    iaxes, jaxes = ("y", "row"), ("z",)
    ysrc, xsrc = lax.axis_size("y"), lax.axis_size("row")
    isrc, jsrc = ysrc * xsrc, lax.axis_size("z")
    rows, cols = isrc * own, jsrc * own

    def swap(value, axes):
        return lax.all_to_all(value, axes, 0, 0, tiled=True)

    def shift(value, axis, k):
        n = lax.axis_size(axis)
        return lax.ppermute(value, axis, [(i, (i + k) % n) for i in range(n)])

    def flip(value, bit):
        return lax.ppermute(value, "z", [(i, i ^ bit) for i in range(jsrc)])

    def call(body, micros, outs, *args, scratch=(), in_specs=None, out_specs=None):
        return pl.pallas_call(
            body,
            out_shape=[jax.ShapeDtypeStruct(s, d) for s, d in outs],
            in_specs=in_specs or whole(len(args)),
            out_specs=out_specs or whole(len(outs)),
            scratch_shapes=list(scratch),
            compiler_params=params(),
            cost_estimate=pl.CostEstimate(flops=int(micros * 1e9), bytes_accessed=1024, transcendentals=0),
        )(*args)

    anywhere = pl.BlockSpec(memory_space=pltpu.HBM)
    ipack, jpack = call(
        functools.partial(pack, own, width, jsrc),
        2,
        [((own + AUX, width), BF16), ((jsrc, 2 * own + AUX, width), BF16)],
        particles,
        cotangent,
        row_potential.reshape(1, own),
        col_potential.reshape(1, own),
        weights.reshape(1, own),
        scratch=[
            pltpu.VMEM((2 * own + AUX, width), BF16),
            pltpu.VMEM((2, AUX, width), F32),
            pltpu.VMEM((3, 1, own), BF16),
            pltpu.SemaphoreType.DMA((5,)),
            pltpu.SemaphoreType.DMA((jsrc,)),
        ],
        in_specs=[anywhere] * 5,
        out_specs=whole(1) + [anywhere],
    )
    jgot = swap(jpack, jaxes)
    near = [shift(ipack, "row", k) for k in range(1, xsrc)]
    (line,) = call(
        functools.partial(stack, own, xsrc), 1, [((xsrc * (own + AUX), width), BF16)], ipack, *near
    )
    igot = [line] + [shift(line, "y", k) for k in range(1, ysrc)]
    plan, inner, xi, xj, gj, wts, send, col_part = call(
        functools.partial(build, own, width, isrc, jsrc),
        5,
        [
            ((rows, cols), F32),
            ((rows, cols), F32),
            ((rows, width), BF16),
            ((cols, width), BF16),
            ((cols, width), BF16),
            ((isrc, LANES), F32),
            ((isrc, 2 * isrc, LANES), F32),
            ((16, LANES), F32),
        ],
        *igot,
        jgot,
    )
    got = swap(send, iaxes)
    mass, send = call(
        functools.partial(phi_first, own, isrc, jsrc),
        1,
        [((2 * isrc, LANES), F32), ((jsrc, 24, LANES), F32)],
        got,
        col_part,
        plan,
    )
    got = swap(send, jaxes)
    col, send = call(
        functools.partial(psi_first, own, isrc),
        1,
        [((16, LANES), F32), ((isrc, isrc, LANES), F32)],
        got,
        plan,
    )
    for step in range(1, ITERS):
        got = swap(send, iaxes)
        phi, send = call(
            functools.partial(phi_next, own, isrc, jsrc),
            1,
            [((isrc, LANES), F32), ((jsrc, 8, LANES), F32)],
            got,
            mass,
            wts,
            plan,
        )
        got = swap(send, jaxes)
        if step < ITERS - 1:
            (send,) = call(
                functools.partial(psi_next, own, isrc),
                1,
                [((isrc, isrc, LANES), F32)],
                got,
                col,
                plan,
            )
    half = cols // 2
    mixed, q, gw, give, keep = call(
        functools.partial(finish_cols, own, width, isrc, jsrc, float(isrc * jsrc * own)),
        3,
        [((rows, cols), BF16), ((rows, 1), F32), ((isrc, LANES), F32), ((half, width), BF16), ((half, width), F32)],
        got,
        col,
        phi,
        plan,
        inner,
        xi,
        scratch=[pltpu.VMEM((cols, width), F32)],
    )
    taken = flip(give, 1)
    (row_send,) = call(
        functools.partial(finish_rows, own, width, isrc),
        3,
        [((isrc, own, width), BF16)],
        plan,
        mixed,
        q,
        xi,
        xj,
        gj,
    )
    row_send, taken = lax.optimization_barrier((row_send, taken))
    row_got = swap(row_send, iaxes)
    for bit in (1, 2):
        half //= 2
        keep, give = call(
            functools.partial(halve, own, bit), 1, [((half, width), F32), ((half, width), BF16)], keep, taken
        )
        taken = flip(give, 1 << bit)
    (grad,) = call(total_up, 1, [((own, width), BF16)], row_got, keep, taken)
    mine = lax.axis_index("y") * xsrc + lax.axis_index("row")
    grad_weights = lax.dynamic_slice(gw, (mine, 0), (1, own)).reshape(own)
    return (grad, grad_weights)


def solution(mesh):
    filt, row, col = mesh.devices.shape
    split = Mesh(mesh.devices.reshape(filt, row, 8, col // 8), ("filt", "row", "z", "y"))
    spec = ("filt", "row", "z", "y")
    return jax.shard_map(
        local,
        mesh=split,
        in_specs=(P(spec, None), P(spec, None), P(spec), P(spec), P(spec)),
        out_specs=(P(spec, None), P(spec)),
        check_vma=False,
    )
```

```python
import functools

import jax
import jax.numpy as jnp
from jax import lax
from jax.experimental import pallas as pl
from jax.experimental.pallas import tpu as pltpu
from jax.sharding import Mesh
from jax.sharding import PartitionSpec as P

ITERS = 4


EPS = 0.09

LANES = 128
AUX = 8
F32 = jnp.float32
BF16 = jnp.bfloat16


def params(mib):
    return pltpu.CompilerParams(vmem_limit_bytes=mib << 20)


def whole(n):
    return [pl.BlockSpec(memory_space=pltpu.VMEM)] * n


def eye(own):
    rows = lax.broadcasted_iota(jnp.int32, (own, LANES), 0)
    lanes = lax.broadcasted_iota(jnp.int32, (own, LANES), 1)
    return rows == lanes


def to_row(col, own):
    return jnp.sum(jnp.where(eye(own), col, 0.0), axis=0, keepdims=True)


def to_col(row, own):
    return jnp.sum(jnp.where(eye(own), row, 0.0), axis=1, keepdims=True)


def lanes_of(col):
    out = []
    for k in range(col.shape[0] // LANES):
        out.append(to_row(col[k * LANES : (k + 1) * LANES], LANES))
    return jnp.concatenate(out, axis=1)


def slots_of(value, own, count):
    return jnp.concatenate([to_row(value[k * own : (k + 1) * own], own) for k in range(count)], axis=0)


def column_of(value, own, count):
    return jnp.concatenate([to_col(value[k : k + 1], own) for k in range(count)], axis=0)


def fold(block):
    return jnp.sum(block.reshape(block.shape[0] // 8, 8, block.shape[1]), axis=0)


def put_lanes(ref, slots, base, row):
    for k in range(row.shape[1] // LANES):
        piece = row[:, k * LANES : (k + 1) * LANES]
        for s in range(slots):
            ref[s, base + k : base + k + 1, :] = piece


def pack(own, width, jsrc, x_ref, gy_ref, f_ref, g_ref, w_ref, ipack_ref, jpack_ref, block_ref, line_ref, vec_ref, in_sem, out_sem):
    copies = [
        pltpu.make_async_copy(f_ref, vec_ref.at[0], in_sem.at[2]),
        pltpu.make_async_copy(w_ref, vec_ref.at[1], in_sem.at[3]),
        pltpu.make_async_copy(g_ref, vec_ref.at[2], in_sem.at[4]),
        pltpu.make_async_copy(x_ref, block_ref.at[pl.ds(0, own)], in_sem.at[0]),
        pltpu.make_async_copy(gy_ref, block_ref.at[pl.ds(own, own)], in_sem.at[1]),
    ]
    for copy in copies:
        copy.start()
    line_ref[...] = jnp.zeros_like(line_ref)
    for copy in copies:
        copy.wait()
    line_ref[0, 0:1, 0:own] = vec_ref[0].astype(F32)
    line_ref[0, 1:2, 0:own] = vec_ref[1].astype(F32)
    line_ref[1, 0:1, 0:own] = vec_ref[2].astype(F32)
    block_ref[2 * own : 2 * own + AUX, :] = line_ref[1].astype(BF16)
    outs = [pltpu.make_async_copy(block_ref, jpack_ref.at[s], out_sem.at[s]) for s in range(jsrc)]
    for copy in outs:
        copy.start()
    ipack_ref[0:own, :] = block_ref[0:own, :]
    ipack_ref[own : own + AUX, :] = line_ref[0].astype(BF16)
    for copy in outs:
        copy.wait()


def stack(own, count, *refs):
    out_ref = refs[count]
    size = own + AUX
    for k in range(count):
        place = behind("row", k, count)
        out_ref[pl.ds(pl.multiple_of(place * size, size), size), :] = refs[k][...]


GROUP = 4
NT = (((1,), (1,)), ((), ()))
TN = (((0,), (0,)), ((), ()))


def behind(axis, k, count):
    return lax.rem(lax.axis_index(axis) + (count - k), count)


def build(own, width, isrc, jsrc, *refs):
    steps = isrc // GROUP
    pi_refs, pj_ref = refs[:steps], refs[steps]
    plan_ref, inner_ref, xi_ref, xj_ref, gj_ref, w_ref, mass_ref, col_ref = refs[steps + 1 :]
    cols = jsrc * own
    size = own + AUX
    scale = 1.0 / (2.0 * width * EPS)
    bias = []
    for k in range(jsrc):
        part = pj_ref[k, 0:own, :]
        xj_ref[k * own : (k + 1) * own, :] = part
        gj_ref[k * own : (k + 1) * own, :] = pj_ref[k, own : 2 * own, :]
        pf = part.astype(F32)
        sq = jnp.sum(pf * pf, axis=1, keepdims=True)
        pot = to_col(pj_ref[k, 2 * own : 2 * own + AUX, :].astype(F32)[0:1, 0:LANES], own)
        bias.append(pot / EPS - sq * scale)
    jbias = lanes_of(jnp.concatenate(bias, axis=0))
    xj = xj_ref[...]
    gj = gj_ref[...]
    span = GROUP * own
    cmass = cph = None
    for m in range(steps):
        src = pi_refs[m]
        t = behind("y", m, steps)
        base = pl.multiple_of(t * span, span)
        first = pl.multiple_of(t * GROUP, GROUP)
        ibias = []
        for k in range(GROUP):
            part = src[k * size : k * size + own, :]
            xi_ref[pl.ds(pl.multiple_of(base + k * own, own), own), :] = part
            aux = src[k * size + own : (k + 1) * size, :].astype(F32)
            w_ref[pl.ds(first + k, 1), :] = aux[1:2, 0:LANES]
            pf = part.astype(F32)
            sq = jnp.sum(pf * pf, axis=1, keepdims=True)
            ibias.append(to_col(aux[0:1, 0:LANES], own) / EPS - sq * scale)
        ibias = jnp.concatenate(ibias, axis=0)
        part = xi_ref[pl.ds(base, span), :]
        cross = lax.dot_general(part, xj, NT, preferred_element_type=F32)
        plan = jnp.exp(cross * (2.0 * scale) + jbias + ibias)
        plan_ref[pl.ds(base, span), :] = plan
        inner = lax.dot_general(part, gj, NT, preferred_element_type=F32)
        inner_ref[pl.ds(base, span), :] = inner
        weighted = plan * inner
        mass = slots_of(jnp.sum(plan, axis=1, keepdims=True), own, GROUP)
        ph = slots_of(jnp.sum(weighted, axis=1, keepdims=True), own, GROUP)
        for k in range(GROUP):
            mass_ref[0, pl.ds(first + k, 1), :] = mass[k : k + 1]
            mass_ref[0, pl.ds(isrc + first + k, 1), :] = ph[k : k + 1]
        plan, weighted = fold(plan), fold(weighted)
        cmass = plan if cmass is None else cmass + plan
        cph = weighted if cph is None else cph + weighted
    for s in range(1, isrc):
        mass_ref[s] = mass_ref[0]
    col_ref[...] = jnp.zeros_like(col_ref)
    cmass = jnp.sum(cmass, axis=0, keepdims=True)
    cph = jnp.sum(cph, axis=0, keepdims=True)
    for k in range(cols // LANES):
        col_ref[k : k + 1, :] = cmass[:, k * LANES : (k + 1) * LANES]
        col_ref[8 + k : 9 + k, :] = cph[:, k * LANES : (k + 1) * LANES]


def apply_cols(own, isrc, phi, plan_ref):
    span = GROUP * own
    acc = None
    for t in range(isrc // GROUP):
        col = column_of(phi[t * GROUP : (t + 1) * GROUP], own, GROUP)
        part = fold(plan_ref[t * span : (t + 1) * span, :] * col)
        acc = part if acc is None else acc + part
    return jnp.sum(acc, axis=0, keepdims=True)


def valid(own, value):
    lanes = lax.broadcasted_iota(jnp.int32, value.shape, 1)
    return jnp.where(lanes < own, value, 0.0)


def phi_first(own, isrc, jsrc, got_ref, col_ref, plan_ref, mass_ref, send_ref):
    total = jnp.sum(got_ref[...], axis=0)
    mass_ref[...] = total
    phi = valid(own, -total[isrc:] / total[:isrc])
    applied = apply_cols(own, isrc, phi, plan_ref)
    for s in range(jsrc):
        send_ref[s, 0:16, :] = col_ref[...]
        send_ref[s, 16:24, :] = jnp.zeros((8, LANES), F32)
    put_lanes(send_ref, jsrc, 16, applied)


def phi_next(own, isrc, jsrc, got_ref, mass_ref, w_ref, plan_ref, phi_ref, send_ref):
    total = jnp.sum(got_ref[...], axis=0)
    mass = mass_ref[...]
    phi = valid(own, -(mass[isrc:] + total) / mass[:isrc])
    phi_ref[...] = phi
    applied = apply_cols(own, isrc, phi, plan_ref)
    wts = valid(own, w_ref[...])
    wsum = jnp.sum(wts, axis=0, keepdims=True)
    wphi = jnp.sum(wts * phi, axis=0, keepdims=True)
    for s in range(jsrc):
        send_ref[s, 6:7, :] = wsum
        send_ref[s, 7:8, :] = wphi
    put_lanes(send_ref, jsrc, 0, applied)


def row_of(value, count):
    return jnp.concatenate([value[k : k + 1, :] for k in range(count)], axis=1)


def apply_rows(own, isrc, psi, plan_ref, send_ref):
    span = GROUP * own
    for t in range(isrc // GROUP):
        col = jnp.sum(plan_ref[t * span : (t + 1) * span, :] * psi, axis=1, keepdims=True)
        part = slots_of(col, own, GROUP)
        for s in range(isrc):
            send_ref[s, t * GROUP : (t + 1) * GROUP, :] = part


def psi_first(own, isrc, got_ref, plan_ref, col_ref, send_ref):
    total = jnp.sum(got_ref[...], axis=0)
    col_ref[...] = total[:16]
    count = plan_ref.shape[1] // LANES
    psi = row_of(-(total[8:16] + total[16:24]) / total[0:8], count)
    apply_rows(own, isrc, psi, plan_ref, send_ref)


def psi_next(own, isrc, got_ref, col_ref, plan_ref, send_ref):
    total = jnp.sum(got_ref[...], axis=0)
    count = plan_ref.shape[1] // LANES
    psi = row_of(-(col_ref[8:16] + total) / col_ref[0:8], count)
    apply_rows(own, isrc, psi, plan_ref, send_ref)


def bit_of(axis, bit):
    return lax.rem(lax.shift_right_logical(lax.axis_index(axis), bit), 2)


def finish_cols(own, width, isrc, jsrc, every, got_ref, col_ref, phi_ref, plan_ref, inner_ref, xi_ref, mixed_ref, q_ref, gw_ref, send_ref, keep_ref, acc_ref):
    total = jnp.sum(got_ref[...], axis=0)
    count = plan_ref.shape[1] // LANES
    psi = row_of(-(col_ref[8:16] + total) / col_ref[0:8], count)
    wsum = jnp.sum(total[6:7], axis=1, keepdims=True)
    wphi = jnp.sum(total[7:8], axis=1, keepdims=True)
    gw_ref[...] = -(every / wsum) * (phi_ref[...] - wphi / wsum)
    span = GROUP * own
    for t in range(isrc // GROUP):
        at = slice(t * span, (t + 1) * span)
        col = column_of(phi_ref[t * GROUP : (t + 1) * GROUP, :], own, GROUP)
        mixed = plan_ref[at, :] * (inner_ref[at, :] + (col + psi))
        q_ref[at, :] = jnp.sum(mixed, axis=1, keepdims=True)
        mixed = mixed.astype(BF16)
        mixed_ref[at, :] = mixed
        term = lax.dot_general(mixed, xi_ref[at, :], TN, preferred_element_type=F32)
        if t:
            term = acc_ref[...] + term
        acc_ref[...] = term
    scale = 1.0 / (width * EPS)
    mine = bit_of("z", 0)
    for m in range(jsrc // 2):
        keep = pl.ds(pl.multiple_of((2 * m + mine) * own, own), own)
        give = pl.ds(pl.multiple_of((2 * m + 1 - mine) * own, own), own)
        at = slice(m * own, (m + 1) * own)
        keep_ref[at, :] = acc_ref[keep, :] * scale
        send_ref[at, :] = (acc_ref[give, :] * scale).astype(BF16)


def halve(own, bit, keep_ref, got_ref, next_ref, send_ref):
    mine = bit_of("z", bit)
    for m in range(next_ref.shape[0] // own):
        keep = pl.ds(pl.multiple_of((2 * m + mine) * own, own), own)
        give = pl.ds(pl.multiple_of((2 * m + 1 - mine) * own, own), own)
        at = slice(m * own, (m + 1) * own)
        next_ref[at, :] = keep_ref[keep, :] + got_ref[keep, :].astype(F32)
        send_ref[at, :] = (keep_ref[give, :] + got_ref[give, :].astype(F32)).astype(BF16)


def spread(own, isrc, plan_ref, gj_ref, after_ref, base_ref):
    span = GROUP * own
    gj = gj_ref[...]
    for t in range(isrc // GROUP):
        at = slice(t * span, (t + 1) * span)
        base_ref[at, :] = jnp.dot(plan_ref[at, :].astype(BF16), gj, preferred_element_type=F32)


def finish_rows(own, width, isrc, base_ref, mixed_ref, q_ref, xi_ref, xj_ref, after_ref, row_ref):
    scale = 1.0 / (width * EPS)
    span = GROUP * own
    xj = xj_ref[...]
    for t in range(isrc // GROUP):
        at = slice(t * span, (t + 1) * span)
        term = jnp.dot(mixed_ref[at, :], xj, preferred_element_type=F32)
        term = base_ref[at, :] + (term - q_ref[at, :] * xi_ref[at, :].astype(F32)) * scale
        term = term.astype(BF16)
        for k in range(GROUP):
            row_ref[t * GROUP + k] = term[k * own : (k + 1) * own]


def total_up(rows_ref, keep_ref, got_ref, out_ref):
    acc = jnp.sum(rows_ref[...].astype(F32), axis=0)
    out_ref[...] = (acc + (keep_ref[...] + got_ref[...].astype(F32))).astype(BF16)


def local(particles, cotangent, row_potential, col_potential, weights):
    own, width = particles.shape
    iaxes, jaxes = ("y", "row"), ("z",)
    ysrc, xsrc = lax.axis_size("y"), lax.axis_size("row")
    isrc, jsrc = ysrc * xsrc, lax.axis_size("z")
    rows, cols = isrc * own, jsrc * own

    def swap(value, axes):
        return lax.all_to_all(value, axes, 0, 0, tiled=True)

    def shift(value, axis, k):
        n = lax.axis_size(axis)
        return lax.ppermute(value, axis, [(i, (i + k) % n) for i in range(n)])

    def flip(value, bit):
        return lax.ppermute(value, "z", [(i, i ^ bit) for i in range(jsrc)])

    def call(body, micros, outs, *args, scratch=(), in_specs=None, out_specs=None, mib=12):
        return pl.pallas_call(
            body,
            out_shape=[jax.ShapeDtypeStruct(s, d) for s, d in outs],
            in_specs=in_specs or whole(len(args)),
            out_specs=out_specs or whole(len(outs)),
            scratch_shapes=list(scratch),
            compiler_params=params(mib),
            cost_estimate=pl.CostEstimate(flops=int(micros * 1e9), bytes_accessed=1024, transcendentals=0),
        )(*args)

    anywhere = pl.BlockSpec(memory_space=pltpu.HBM)
    ipack, jpack = call(
        functools.partial(pack, own, width, jsrc),
        2,
        [((own + AUX, width), BF16), ((jsrc, 2 * own + AUX, width), BF16)],
        particles,
        cotangent,
        row_potential.reshape(1, own),
        col_potential.reshape(1, own),
        weights.reshape(1, own),
        scratch=[
            pltpu.VMEM((2 * own + AUX, width), BF16),
            pltpu.VMEM((2, AUX, width), F32),
            pltpu.VMEM((3, 1, own), BF16),
            pltpu.SemaphoreType.DMA((5,)),
            pltpu.SemaphoreType.DMA((jsrc,)),
        ],
        in_specs=[anywhere] * 5,
        out_specs=whole(1) + [anywhere],
        mib=60,
    )
    jgot = swap(jpack, jaxes)
    near = [shift(ipack, "row", k) for k in range(1, xsrc)]
    (line,) = call(
        functools.partial(stack, own, xsrc), 1, [((xsrc * (own + AUX), width), BF16)], ipack, *near
    )
    igot = [line] + [shift(line, "y", k) for k in range(1, ysrc)]
    plan, inner, xi, xj, gj, wts, send, col_part = call(
        functools.partial(build, own, width, isrc, jsrc),
        5,
        [
            ((rows, cols), F32),
            ((rows, cols), F32),
            ((rows, width), BF16),
            ((cols, width), BF16),
            ((cols, width), BF16),
            ((isrc, LANES), F32),
            ((isrc, 2 * isrc, LANES), F32),
            ((16, LANES), F32),
        ],
        *igot,
        jgot,
    )
    got = swap(send, iaxes)
    mass, send = call(
        functools.partial(phi_first, own, isrc, jsrc),
        1,
        [((2 * isrc, LANES), F32), ((jsrc, 24, LANES), F32)],
        got,
        col_part,
        plan,
    )
    got = swap(send, jaxes)
    col, send = call(
        functools.partial(psi_first, own, isrc),
        1,
        [((16, LANES), F32), ((isrc, isrc, LANES), F32)],
        got,
        plan,
    )
    for step in range(1, ITERS):
        got = swap(send, iaxes)
        phi, send = call(
            functools.partial(phi_next, own, isrc, jsrc),
            1,
            [((isrc, LANES), F32), ((jsrc, 8, LANES), F32)],
            got,
            mass,
            wts,
            plan,
        )
        got = swap(send, jaxes)
        if step < ITERS - 1:
            (send,) = call(
                functools.partial(psi_next, own, isrc),
                1,
                [((isrc, isrc, LANES), F32)],
                got,
                col,
                plan,
            )
    half = cols // 2
    mixed, q, gw, give, keep = call(
        functools.partial(finish_cols, own, width, isrc, jsrc, float(isrc * jsrc * own)),
        3,
        [((rows, cols), BF16), ((rows, 1), F32), ((isrc, LANES), F32), ((half, width), BF16), ((half, width), F32)],
        got,
        col,
        phi,
        plan,
        inner,
        xi,
        scratch=[pltpu.VMEM((cols, width), F32)],
    )
    taken = flip(give, 1)
    (base,) = call(functools.partial(spread, own, isrc), 1, [((rows, width), F32)], plan, gj, gw)
    base, taken = lax.optimization_barrier((base, taken))
    half //= 2
    keep, give = call(
        functools.partial(halve, own, 1), 1, [((half, width), F32), ((half, width), BF16)], keep, taken
    )
    taken = flip(give, 2)
    (row_send,) = call(
        functools.partial(finish_rows, own, width, isrc),
        2,
        [((isrc, own, width), BF16)],
        base,
        mixed,
        q,
        xi,
        xj,
        keep,
    )
    row_send, taken = lax.optimization_barrier((row_send, taken))
    half //= 2
    keep, give = call(
        functools.partial(halve, own, 2), 1, [((half, width), F32), ((half, width), BF16)], keep, taken
    )
    taken = flip(give, 4)
    row_got = swap(row_send, iaxes)
    (grad,) = call(total_up, 1, [((own, width), BF16)], row_got, keep, taken)
    mine = lax.axis_index("y") * xsrc + lax.axis_index("row")
    grad_weights = lax.dynamic_slice(gw, (mine, 0), (1, own)).reshape(own)
    return (grad, grad_weights)


def solution(mesh):
    filt, row, col = mesh.devices.shape
    split = Mesh(mesh.devices.reshape(filt, row, 8, col // 8), ("filt", "row", "z", "y"))
    spec = ("filt", "row", "z", "y")
    return jax.shard_map(
        local,
        mesh=split,
        in_specs=(P(spec, None), P(spec, None), P(spec), P(spec), P(spec)),
        out_specs=(P(spec, None), P(spec)),
        check_vma=False,
    )
```

```python
import functools

import jax
import jax.numpy as jnp
from jax import lax
from jax.experimental import pallas as pl
from jax.experimental.pallas import tpu as pltpu
from jax.sharding import Mesh
from jax.sharding import PartitionSpec as P

ITERS = 4


EPS = 0.09

LANES = 128
AUX = 8
F32 = jnp.float32
BF16 = jnp.bfloat16


def params(mib):
    return pltpu.CompilerParams(vmem_limit_bytes=mib << 20)


def whole(n):
    return [pl.BlockSpec(memory_space=pltpu.VMEM)] * n


def eye(own):
    rows = lax.broadcasted_iota(jnp.int32, (own, LANES), 0)
    lanes = lax.broadcasted_iota(jnp.int32, (own, LANES), 1)
    return rows == lanes


def to_row(col, own):
    return jnp.sum(jnp.where(eye(own), col, 0.0), axis=0, keepdims=True)


def to_col(row, own):
    return jnp.sum(jnp.where(eye(own), row, 0.0), axis=1, keepdims=True)


def lanes_of(col):
    out = []
    for k in range(col.shape[0] // LANES):
        out.append(to_row(col[k * LANES : (k + 1) * LANES], LANES))
    return jnp.concatenate(out, axis=1)


def slots_of(value, own, count):
    return jnp.concatenate([to_row(value[k * own : (k + 1) * own], own) for k in range(count)], axis=0)


def column_of(value, own, count):
    return jnp.concatenate([to_col(value[k : k + 1], own) for k in range(count)], axis=0)


def fold(block):
    return jnp.sum(block.reshape(block.shape[0] // 8, 8, block.shape[1]), axis=0)


def put_lanes(ref, slots, base, row):
    for k in range(row.shape[1] // LANES):
        piece = row[:, k * LANES : (k + 1) * LANES]
        for s in range(slots):
            ref[s, base + k : base + k + 1, :] = piece


def pack(own, width, jsrc, x_ref, gy_ref, f_ref, g_ref, w_ref, ipack_ref, jpack_ref, block_ref, line_ref, vec_ref, in_sem, out_sem):
    copies = [
        pltpu.make_async_copy(f_ref, vec_ref.at[0], in_sem.at[2]),
        pltpu.make_async_copy(w_ref, vec_ref.at[1], in_sem.at[3]),
        pltpu.make_async_copy(g_ref, vec_ref.at[2], in_sem.at[4]),
        pltpu.make_async_copy(x_ref, block_ref.at[pl.ds(0, own)], in_sem.at[0]),
        pltpu.make_async_copy(gy_ref, block_ref.at[pl.ds(own, own)], in_sem.at[1]),
    ]
    for copy in copies:
        copy.start()
    line_ref[...] = jnp.zeros_like(line_ref)
    for copy in copies:
        copy.wait()
    line_ref[0, 0:1, 0:own] = vec_ref[0].astype(F32)
    line_ref[0, 1:2, 0:own] = vec_ref[1].astype(F32)
    line_ref[1, 0:1, 0:own] = vec_ref[2].astype(F32)
    block_ref[2 * own : 2 * own + AUX, :] = line_ref[1].astype(BF16)
    outs = [pltpu.make_async_copy(block_ref, jpack_ref.at[s], out_sem.at[s]) for s in range(jsrc)]
    for copy in outs:
        copy.start()
    ipack_ref[0:own, :] = block_ref[0:own, :]
    ipack_ref[own : own + AUX, :] = line_ref[0].astype(BF16)
    for copy in outs:
        copy.wait()


def stack(own, count, *refs):
    out_ref = refs[count]
    size = own + AUX
    for k in range(count):
        place = behind("row", k, count)
        out_ref[pl.ds(pl.multiple_of(place * size, size), size), :] = refs[k][...]


GROUP = 4
NT = (((1,), (1,)), ((), ()))
TN = (((0,), (0,)), ((), ()))


def behind(axis, k, count):
    return lax.rem(lax.axis_index(axis) + (count - k), count)


def build(own, width, isrc, jsrc, *refs):
    steps = isrc // GROUP
    pi_refs, pj_ref = refs[:steps], refs[steps]
    plan_ref, inner_ref, xi_ref, xj_hbm, gj_hbm, w_ref, mass_ref, col_ref, xj_ref, gj_ref, sem = refs[steps + 1 :]
    cols = jsrc * own
    size = own + AUX
    scale = 1.0 / (2.0 * width * EPS)
    bias = []
    for k in range(jsrc):
        part = pj_ref[k, 0:own, :]
        xj_ref[k * own : (k + 1) * own, :] = part
        gj_ref[k * own : (k + 1) * own, :] = pj_ref[k, own : 2 * own, :]
        pf = part.astype(F32)
        sq = jnp.sum(pf * pf, axis=1, keepdims=True)
        pot = to_col(pj_ref[k, 2 * own : 2 * own + AUX, :].astype(F32)[0:1, 0:LANES], own)
        bias.append(pot / EPS - sq * scale)
    jbias = lanes_of(jnp.concatenate(bias, axis=0))
    copies = [pltpu.make_async_copy(xj_ref, xj_hbm, sem.at[0]), pltpu.make_async_copy(gj_ref, gj_hbm, sem.at[1])]
    for copy in copies:
        copy.start()
    xj = xj_ref[...]
    gj = gj_ref[...]
    span = GROUP * own
    cmass = cph = None
    for m in range(steps):
        src = pi_refs[m]
        t = behind("y", m, steps)
        base = pl.multiple_of(t * span, span)
        first = pl.multiple_of(t * GROUP, GROUP)
        ibias = []
        for k in range(GROUP):
            part = src[k * size : k * size + own, :]
            xi_ref[pl.ds(pl.multiple_of(base + k * own, own), own), :] = part
            aux = src[k * size + own : (k + 1) * size, :].astype(F32)
            w_ref[pl.ds(first + k, 1), :] = aux[1:2, 0:LANES]
            pf = part.astype(F32)
            sq = jnp.sum(pf * pf, axis=1, keepdims=True)
            ibias.append(to_col(aux[0:1, 0:LANES], own) / EPS - sq * scale)
        ibias = jnp.concatenate(ibias, axis=0)
        part = xi_ref[pl.ds(base, span), :]
        cross = lax.dot_general(part, xj, NT, preferred_element_type=F32)
        plan = jnp.exp(cross * (2.0 * scale) + jbias + ibias)
        plan_ref[pl.ds(base, span), :] = plan
        inner = lax.dot_general(part, gj, NT, preferred_element_type=F32)
        inner_ref[pl.ds(base, span), :] = inner
        weighted = plan * inner
        mass = slots_of(jnp.sum(plan, axis=1, keepdims=True), own, GROUP)
        ph = slots_of(jnp.sum(weighted, axis=1, keepdims=True), own, GROUP)
        for k in range(GROUP):
            mass_ref[0, pl.ds(first + k, 1), :] = mass[k : k + 1]
            mass_ref[0, pl.ds(isrc + first + k, 1), :] = ph[k : k + 1]
        plan, weighted = fold(plan), fold(weighted)
        cmass = plan if cmass is None else cmass + plan
        cph = weighted if cph is None else cph + weighted
    for s in range(1, isrc):
        mass_ref[s] = mass_ref[0]
    for copy in copies:
        copy.wait()
    col_ref[...] = jnp.zeros_like(col_ref)
    cmass = jnp.sum(cmass, axis=0, keepdims=True)
    cph = jnp.sum(cph, axis=0, keepdims=True)
    for k in range(cols // LANES):
        col_ref[k : k + 1, :] = cmass[:, k * LANES : (k + 1) * LANES]
        col_ref[8 + k : 9 + k, :] = cph[:, k * LANES : (k + 1) * LANES]


def apply_cols(own, isrc, phi, plan_ref):
    span = GROUP * own
    acc = None
    for t in range(isrc // GROUP):
        col = column_of(phi[t * GROUP : (t + 1) * GROUP], own, GROUP)
        part = fold(plan_ref[t * span : (t + 1) * span, :] * col)
        acc = part if acc is None else acc + part
    return jnp.sum(acc, axis=0, keepdims=True)


def valid(own, value):
    lanes = lax.broadcasted_iota(jnp.int32, value.shape, 1)
    return jnp.where(lanes < own, value, 0.0)


def phi_first(own, isrc, jsrc, got_ref, col_ref, plan_ref, mass_ref, send_ref):
    total = jnp.sum(got_ref[...], axis=0)
    mass_ref[...] = total
    phi = valid(own, -total[isrc:] / total[:isrc])
    applied = apply_cols(own, isrc, phi, plan_ref)
    for s in range(jsrc):
        send_ref[s, 0:16, :] = col_ref[...]
        send_ref[s, 16:24, :] = jnp.zeros((8, LANES), F32)
    put_lanes(send_ref, jsrc, 16, applied)


def phi_next(own, isrc, jsrc, got_ref, mass_ref, w_ref, plan_ref, phi_ref, send_ref):
    total = jnp.sum(got_ref[...], axis=0)
    mass = mass_ref[...]
    phi = valid(own, -(mass[isrc:] + total) / mass[:isrc])
    phi_ref[...] = phi
    applied = apply_cols(own, isrc, phi, plan_ref)
    wts = valid(own, w_ref[...])
    wsum = jnp.sum(wts, axis=0, keepdims=True)
    wphi = jnp.sum(wts * phi, axis=0, keepdims=True)
    for s in range(jsrc):
        send_ref[s, 6:7, :] = wsum
        send_ref[s, 7:8, :] = wphi
    put_lanes(send_ref, jsrc, 0, applied)


def row_of(value, count):
    return jnp.concatenate([value[k : k + 1, :] for k in range(count)], axis=1)


def apply_rows(own, isrc, psi, plan_ref, send_ref):
    span = GROUP * own
    for t in range(isrc // GROUP):
        col = jnp.sum(plan_ref[t * span : (t + 1) * span, :] * psi, axis=1, keepdims=True)
        part = slots_of(col, own, GROUP)
        for s in range(isrc):
            send_ref[s, t * GROUP : (t + 1) * GROUP, :] = part


def psi_first(own, isrc, got_ref, plan_ref, col_ref, send_ref):
    total = jnp.sum(got_ref[...], axis=0)
    col_ref[...] = total[:16]
    count = plan_ref.shape[1] // LANES
    psi = row_of(-(total[8:16] + total[16:24]) / total[0:8], count)
    apply_rows(own, isrc, psi, plan_ref, send_ref)


def psi_next(own, isrc, got_ref, col_ref, plan_ref, psi_ref, send_ref):
    total = jnp.sum(got_ref[...], axis=0)
    count = plan_ref.shape[1] // LANES
    psi = -(col_ref[8:16] + total) / col_ref[0:8]
    psi_ref[...] = psi
    apply_rows(own, isrc, row_of(psi, count), plan_ref, send_ref)


def bit_of(axis, bit):
    return lax.rem(lax.shift_right_logical(lax.axis_index(axis), bit), 2)


def early_cols(own, width, isrc, jsrc, phi_ref, psi_ref, plan_ref, inner_ref, xi_ref, keep_ref, send_ref, acc_ref):
    cols = plan_ref.shape[1]
    psi = row_of(psi_ref[...], cols // LANES)
    span = GROUP * own
    for t in range(isrc // GROUP):
        at = slice(t * span, (t + 1) * span)
        col = column_of(phi_ref[t * GROUP : (t + 1) * GROUP, :], own, GROUP)
        plan = plan_ref[at, :]
        mixed = (plan * (inner_ref[at, :] + (col + psi))).astype(BF16)
        part = xi_ref[at, :]
        for q, value in enumerate((mixed, plan.astype(BF16))):
            term = lax.dot_general(value, part, TN, preferred_element_type=F32)
            place = slice(q * cols, (q + 1) * cols)
            if t:
                term = acc_ref[place, :] + term
            acc_ref[place, :] = term
    scale = 1.0 / (width * EPS)
    mine = bit_of("z", 0)
    for q in range(2):
        for m in range(jsrc // 2):
            keep = pl.ds(pl.multiple_of(q * cols + (2 * m + mine) * own, own), own)
            give = pl.ds(pl.multiple_of(q * cols + (2 * m + 1 - mine) * own, own), own)
            first = q * (cols // 2) + m * own
            at = slice(first, first + own)
            keep_ref[at, :] = acc_ref[keep, :] * scale
            send_ref[at, :] = (acc_ref[give, :] * scale).astype(BF16)


def halve(own, bit, keep_ref, got_ref, next_ref, send_ref):
    mine = bit_of("z", bit)
    size, out = keep_ref.shape[0] // 2, next_ref.shape[0] // 2
    for q in range(2):
        for m in range(out // own):
            keep = pl.ds(pl.multiple_of(q * size + (2 * m + mine) * own, own), own)
            give = pl.ds(pl.multiple_of(q * size + (2 * m + 1 - mine) * own, own), own)
            first = q * out + m * own
            at = slice(first, first + own)
            next_ref[at, :] = keep_ref[keep, :] + got_ref[keep, :].astype(F32)
            send_ref[at, :] = (keep_ref[give, :] + got_ref[give, :].astype(F32)).astype(BF16)


def finish_rows(own, width, isrc, every, *refs):
    got_ref, col_ref, phi_ref, psi_ref, plan_hbm, inner_hbm, xi_hbm, xj_hbm, gj_hbm, after_ref = refs[:10]
    row_ref, gw_ref, delta_ref, plan_ref, inner_ref, xi_ref, xj_ref, gj_ref, sem = refs[10:]
    span = GROUP * own
    steps = isrc // GROUP
    head = [pltpu.make_async_copy(xj_hbm, xj_ref, sem.at[3 * steps]), pltpu.make_async_copy(gj_hbm, gj_ref, sem.at[3 * steps + 1])]
    parts = []
    for t in range(steps):
        at = pl.ds(t * span, span)
        pairs = ((plan_hbm, plan_ref), (inner_hbm, inner_ref), (xi_hbm, xi_ref))
        parts.append([pltpu.make_async_copy(a.at[at], b.at[at], sem.at[3 * t + n]) for n, (a, b) in enumerate(pairs)])
    for copy in head + sum(parts, []):
        copy.start()
    total = jnp.sum(got_ref[...], axis=0)
    cols = plan_ref.shape[1]
    psi = -(col_ref[8:16] + total) / col_ref[0:8]
    delta = row_of(psi - psi_ref[...], cols // LANES)
    psi = row_of(psi, cols // LANES)
    rows = lax.broadcasted_iota(jnp.int32, (own, cols), 0)
    lanes = lax.broadcasted_iota(jnp.int32, (own, cols), 1)
    first = lax.axis_index("z") * own
    delta_ref[...] = jnp.sum(jnp.where(lanes == rows + first, delta, 0.0), axis=1, keepdims=True)
    wsum = jnp.sum(total[6:7], axis=1, keepdims=True)
    wphi = jnp.sum(total[7:8], axis=1, keepdims=True)
    gw_ref[...] = -(every / wsum) * (phi_ref[...] - wphi / wsum)
    scale = 1.0 / (width * EPS)
    for copy in head:
        copy.wait()
    xj = xj_ref[...]
    gj = gj_ref[...]
    for t in range(steps):
        at = slice(t * span, (t + 1) * span)
        col = column_of(phi_ref[t * GROUP : (t + 1) * GROUP, :], own, GROUP)
        for copy in parts[t]:
            copy.wait()
        plan = plan_ref[at, :]
        mixed = plan * (inner_ref[at, :] + (col + psi))
        qrow = jnp.sum(mixed, axis=1, keepdims=True)
        base = jnp.dot(plan.astype(BF16), gj, preferred_element_type=F32)
        term = jnp.dot(mixed.astype(BF16), xj, preferred_element_type=F32)
        term = base + (term - qrow * xi_ref[at, :].astype(F32)) * scale
        term = term.astype(BF16)
        for k in range(GROUP):
            row_ref[t * GROUP + k] = term[k * own : (k + 1) * own]


def total_up(own, rows_ref, keep_ref, got_ref, delta_ref, out_ref):
    acc = jnp.sum(rows_ref[...].astype(F32), axis=0)
    sums = keep_ref[...] + got_ref[...].astype(F32)
    out_ref[...] = (acc + (sums[:own] + delta_ref[...] * sums[own:])).astype(BF16)


def local(particles, cotangent, row_potential, col_potential, weights):
    own, width = particles.shape
    iaxes, jaxes = ("y", "row"), ("z",)
    ysrc, xsrc = lax.axis_size("y"), lax.axis_size("row")
    isrc, jsrc = ysrc * xsrc, lax.axis_size("z")
    rows, cols = isrc * own, jsrc * own

    def swap(value, axes):
        return lax.all_to_all(value, axes, 0, 0, tiled=True)

    def shift(value, axis, k):
        n = lax.axis_size(axis)
        return lax.ppermute(value, axis, [(i, (i + k) % n) for i in range(n)])

    def flip(value, bit):
        return lax.ppermute(value, "z", [(i, i ^ bit) for i in range(jsrc)])

    def call(body, micros, outs, *args, scratch=(), in_specs=None, out_specs=None, mib=12, hbm=()):
        return pl.pallas_call(
            body,
            out_shape=[(pltpu.HBM if n in hbm else jax.ShapeDtypeStruct)(s, d) for n, (s, d) in enumerate(outs)],
            in_specs=in_specs or whole(len(args)),
            out_specs=out_specs or whole(len(outs)),
            scratch_shapes=list(scratch),
            compiler_params=params(mib),
            cost_estimate=pl.CostEstimate(flops=int(micros * 1e9), bytes_accessed=1024, transcendentals=0),
        )(*args)

    anywhere = pl.BlockSpec(memory_space=pltpu.HBM)
    ipack, jpack = call(
        functools.partial(pack, own, width, jsrc),
        2,
        [((own + AUX, width), BF16), ((jsrc, 2 * own + AUX, width), BF16)],
        *[
            pltpu.with_memory_space_constraint(v, pltpu.HBM)
            for v in (
                particles,
                cotangent,
                row_potential.reshape(1, own),
                col_potential.reshape(1, own),
                weights.reshape(1, own),
            )
        ],
        scratch=[
            pltpu.VMEM((2 * own + AUX, width), BF16),
            pltpu.VMEM((2, AUX, width), F32),
            pltpu.VMEM((3, 1, own), BF16),
            pltpu.SemaphoreType.DMA((5,)),
            pltpu.SemaphoreType.DMA((jsrc,)),
        ],
        in_specs=[anywhere] * 5,
        out_specs=whole(1) + [anywhere],
        hbm=(1,),
    )
    jgot = swap(jpack, jaxes)
    near = [shift(ipack, "row", k) for k in range(1, xsrc)]
    (line,) = call(
        functools.partial(stack, own, xsrc), 1, [((xsrc * (own + AUX), width), BF16)], ipack, *near
    )
    igot = [line] + [shift(line, "y", k) for k in range(1, ysrc)]
    plan, inner, xi, xj, gj, wts, send, col_part = call(
        functools.partial(build, own, width, isrc, jsrc),
        5,
        [
            ((rows, cols), F32),
            ((rows, cols), F32),
            ((rows, width), BF16),
            ((cols, width), BF16),
            ((cols, width), BF16),
            ((isrc, LANES), F32),
            ((isrc, 2 * isrc, LANES), F32),
            ((16, LANES), F32),
        ],
        *igot,
        jgot,
        scratch=[pltpu.VMEM((cols, width), BF16), pltpu.VMEM((cols, width), BF16), pltpu.SemaphoreType.DMA((2,))],
        out_specs=whole(3) + [anywhere] * 2 + whole(3),
        hbm=(3, 4),
    )
    got = swap(send, iaxes)
    mass, send = call(
        functools.partial(phi_first, own, isrc, jsrc),
        1,
        [((2 * isrc, LANES), F32), ((jsrc, 24, LANES), F32)],
        got,
        col_part,
        plan,
    )
    got = swap(send, jaxes)
    col, send = call(
        functools.partial(psi_first, own, isrc),
        1,
        [((16, LANES), F32), ((isrc, isrc, LANES), F32)],
        got,
        plan,
    )
    for step in range(1, ITERS):
        got = swap(send, iaxes)
        phi, send = call(
            functools.partial(phi_next, own, isrc, jsrc),
            1,
            [((isrc, LANES), F32), ((jsrc, 8, LANES), F32)],
            got,
            mass,
            wts,
            plan,
        )
        if step < ITERS - 1:
            got = swap(send, jaxes)
            psi, send = call(
                functools.partial(psi_next, own, isrc),
                1,
                [((8, LANES), F32), ((isrc, isrc, LANES), F32)],
                got,
                col,
                plan,
            )
    half = cols
    keep, give = call(
        functools.partial(early_cols, own, width, isrc, jsrc),
        3,
        [((half, width), F32), ((half, width), BF16)],
        phi,
        psi,
        plan,
        inner,
        xi,
        scratch=[pltpu.VMEM((2 * cols, width), F32)],
    )
    send, give = lax.optimization_barrier((send, give))
    taken = flip(give, 1)
    got = swap(send, jaxes)
    half //= 2
    keep, give = call(
        functools.partial(halve, own, 1), 1, [((half, width), F32), ((half, width), BF16)], keep, taken
    )
    taken = flip(give, 2)
    row_send, gw, delta = call(
        functools.partial(finish_rows, own, width, isrc, float(isrc * jsrc * own)),
        4,
        [((isrc, own, width), BF16), ((isrc, LANES), F32), ((own, 1), F32)],
        got,
        col,
        phi,
        psi,
        *[pltpu.with_memory_space_constraint(v, pltpu.HBM) for v in (plan, inner, xi, xj, gj)],
        keep,
        scratch=[
            pltpu.VMEM((rows, cols), F32),
            pltpu.VMEM((rows, cols), F32),
            pltpu.VMEM((rows, width), BF16),
            pltpu.VMEM((cols, width), BF16),
            pltpu.VMEM((cols, width), BF16),
            pltpu.SemaphoreType.DMA((3 * (isrc // GROUP) + 2,)),
        ],
        in_specs=whole(4) + [anywhere] * 5 + whole(1),
        mib=24,
    )
    row_send, taken = lax.optimization_barrier((row_send, taken))
    half //= 2
    keep, give = call(
        functools.partial(halve, own, 2), 1, [((half, width), F32), ((half, width), BF16)], keep, taken
    )
    taken = flip(give, 4)
    row_got = swap(row_send, iaxes)
    (grad,) = call(
        functools.partial(total_up, own), 1, [((own, width), BF16)], row_got, keep, taken, delta
    )
    mine = lax.axis_index("y") * xsrc + lax.axis_index("row")
    grad_weights = lax.dynamic_slice(gw, (mine, 0), (1, own)).reshape(own)
    return (grad, grad_weights)


def solution(mesh):
    filt, row, col = mesh.devices.shape
    split = Mesh(mesh.devices.reshape(filt, row, 8, col // 8), ("filt", "row", "z", "y"))
    spec = ("filt", "row", "z", "y")
    return jax.shard_map(
        local,
        mesh=split,
        in_specs=(P(spec, None), P(spec, None), P(spec), P(spec), P(spec)),
        out_specs=(P(spec, None), P(spec)),
        check_vma=False,
    )
```

```python
import functools

import jax
import jax.numpy as jnp
from jax import lax
from jax.experimental import pallas as pl
from jax.experimental.pallas import tpu as pltpu
from jax.sharding import Mesh
from jax.sharding import PartitionSpec as P

ITERS = 4


EPS = 0.09

LANES = 128
AUX = 8
F32 = jnp.float32
BF16 = jnp.bfloat16


def params(mib):
    return pltpu.CompilerParams(vmem_limit_bytes=mib << 20)


def whole(n):
    return [pl.BlockSpec(memory_space=pltpu.VMEM)] * n


def eye(own):
    rows = lax.broadcasted_iota(jnp.int32, (own, LANES), 0)
    lanes = lax.broadcasted_iota(jnp.int32, (own, LANES), 1)
    return rows == lanes


def to_row(col, own):
    return jnp.sum(jnp.where(eye(own), col, 0.0), axis=0, keepdims=True)


def to_col(row, own):
    return jnp.sum(jnp.where(eye(own), row, 0.0), axis=1, keepdims=True)


def lanes_of(col):
    out = []
    for k in range(col.shape[0] // LANES):
        out.append(to_row(col[k * LANES : (k + 1) * LANES], LANES))
    return jnp.concatenate(out, axis=1)


def slots_of(value, own, count):
    return jnp.concatenate([to_row(value[k * own : (k + 1) * own], own) for k in range(count)], axis=0)


def column_of(value, own, count):
    return jnp.concatenate([to_col(value[k : k + 1], own) for k in range(count)], axis=0)


def fold(block):
    return jnp.sum(block.reshape(block.shape[0] // 8, 8, block.shape[1]), axis=0)


def put_lanes(ref, slots, base, row):
    for k in range(row.shape[1] // LANES):
        piece = row[:, k * LANES : (k + 1) * LANES]
        for s in range(slots):
            ref[s, base + k : base + k + 1, :] = piece


def pack(own, width, jsrc, x_ref, gy_ref, f_ref, g_ref, w_ref, ipack_ref, jpack_ref, block_ref, line_ref, vec_ref, in_sem, out_sem):
    copies = [
        pltpu.make_async_copy(f_ref, vec_ref.at[0], in_sem.at[2]),
        pltpu.make_async_copy(w_ref, vec_ref.at[1], in_sem.at[3]),
        pltpu.make_async_copy(g_ref, vec_ref.at[2], in_sem.at[4]),
        pltpu.make_async_copy(x_ref, block_ref.at[pl.ds(0, own)], in_sem.at[0]),
        pltpu.make_async_copy(gy_ref, block_ref.at[pl.ds(own, own)], in_sem.at[1]),
    ]
    for copy in copies:
        copy.start()
    line_ref[...] = jnp.zeros_like(line_ref)
    for copy in copies:
        copy.wait()
    line_ref[0, 0:1, 0:own] = vec_ref[0].astype(F32)
    line_ref[0, 1:2, 0:own] = vec_ref[1].astype(F32)
    line_ref[1, 0:1, 0:own] = vec_ref[2].astype(F32)
    block_ref[2 * own : 2 * own + AUX, :] = line_ref[1].astype(BF16)
    outs = [pltpu.make_async_copy(block_ref, jpack_ref.at[s], out_sem.at[s]) for s in range(jsrc)]
    for copy in outs:
        copy.start()
    ipack_ref[0:own, :] = block_ref[0:own, :]
    ipack_ref[own : own + AUX, :] = line_ref[0].astype(BF16)
    for copy in outs:
        copy.wait()


def stack(own, count, *refs):
    out_ref = refs[count]
    size = own + AUX
    for k in range(count):
        place = behind("row", k, count)
        out_ref[pl.ds(pl.multiple_of(place * size, size), size), :] = refs[k][...]


GROUP = 4
NT = (((1,), (1,)), ((), ()))
TN = (((0,), (0,)), ((), ()))


def behind(axis, k, count):
    return lax.rem(lax.axis_index(axis) + (count - k), count)


def build(own, width, isrc, jsrc, *refs):
    steps = isrc // GROUP
    pi_refs, pj_ref = refs[:steps], refs[steps]
    plan_ref, inner_ref, xi_ref, w_ref, mass_ref, col_ref, xj_ref, gj_ref = refs[steps + 1 :]
    cols = jsrc * own
    size = own + AUX
    scale = 1.0 / (2.0 * width * EPS)
    bias = []
    for k in range(jsrc):
        part = pj_ref[k, 0:own, :]
        xj_ref[k * own : (k + 1) * own, :] = part
        gj_ref[k * own : (k + 1) * own, :] = pj_ref[k, own : 2 * own, :]
        pf = part.astype(F32)
        sq = jnp.sum(pf * pf, axis=1, keepdims=True)
        pot = to_col(pj_ref[k, 2 * own : 2 * own + AUX, :].astype(F32)[0:1, 0:LANES], own)
        bias.append(pot / EPS - sq * scale)
    jbias = lanes_of(jnp.concatenate(bias, axis=0))
    xj = xj_ref[...]
    gj = gj_ref[...]
    span = GROUP * own
    cmass = cph = None
    for m in range(steps):
        src = pi_refs[m]
        t = behind("y", m, steps)
        base = pl.multiple_of(t * span, span)
        first = pl.multiple_of(t * GROUP, GROUP)
        ibias = []
        for k in range(GROUP):
            part = src[k * size : k * size + own, :]
            xi_ref[pl.ds(pl.multiple_of(base + k * own, own), own), :] = part
            aux = src[k * size + own : (k + 1) * size, :].astype(F32)
            w_ref[pl.ds(first + k, 1), :] = aux[1:2, 0:LANES]
            pf = part.astype(F32)
            sq = jnp.sum(pf * pf, axis=1, keepdims=True)
            ibias.append(to_col(aux[0:1, 0:LANES], own) / EPS - sq * scale)
        ibias = jnp.concatenate(ibias, axis=0)
        part = xi_ref[pl.ds(base, span), :]
        cross = lax.dot_general(part, xj, NT, preferred_element_type=F32)
        plan = jnp.exp(cross * (2.0 * scale) + jbias + ibias)
        plan_ref[pl.ds(base, span), :] = plan
        inner = lax.dot_general(part, gj, NT, preferred_element_type=F32)
        inner_ref[pl.ds(base, span), :] = inner
        weighted = plan * inner
        mass = slots_of(jnp.sum(plan, axis=1, keepdims=True), own, GROUP)
        ph = slots_of(jnp.sum(weighted, axis=1, keepdims=True), own, GROUP)
        for k in range(GROUP):
            mass_ref[0, pl.ds(first + k, 1), :] = mass[k : k + 1]
            mass_ref[0, pl.ds(isrc + first + k, 1), :] = ph[k : k + 1]
        plan, weighted = fold(plan), fold(weighted)
        cmass = plan if cmass is None else cmass + plan
        cph = weighted if cph is None else cph + weighted
    for s in range(1, isrc):
        mass_ref[s] = mass_ref[0]
    col_ref[...] = jnp.zeros_like(col_ref)
    cmass = jnp.sum(cmass, axis=0, keepdims=True)
    cph = jnp.sum(cph, axis=0, keepdims=True)
    for k in range(cols // LANES):
        col_ref[k : k + 1, :] = cmass[:, k * LANES : (k + 1) * LANES]
        col_ref[8 + k : 9 + k, :] = cph[:, k * LANES : (k + 1) * LANES]


def apply_cols(own, isrc, phi, plan_ref):
    span = GROUP * own
    acc = None
    for t in range(isrc // GROUP):
        col = column_of(phi[t * GROUP : (t + 1) * GROUP], own, GROUP)
        part = fold(plan_ref[t * span : (t + 1) * span, :] * col)
        acc = part if acc is None else acc + part
    return jnp.sum(acc, axis=0, keepdims=True)


def valid(own, value):
    lanes = lax.broadcasted_iota(jnp.int32, value.shape, 1)
    return jnp.where(lanes < own, value, 0.0)


def phi_first(own, isrc, jsrc, got_ref, col_ref, plan_ref, mass_ref, send_ref):
    total = jnp.sum(got_ref[...], axis=0)
    mass_ref[...] = total
    phi = valid(own, -total[isrc:] / total[:isrc])
    applied = apply_cols(own, isrc, phi, plan_ref)
    for s in range(jsrc):
        send_ref[s, 0:16, :] = col_ref[...]
        send_ref[s, 16:24, :] = jnp.zeros((8, LANES), F32)
    put_lanes(send_ref, jsrc, 16, applied)


def phi_next(own, isrc, jsrc, got_ref, mass_ref, w_ref, plan_ref, phi_ref, send_ref):
    total = jnp.sum(got_ref[...], axis=0)
    mass = mass_ref[...]
    phi = valid(own, -(mass[isrc:] + total) / mass[:isrc])
    phi_ref[...] = phi
    applied = apply_cols(own, isrc, phi, plan_ref)
    wts = valid(own, w_ref[...])
    wsum = jnp.sum(wts, axis=0, keepdims=True)
    wphi = jnp.sum(wts * phi, axis=0, keepdims=True)
    for s in range(jsrc):
        send_ref[s, 6:7, :] = wsum
        send_ref[s, 7:8, :] = wphi
    put_lanes(send_ref, jsrc, 0, applied)


def row_of(value, count):
    return jnp.concatenate([value[k : k + 1, :] for k in range(count)], axis=1)


def apply_rows(own, isrc, psi, plan_ref, send_ref):
    span = GROUP * own
    for t in range(isrc // GROUP):
        col = jnp.sum(plan_ref[t * span : (t + 1) * span, :] * psi, axis=1, keepdims=True)
        part = slots_of(col, own, GROUP)
        for s in range(isrc):
            send_ref[s, t * GROUP : (t + 1) * GROUP, :] = part


def psi_first(own, isrc, got_ref, plan_ref, col_ref, send_ref):
    total = jnp.sum(got_ref[...], axis=0)
    col_ref[...] = total[:16]
    count = plan_ref.shape[1] // LANES
    psi = row_of(-(total[8:16] + total[16:24]) / total[0:8], count)
    apply_rows(own, isrc, psi, plan_ref, send_ref)


def psi_next(own, isrc, got_ref, col_ref, plan_ref, send_ref, *psi_refs):
    total = jnp.sum(got_ref[...], axis=0)
    count = plan_ref.shape[1] // LANES
    psi = -(col_ref[8:16] + total) / col_ref[0:8]
    for ref in psi_refs:
        ref[...] = psi
    apply_rows(own, isrc, row_of(psi, count), plan_ref, send_ref)


def bit_of(axis, bit):
    return lax.rem(lax.shift_right_logical(lax.axis_index(axis), bit), 2)


def early_cols(own, width, isrc, jsrc, phi_ref, psi_ref, plan_ref, inner_ref, xi_ref, keep_ref, send_ref, acc_ref):
    cols = plan_ref.shape[1]
    psi = row_of(psi_ref[...], cols // LANES)
    span = GROUP * own
    for t in range(isrc // GROUP):
        at = slice(t * span, (t + 1) * span)
        col = column_of(phi_ref[t * GROUP : (t + 1) * GROUP, :], own, GROUP)
        plan = plan_ref[at, :]
        mixed = (plan * (inner_ref[at, :] + (col + psi))).astype(BF16)
        part = xi_ref[at, :]
        for q, value in enumerate((mixed, plan.astype(BF16))):
            term = lax.dot_general(value, part, TN, preferred_element_type=F32)
            place = slice(q * cols, (q + 1) * cols)
            if t:
                term = acc_ref[place, :] + term
            acc_ref[place, :] = term
    scale = 1.0 / (width * EPS)
    mine = bit_of("z", 0)
    for q in range(2):
        for m in range(jsrc // 2):
            keep = pl.ds(pl.multiple_of(q * cols + (2 * m + mine) * own, own), own)
            give = pl.ds(pl.multiple_of(q * cols + (2 * m + 1 - mine) * own, own), own)
            first = q * (cols // 2) + m * own
            at = slice(first, first + own)
            keep_ref[at, :] = acc_ref[keep, :] * scale
            send_ref[at, :] = (acc_ref[give, :] * scale).astype(BF16)


def halve(own, bit, keep_ref, got_ref, next_ref, send_ref):
    mine = bit_of("z", bit)
    size, out = keep_ref.shape[0] // 2, next_ref.shape[0] // 2
    for q in range(2):
        for m in range(out // own):
            keep = pl.ds(pl.multiple_of(q * size + (2 * m + mine) * own, own), own)
            give = pl.ds(pl.multiple_of(q * size + (2 * m + 1 - mine) * own, own), own)
            first = q * out + m * own
            at = slice(first, first + own)
            next_ref[at, :] = keep_ref[keep, :] + got_ref[keep, :].astype(F32)
            send_ref[at, :] = (keep_ref[give, :] + got_ref[give, :].astype(F32)).astype(BF16)


def finish_rows(own, width, isrc, every, *refs):
    got_ref, col_ref, phi_ref, psi_ref, plan_hbm, xi_hbm, pj_hbm, after_ref = refs[:8]
    row_ref, gw_ref, delta_ref, plan_ref, xi_ref, xj_ref, gj_ref, sem = refs[8:]
    span = GROUP * own
    steps = isrc // GROUP
    jsrc = pj_hbm.shape[0]
    head = []
    for k in range(jsrc):
        place = pl.ds(k * own, own)
        for n, ref in enumerate((gj_ref, xj_ref)):
            first = own if n == 0 else 0
            head.append(pltpu.make_async_copy(pj_hbm.at[k, pl.ds(first, own)], ref.at[place], sem.at[2 * steps + 2 * k + n]))
    parts = []
    for t in range(steps):
        at = pl.ds(t * span, span)
        pairs = ((xi_hbm, xi_ref), (plan_hbm, plan_ref))
        parts.append([pltpu.make_async_copy(a.at[at], b.at[at], sem.at[2 * t + n]) for n, (a, b) in enumerate(pairs)])
    for copy in head + sum(parts, []):
        copy.start()
    total = jnp.sum(got_ref[...], axis=0)
    cols = plan_ref.shape[1]
    psi = -(col_ref[8:16] + total) / col_ref[0:8]
    delta = row_of(psi - psi_ref[...], cols // LANES)
    psi = row_of(psi, cols // LANES)
    rows = lax.broadcasted_iota(jnp.int32, (own, cols), 0)
    lanes = lax.broadcasted_iota(jnp.int32, (own, cols), 1)
    first = lax.axis_index("z") * own
    delta_ref[...] = jnp.sum(jnp.where(lanes == rows + first, delta, 0.0), axis=1, keepdims=True)
    wsum = jnp.sum(total[6:7], axis=1, keepdims=True)
    wphi = jnp.sum(total[7:8], axis=1, keepdims=True)
    gw_ref[...] = -(every / wsum) * (phi_ref[...] - wphi / wsum)
    scale = 1.0 / (width * EPS)
    for copy in head:
        copy.wait()
    xj = xj_ref[...]
    gj = gj_ref[...]
    for t in range(steps):
        at = slice(t * span, (t + 1) * span)
        col = column_of(phi_ref[t * GROUP : (t + 1) * GROUP, :], own, GROUP)
        for copy in parts[t]:
            copy.wait()
        plan = plan_ref[at, :]
        inner = lax.dot_general(xi_ref[at, :], gj, NT, preferred_element_type=F32)
        mixed = plan * (inner + (col + psi))
        qrow = jnp.sum(mixed, axis=1, keepdims=True)
        base = jnp.dot(plan.astype(BF16), gj, preferred_element_type=F32)
        term = jnp.dot(mixed.astype(BF16), xj, preferred_element_type=F32)
        term = base + (term - qrow * xi_ref[at, :].astype(F32)) * scale
        term = term.astype(BF16)
        for k in range(GROUP):
            row_ref[t * GROUP + k] = term[k * own : (k + 1) * own]


def total_up(own, rows_ref, keep_ref, got_ref, delta_ref, out_ref):
    acc = jnp.sum(rows_ref[...].astype(F32), axis=0)
    sums = keep_ref[...] + got_ref[...].astype(F32)
    out_ref[...] = (acc + (sums[:own] + delta_ref[...] * sums[own:])).astype(BF16)


def local(particles, cotangent, row_potential, col_potential, weights):
    own, width = particles.shape
    iaxes, jaxes = ("y", "row"), ("z",)
    ysrc, xsrc = lax.axis_size("y"), lax.axis_size("row")
    isrc, jsrc = ysrc * xsrc, lax.axis_size("z")
    rows, cols = isrc * own, jsrc * own

    def swap(value, axes):
        return lax.all_to_all(value, axes, 0, 0, tiled=True)

    def shift(value, axis, k):
        n = lax.axis_size(axis)
        return lax.ppermute(value, axis, [(i, (i + k) % n) for i in range(n)])

    def flip(value, bit):
        return lax.ppermute(value, "z", [(i, i ^ bit) for i in range(jsrc)])

    def call(body, micros, outs, *args, scratch=(), in_specs=None, out_specs=None, mib=12, hbm=()):
        return pl.pallas_call(
            body,
            out_shape=[(pltpu.HBM if n in hbm else jax.ShapeDtypeStruct)(s, d) for n, (s, d) in enumerate(outs)],
            in_specs=in_specs or whole(len(args)),
            out_specs=out_specs or whole(len(outs)),
            scratch_shapes=list(scratch),
            compiler_params=params(mib),
            cost_estimate=pl.CostEstimate(flops=int(micros * 1e9), bytes_accessed=1024, transcendentals=0),
        )(*args)

    anywhere = pl.BlockSpec(memory_space=pltpu.HBM)
    ipack, jpack = call(
        functools.partial(pack, own, width, jsrc),
        2,
        [((own + AUX, width), BF16), ((jsrc, 2 * own + AUX, width), BF16)],
        *[
            pltpu.with_memory_space_constraint(v, pltpu.HBM)
            for v in (
                particles,
                cotangent,
                row_potential.reshape(1, own),
                col_potential.reshape(1, own),
                weights.reshape(1, own),
            )
        ],
        scratch=[
            pltpu.VMEM((2 * own + AUX, width), BF16),
            pltpu.VMEM((2, AUX, width), F32),
            pltpu.VMEM((3, 1, own), BF16),
            pltpu.SemaphoreType.DMA((5,)),
            pltpu.SemaphoreType.DMA((jsrc,)),
        ],
        in_specs=[anywhere] * 5,
        out_specs=whole(1) + [anywhere],
        hbm=(1,),
    )
    jgot = swap(jpack, jaxes)
    near = [shift(ipack, "row", k) for k in range(1, xsrc)]
    (line,) = call(
        functools.partial(stack, own, xsrc), 1, [((xsrc * (own + AUX), width), BF16)], ipack, *near
    )
    igot = [line] + [shift(line, "y", k) for k in range(1, ysrc)]
    plan, inner, xi, wts, send, col_part = call(
        functools.partial(build, own, width, isrc, jsrc),
        5,
        [
            ((rows, cols), F32),
            ((rows, cols), F32),
            ((rows, width), BF16),
            ((isrc, LANES), F32),
            ((isrc, 2 * isrc, LANES), F32),
            ((16, LANES), F32),
        ],
        *igot,
        jgot,
        scratch=[pltpu.VMEM((cols, width), BF16), pltpu.VMEM((cols, width), BF16)],
    )
    got = swap(send, iaxes)
    mass, send = call(
        functools.partial(phi_first, own, isrc, jsrc),
        1,
        [((2 * isrc, LANES), F32), ((jsrc, 24, LANES), F32)],
        got,
        col_part,
        plan,
    )
    got = swap(send, jaxes)
    col, send = call(
        functools.partial(psi_first, own, isrc),
        1,
        [((16, LANES), F32), ((isrc, isrc, LANES), F32)],
        got,
        plan,
    )
    for step in range(1, ITERS):
        got = swap(send, iaxes)
        phi, send = call(
            functools.partial(phi_next, own, isrc, jsrc),
            1,
            [((isrc, LANES), F32), ((jsrc, 8, LANES), F32)],
            got,
            mass,
            wts,
            plan,
        )
        if step < ITERS - 1:
            got = swap(send, jaxes)
            send, *kept = call(
                functools.partial(psi_next, own, isrc),
                1,
                [((isrc, isrc, LANES), F32)] + [((8, LANES), F32)] * (step == ITERS - 2),
                got,
                col,
                plan,
            )
    half = cols
    keep, give = call(
        functools.partial(early_cols, own, width, isrc, jsrc),
        3,
        [((half, width), F32), ((half, width), BF16)],
        phi,
        *kept,
        plan,
        inner,
        xi,
        scratch=[pltpu.VMEM((2 * cols, width), F32)],
    )
    send, give = lax.optimization_barrier((send, give))
    taken = flip(give, 1)
    got = swap(send, jaxes)
    half //= 2
    keep, give = call(
        functools.partial(halve, own, 1), 1, [((half, width), F32), ((half, width), BF16)], keep, taken
    )
    taken = flip(give, 2)
    row_send, gw, delta = call(
        functools.partial(finish_rows, own, width, isrc, float(isrc * jsrc * own)),
        4,
        [((isrc, own, width), BF16), ((isrc, LANES), F32), ((own, 1), F32)],
        got,
        col,
        phi,
        *kept,
        *[pltpu.with_memory_space_constraint(v, pltpu.HBM) for v in (plan, xi, jgot)],
        keep,
        scratch=[
            pltpu.VMEM((rows, cols), F32),
            pltpu.VMEM((rows, width), BF16),
            pltpu.VMEM((cols, width), BF16),
            pltpu.VMEM((cols, width), BF16),
            pltpu.SemaphoreType.DMA((2 * (isrc // GROUP) + 2 * jsrc,)),
        ],
        in_specs=whole(4) + [anywhere] * 3 + whole(1),
        mib=24,
    )
    row_send, taken = lax.optimization_barrier((row_send, taken))
    half //= 2
    keep, give = call(
        functools.partial(halve, own, 2), 1, [((half, width), F32), ((half, width), BF16)], keep, taken
    )
    taken = flip(give, 4)
    row_got = swap(row_send, iaxes)
    (grad,) = call(
        functools.partial(total_up, own), 1, [((own, width), BF16)], row_got, keep, taken, delta
    )
    mine = lax.axis_index("y") * xsrc + lax.axis_index("row")
    grad_weights = lax.dynamic_slice(gw, (mine, 0), (1, own)).reshape(own)
    return (grad, grad_weights)


def solution(mesh):
    filt, row, col = mesh.devices.shape
    split = Mesh(mesh.devices.reshape(filt, row, 8, col // 8), ("filt", "row", "z", "y"))
    spec = ("filt", "row", "z", "y")
    return jax.shard_map(
        local,
        mesh=split,
        in_specs=(P(spec, None), P(spec, None), P(spec), P(spec), P(spec)),
        out_specs=(P(spec, None), P(spec)),
        check_vma=False,
    )
```

```python
import functools

import jax
import jax.numpy as jnp
from jax import lax
from jax.experimental import pallas as pl
from jax.experimental.pallas import tpu as pltpu
from jax.sharding import Mesh
from jax.sharding import PartitionSpec as P

ITERS = 4


EPS = 0.09

LANES = 128
AUX = 8
F32 = jnp.float32
BF16 = jnp.bfloat16


def params(mib):
    return pltpu.CompilerParams(vmem_limit_bytes=mib << 20)


def whole(n):
    return [pl.BlockSpec(memory_space=pltpu.VMEM)] * n


def eye(own):
    rows = lax.broadcasted_iota(jnp.int32, (own, LANES), 0)
    lanes = lax.broadcasted_iota(jnp.int32, (own, LANES), 1)
    return rows == lanes


def to_row(col, own):
    return jnp.sum(jnp.where(eye(own), col, 0.0), axis=0, keepdims=True)


def to_col(row, own):
    return jnp.sum(jnp.where(eye(own), row, 0.0), axis=1, keepdims=True)


def lanes_of(col):
    out = []
    for k in range(col.shape[0] // LANES):
        out.append(to_row(col[k * LANES : (k + 1) * LANES], LANES))
    return jnp.concatenate(out, axis=1)


def slots_of(value, own, count):
    return jnp.concatenate([to_row(value[k * own : (k + 1) * own], own) for k in range(count)], axis=0)


def column_of(value, own, count):
    return jnp.concatenate([to_col(value[k : k + 1], own) for k in range(count)], axis=0)


def fold(block):
    return jnp.sum(block.reshape(block.shape[0] // 8, 8, block.shape[1]), axis=0)


def put_lanes(ref, slots, base, row):
    for k in range(row.shape[1] // LANES):
        piece = row[:, k * LANES : (k + 1) * LANES]
        for s in range(slots):
            ref[s, base + k : base + k + 1, :] = piece


def pack(own, width, jsrc, x_ref, gy_ref, f_ref, g_ref, w_ref, ipack_ref, jpack_ref, block_ref, line_ref, vec_ref, in_sem, out_sem):
    copies = [
        pltpu.make_async_copy(f_ref, vec_ref.at[0], in_sem.at[2]),
        pltpu.make_async_copy(w_ref, vec_ref.at[1], in_sem.at[3]),
        pltpu.make_async_copy(g_ref, vec_ref.at[2], in_sem.at[4]),
        pltpu.make_async_copy(x_ref, block_ref.at[pl.ds(0, own)], in_sem.at[0]),
        pltpu.make_async_copy(gy_ref, block_ref.at[pl.ds(own, own)], in_sem.at[1]),
    ]
    for copy in copies:
        copy.start()
    line_ref[...] = jnp.zeros_like(line_ref)
    for copy in copies:
        copy.wait()
    line_ref[0, 0:1, 0:own] = vec_ref[0].astype(F32)
    line_ref[0, 1:2, 0:own] = vec_ref[1].astype(F32)
    line_ref[1, 0:1, 0:own] = vec_ref[2].astype(F32)
    block_ref[2 * own : 2 * own + AUX, :] = line_ref[1].astype(BF16)
    outs = [pltpu.make_async_copy(block_ref, jpack_ref.at[s], out_sem.at[s]) for s in range(jsrc)]
    for copy in outs:
        copy.start()
    ipack_ref[0:own, :] = block_ref[0:own, :]
    ipack_ref[own : own + AUX, :] = line_ref[0].astype(BF16)
    for copy in outs:
        copy.wait()


def stack(own, count, *refs):
    out_ref = refs[count]
    size = own + AUX
    for k in range(count):
        place = behind("row", k, count)
        out_ref[pl.ds(pl.multiple_of(place * size, size), size), :] = refs[k][...]


GROUP = 4
NT = (((1,), (1,)), ((), ()))
TN = (((0,), (0,)), ((), ()))


def behind(axis, k, count):
    return lax.rem(lax.axis_index(axis) + (count - k), count)


def build(own, width, isrc, jsrc, *refs):
    steps = isrc // GROUP
    pi_refs, pj_ref = refs[:steps], refs[steps]
    plan_ref, inner_ref, xi_ref, w_ref, mass_ref, col_ref, xj_ref, gj_ref = refs[steps + 1 :]
    cols = jsrc * own
    size = own + AUX
    scale = 1.0 / (2.0 * width * EPS)
    bias = []
    for k in range(jsrc):
        part = pj_ref[k, 0:own, :]
        xj_ref[k * own : (k + 1) * own, :] = part
        gj_ref[k * own : (k + 1) * own, :] = pj_ref[k, own : 2 * own, :]
        pf = part.astype(F32)
        sq = jnp.sum(pf * pf, axis=1, keepdims=True)
        pot = to_col(pj_ref[k, 2 * own : 2 * own + AUX, :].astype(F32)[0:1, 0:LANES], own)
        bias.append(pot / EPS - sq * scale)
    jbias = lanes_of(jnp.concatenate(bias, axis=0))
    xj = xj_ref[...]
    gj = gj_ref[...]
    span = GROUP * own
    cmass = cph = None
    for m in range(steps):
        src = pi_refs[m]
        t = behind("y", m, steps)
        base = pl.multiple_of(t * span, span)
        first = pl.multiple_of(t * GROUP, GROUP)
        ibias = []
        for k in range(GROUP):
            part = src[k * size : k * size + own, :]
            xi_ref[pl.ds(pl.multiple_of(base + k * own, own), own), :] = part
            aux = src[k * size + own : (k + 1) * size, :].astype(F32)
            w_ref[pl.ds(first + k, 1), :] = aux[1:2, 0:LANES]
            pf = part.astype(F32)
            sq = jnp.sum(pf * pf, axis=1, keepdims=True)
            ibias.append(to_col(aux[0:1, 0:LANES], own) / EPS - sq * scale)
        ibias = jnp.concatenate(ibias, axis=0)
        part = xi_ref[pl.ds(base, span), :]
        cross = lax.dot_general(part, xj, NT, preferred_element_type=F32)
        plan = jnp.exp(cross * (2.0 * scale) + jbias + ibias)
        plan_ref[pl.ds(base, span), :] = plan
        inner = lax.dot_general(part, gj, NT, preferred_element_type=F32)
        inner_ref[pl.ds(base, span), :] = inner
        weighted = plan * inner
        mass = slots_of(jnp.sum(plan, axis=1, keepdims=True), own, GROUP)
        ph = slots_of(jnp.sum(weighted, axis=1, keepdims=True), own, GROUP)
        for k in range(GROUP):
            mass_ref[0, pl.ds(first + k, 1), :] = mass[k : k + 1]
            mass_ref[0, pl.ds(isrc + first + k, 1), :] = ph[k : k + 1]
        plan, weighted = fold(plan), fold(weighted)
        cmass = plan if cmass is None else cmass + plan
        cph = weighted if cph is None else cph + weighted
    for s in range(1, isrc):
        mass_ref[s] = mass_ref[0]
    col_ref[...] = jnp.zeros_like(col_ref)
    cmass = jnp.sum(cmass, axis=0, keepdims=True)
    cph = jnp.sum(cph, axis=0, keepdims=True)
    for k in range(cols // LANES):
        col_ref[k : k + 1, :] = cmass[:, k * LANES : (k + 1) * LANES]
        col_ref[8 + k : 9 + k, :] = cph[:, k * LANES : (k + 1) * LANES]


def apply_cols(own, isrc, phi, plan_ref):
    span = GROUP * own
    acc = None
    for t in range(isrc // GROUP):
        col = column_of(phi[t * GROUP : (t + 1) * GROUP], own, GROUP)
        part = fold(plan_ref[t * span : (t + 1) * span, :] * col)
        acc = part if acc is None else acc + part
    return jnp.sum(acc, axis=0, keepdims=True)


def valid(own, value):
    lanes = lax.broadcasted_iota(jnp.int32, value.shape, 1)
    return jnp.where(lanes < own, value, 0.0)


def phi_first(own, isrc, jsrc, got_ref, col_ref, plan_ref, mass_ref, send_ref):
    total = jnp.sum(got_ref[...], axis=0)
    mass_ref[...] = total
    phi = valid(own, -total[isrc:] / total[:isrc])
    applied = apply_cols(own, isrc, phi, plan_ref)
    for s in range(jsrc):
        send_ref[s, 0:16, :] = col_ref[...]
        send_ref[s, 16:24, :] = jnp.zeros((8, LANES), F32)
    put_lanes(send_ref, jsrc, 16, applied)


def phi_next(own, isrc, jsrc, got_ref, mass_ref, w_ref, plan_ref, phi_ref, send_ref):
    total = jnp.sum(got_ref[...], axis=0)
    mass = mass_ref[...]
    phi = valid(own, -(mass[isrc:] + total) / mass[:isrc])
    phi_ref[...] = phi
    applied = apply_cols(own, isrc, phi, plan_ref)
    wts = valid(own, w_ref[...])
    wsum = jnp.sum(wts, axis=0, keepdims=True)
    wphi = jnp.sum(wts * phi, axis=0, keepdims=True)
    for s in range(jsrc):
        send_ref[s, 6:7, :] = wsum
        send_ref[s, 7:8, :] = wphi
    put_lanes(send_ref, jsrc, 0, applied)


def row_of(value, count):
    return jnp.concatenate([value[k : k + 1, :] for k in range(count)], axis=1)


def apply_rows(own, isrc, psi, plan_ref, send_ref):
    span = GROUP * own
    for t in range(isrc // GROUP):
        col = jnp.sum(plan_ref[t * span : (t + 1) * span, :] * psi, axis=1, keepdims=True)
        part = slots_of(col, own, GROUP)
        for s in range(isrc):
            send_ref[s, t * GROUP : (t + 1) * GROUP, :] = part


def psi_first(own, isrc, got_ref, plan_ref, col_ref, send_ref):
    total = jnp.sum(got_ref[...], axis=0)
    col_ref[...] = total[:16]
    count = plan_ref.shape[1] // LANES
    psi = row_of(-(total[8:16] + total[16:24]) / total[0:8], count)
    apply_rows(own, isrc, psi, plan_ref, send_ref)


def psi_next(own, isrc, got_ref, col_ref, plan_ref, send_ref, *psi_refs):
    total = jnp.sum(got_ref[...], axis=0)
    count = plan_ref.shape[1] // LANES
    psi = -(col_ref[8:16] + total) / col_ref[0:8]
    for ref in psi_refs:
        ref[...] = psi
    apply_rows(own, isrc, row_of(psi, count), plan_ref, send_ref)


def bit_of(axis, bit):
    return lax.rem(lax.shift_right_logical(lax.axis_index(axis), bit), 2)


def phi_last(own, width, isrc, jsrc, *refs):
    got_ref, mass_ref, w_ref, psi_ref, plan_ref, inner_ref, xi_ref = refs[:7]
    phi_ref, send_hbm, keep_ref, give_ref, send_ref, mixed_ref, acc_ref, sem = refs[7:]
    phi_next(own, isrc, jsrc, got_ref, mass_ref, w_ref, plan_ref, phi_ref, send_ref)
    sent = pltpu.make_async_copy(send_ref, send_hbm, sem)
    sent.start()
    cols = plan_ref.shape[1]
    psi = row_of(psi_ref[...], cols // LANES)
    span = GROUP * own
    for t in range(isrc // GROUP):
        at = slice(t * span, (t + 1) * span)
        col = column_of(phi_ref[t * GROUP : (t + 1) * GROUP, :], own, GROUP)
        plan = plan_ref[at, :]
        mixed_ref[0, at, :] = (plan * (inner_ref[at, :] + (col + psi))).astype(BF16)
        mixed_ref[1, at, :] = plan.astype(BF16)
    part = xi_ref[...]
    for q in range(2):
        term = lax.dot_general(mixed_ref[q], part, TN, preferred_element_type=F32)
        acc_ref[q * cols : (q + 1) * cols, :] = term
    scale = 1.0 / (width * EPS)
    mine = bit_of("z", 0)
    for q in range(2):
        for m in range(jsrc // 2):
            keep = pl.ds(pl.multiple_of(q * cols + (2 * m + mine) * own, own), own)
            give = pl.ds(pl.multiple_of(q * cols + (2 * m + 1 - mine) * own, own), own)
            first = q * (cols // 2) + m * own
            at = slice(first, first + own)
            keep_ref[at, :] = acc_ref[keep, :] * scale
            give_ref[at, :] = (acc_ref[give, :] * scale).astype(BF16)
    sent.wait()


def halve(own, bit, keep_ref, got_ref, next_ref, send_ref):
    mine = bit_of("z", bit)
    size, out = keep_ref.shape[0] // 2, next_ref.shape[0] // 2
    for q in range(2):
        for m in range(out // own):
            keep = pl.ds(pl.multiple_of(q * size + (2 * m + mine) * own, own), own)
            give = pl.ds(pl.multiple_of(q * size + (2 * m + 1 - mine) * own, own), own)
            first = q * out + m * own
            at = slice(first, first + own)
            next_ref[at, :] = keep_ref[keep, :] + got_ref[keep, :].astype(F32)
            send_ref[at, :] = (keep_ref[give, :] + got_ref[give, :].astype(F32)).astype(BF16)


def finish_rows(own, width, isrc, every, *refs):
    got_ref, col_ref, phi_ref, psi_ref, plan_hbm, xi_hbm, pj_hbm, after_ref = refs[:8]
    row_hbm, gw_ref, delta_ref, row_ref, plan_ref, xi_ref, xj_ref, gj_ref, sem, out_sem = refs[8:]
    span = GROUP * own
    steps = isrc // GROUP
    jsrc = pj_hbm.shape[0]
    head = []
    for k in range(jsrc):
        place = pl.ds(k * own, own)
        for n, ref in enumerate((gj_ref, xj_ref)):
            first = own if n == 0 else 0
            head.append(pltpu.make_async_copy(pj_hbm.at[k, pl.ds(first, own)], ref.at[place], sem.at[2 * steps + 2 * k + n]))
    parts = []
    for t in range(steps):
        at = pl.ds(t * span, span)
        pairs = ((xi_hbm, xi_ref), (plan_hbm, plan_ref))
        parts.append([pltpu.make_async_copy(a.at[at], b.at[at], sem.at[2 * t + n]) for n, (a, b) in enumerate(pairs)])
    for copy in head + parts[0] + parts[1]:
        copy.start()
    total = jnp.sum(got_ref[...], axis=0)
    cols = plan_ref.shape[1]
    psi = -(col_ref[8:16] + total) / col_ref[0:8]
    delta = row_of(psi - psi_ref[...], cols // LANES)
    psi = row_of(psi, cols // LANES)
    rows = lax.broadcasted_iota(jnp.int32, (own, cols), 0)
    lanes = lax.broadcasted_iota(jnp.int32, (own, cols), 1)
    first = lax.axis_index("z") * own
    delta_ref[...] = jnp.sum(jnp.where(lanes == rows + first, delta, 0.0), axis=1, keepdims=True)
    wsum = jnp.sum(total[6:7], axis=1, keepdims=True)
    wphi = jnp.sum(total[7:8], axis=1, keepdims=True)
    gw_ref[...] = -(every / wsum) * (phi_ref[...] - wphi / wsum)
    scale = 1.0 / (width * EPS)
    outs = []
    for copy in head:
        copy.wait()
    xj = xj_ref[...]
    gj = gj_ref[...]
    for t in range(steps):
        at = slice(t * span, (t + 1) * span)
        col = column_of(phi_ref[t * GROUP : (t + 1) * GROUP, :], own, GROUP)
        for copy in parts[t]:
            copy.wait()
        if t + 2 < steps:
            for copy in parts[t + 2]:
                copy.start()
        plan = plan_ref[at, :]
        inner = lax.dot_general(xi_ref[at, :], gj, NT, preferred_element_type=F32)
        mixed = plan * (inner + (col + psi))
        qrow = jnp.sum(mixed, axis=1, keepdims=True)
        base = jnp.dot(plan.astype(BF16), gj, preferred_element_type=F32)
        term = jnp.dot(mixed.astype(BF16), xj, preferred_element_type=F32)
        term = base + (term - qrow * xi_ref[at, :].astype(F32)) * scale
        term = term.astype(BF16)
        for k in range(GROUP):
            row_ref[t * GROUP + k] = term[k * own : (k + 1) * own]
        group = pl.ds(t * GROUP, GROUP)
        outs.append(pltpu.make_async_copy(row_ref.at[group], row_hbm.at[group], out_sem.at[t]))
        outs[t].start()
    for copy in outs:
        copy.wait()


def total_up(own, rows_ref, keep_ref, got_ref, delta_ref, out_ref):
    acc = jnp.sum(rows_ref[...].astype(F32), axis=0)
    sums = keep_ref[...] + got_ref[...].astype(F32)
    out_ref[...] = (acc + (sums[:own] + delta_ref[...] * sums[own:])).astype(BF16)


def local(particles, cotangent, row_potential, col_potential, weights):
    own, width = particles.shape
    iaxes, jaxes = ("y", "row"), ("z",)
    ysrc, xsrc = lax.axis_size("y"), lax.axis_size("row")
    isrc, jsrc = ysrc * xsrc, lax.axis_size("z")
    rows, cols = isrc * own, jsrc * own

    def swap(value, axes):
        return lax.all_to_all(value, axes, 0, 0, tiled=True)

    def shift(value, axis, k):
        n = lax.axis_size(axis)
        return lax.ppermute(value, axis, [(i, (i + k) % n) for i in range(n)])

    def flip(value, bit):
        return lax.ppermute(value, "z", [(i, i ^ bit) for i in range(jsrc)])

    def call(body, micros, outs, *args, scratch=(), in_specs=None, out_specs=None, mib=12, hbm=()):
        return pl.pallas_call(
            body,
            out_shape=[(pltpu.HBM if n in hbm else jax.ShapeDtypeStruct)(s, d) for n, (s, d) in enumerate(outs)],
            in_specs=in_specs or whole(len(args)),
            out_specs=out_specs or whole(len(outs)),
            scratch_shapes=list(scratch),
            compiler_params=params(mib),
            cost_estimate=pl.CostEstimate(flops=int(micros * 1e9), bytes_accessed=1024, transcendentals=0),
        )(*args)

    anywhere = pl.BlockSpec(memory_space=pltpu.HBM)
    ipack, jpack = call(
        functools.partial(pack, own, width, jsrc),
        2,
        [((own + AUX, width), BF16), ((jsrc, 2 * own + AUX, width), BF16)],
        *[
            pltpu.with_memory_space_constraint(v, pltpu.HBM)
            for v in (
                particles,
                cotangent,
                row_potential.reshape(1, own),
                col_potential.reshape(1, own),
                weights.reshape(1, own),
            )
        ],
        scratch=[
            pltpu.VMEM((2 * own + AUX, width), BF16),
            pltpu.VMEM((2, AUX, width), F32),
            pltpu.VMEM((3, 1, own), BF16),
            pltpu.SemaphoreType.DMA((5,)),
            pltpu.SemaphoreType.DMA((jsrc,)),
        ],
        in_specs=[anywhere] * 5,
        out_specs=whole(1) + [anywhere],
        hbm=(1,),
    )
    jgot = swap(jpack, jaxes)
    near = [shift(ipack, "row", k) for k in range(1, xsrc)]
    (line,) = call(
        functools.partial(stack, own, xsrc), 1, [((xsrc * (own + AUX), width), BF16)], ipack, *near
    )
    igot = [line] + [shift(line, "y", k) for k in range(1, ysrc)]
    plan, inner, xi, wts, send, col_part = call(
        functools.partial(build, own, width, isrc, jsrc),
        5,
        [
            ((rows, cols), F32),
            ((rows, cols), F32),
            ((rows, width), BF16),
            ((isrc, LANES), F32),
            ((isrc, 2 * isrc, LANES), F32),
            ((16, LANES), F32),
        ],
        *igot,
        jgot,
        scratch=[pltpu.VMEM((cols, width), BF16), pltpu.VMEM((cols, width), BF16)],
    )
    got = swap(send, iaxes)
    mass, send = call(
        functools.partial(phi_first, own, isrc, jsrc),
        1,
        [((2 * isrc, LANES), F32), ((jsrc, 24, LANES), F32)],
        got,
        col_part,
        plan,
    )
    got = swap(send, jaxes)
    col, send = call(
        functools.partial(psi_first, own, isrc),
        1,
        [((16, LANES), F32), ((isrc, isrc, LANES), F32)],
        got,
        plan,
    )
    for step in range(1, ITERS):
        got = swap(send, iaxes)
        if step < ITERS - 1:
            phi, send = call(
                functools.partial(phi_next, own, isrc, jsrc),
                1,
                [((isrc, LANES), F32), ((jsrc, 8, LANES), F32)],
                got,
                mass,
                wts,
                plan,
            )
            got = swap(send, jaxes)
            send, *kept = call(
                functools.partial(psi_next, own, isrc),
                1,
                [((isrc, isrc, LANES), F32)] + [((8, LANES), F32)] * (step == ITERS - 2),
                got,
                col,
                plan,
            )
    half = cols
    phi, send, keep, give = call(
        functools.partial(phi_last, own, width, isrc, jsrc),
        4,
        [((isrc, LANES), F32), ((jsrc, 8, LANES), F32), ((half, width), F32), ((half, width), BF16)],
        got,
        mass,
        wts,
        *kept,
        plan,
        inner,
        xi,
        scratch=[
            pltpu.VMEM((jsrc, 8, LANES), F32),
            pltpu.VMEM((2, rows, cols), BF16),
            pltpu.VMEM((2 * cols, width), F32),
            pltpu.SemaphoreType.DMA,
        ],
        out_specs=whole(1) + [anywhere] + whole(2),
        hbm=(1,),
        mib=20,
    )
    send, give = lax.optimization_barrier((send, give))
    taken = flip(give, 1)
    got = swap(send, jaxes)
    half //= 2
    keep, give = call(
        functools.partial(halve, own, 1), 1, [((half, width), F32), ((half, width), BF16)], keep, taken
    )
    taken = flip(give, 2)
    row_send, gw, delta = call(
        functools.partial(finish_rows, own, width, isrc, float(isrc * jsrc * own)),
        4,
        [((isrc, own, width), BF16), ((isrc, LANES), F32), ((own, 1), F32)],
        got,
        col,
        phi,
        *kept,
        *[pltpu.with_memory_space_constraint(v, pltpu.HBM) for v in (plan, xi, jgot)],
        keep,
        scratch=[
            pltpu.VMEM((isrc, own, width), BF16),
            pltpu.VMEM((rows, cols), F32),
            pltpu.VMEM((rows, width), BF16),
            pltpu.VMEM((cols, width), BF16),
            pltpu.VMEM((cols, width), BF16),
            pltpu.SemaphoreType.DMA((2 * (isrc // GROUP) + 2 * jsrc,)),
            pltpu.SemaphoreType.DMA((isrc // GROUP,)),
        ],
        in_specs=whole(4) + [anywhere] * 3 + whole(1),
        out_specs=[anywhere] + whole(2),
        hbm=(0,),
        mib=24,
    )
    row_send, taken = lax.optimization_barrier((row_send, taken))
    half //= 2
    keep, give = call(
        functools.partial(halve, own, 2), 1, [((half, width), F32), ((half, width), BF16)], keep, taken
    )
    taken = flip(give, 4)
    row_got = swap(row_send, iaxes)
    (grad,) = call(
        functools.partial(total_up, own), 1, [((own, width), BF16)], row_got, keep, taken, delta
    )
    mine = lax.axis_index("y") * xsrc + lax.axis_index("row")
    grad_weights = lax.dynamic_slice(gw, (mine, 0), (1, own)).reshape(own)
    return (grad, grad_weights)


def solution(mesh):
    filt, row, col = mesh.devices.shape
    split = Mesh(mesh.devices.reshape(filt, row, 8, col // 8), ("filt", "row", "z", "y"))
    spec = ("filt", "row", "z", "y")
    return jax.shard_map(
        local,
        mesh=split,
        in_specs=(P(spec, None), P(spec, None), P(spec), P(spec), P(spec)),
        out_specs=(P(spec, None), P(spec)),
        check_vma=False,
    )
```

```python
import functools

import jax
import jax.numpy as jnp
from jax import lax
from jax.experimental import pallas as pl
from jax.experimental.pallas import tpu as pltpu
from jax.sharding import Mesh
from jax.sharding import PartitionSpec as P

ITERS = 4


EPS = 0.09

LANES = 128
AUX = 8
F32 = jnp.float32
BF16 = jnp.bfloat16


def params(mib):
    return pltpu.CompilerParams(vmem_limit_bytes=mib << 20)


def whole(n):
    return [pl.BlockSpec(memory_space=pltpu.VMEM)] * n


def eye(own):
    rows = lax.broadcasted_iota(jnp.int32, (own, LANES), 0)
    lanes = lax.broadcasted_iota(jnp.int32, (own, LANES), 1)
    return rows == lanes


def to_row(col, own):
    return jnp.sum(jnp.where(eye(own), col, 0.0), axis=0, keepdims=True)


def to_col(row, own):
    return jnp.sum(jnp.where(eye(own), row, 0.0), axis=1, keepdims=True)


def lanes_of(col):
    out = []
    for k in range(col.shape[0] // LANES):
        out.append(to_row(col[k * LANES : (k + 1) * LANES], LANES))
    return jnp.concatenate(out, axis=1)


def slots_of(value, own, count):
    return jnp.concatenate([to_row(value[k * own : (k + 1) * own], own) for k in range(count)], axis=0)


def column_of(value, own, count):
    return jnp.concatenate([to_col(value[k : k + 1], own) for k in range(count)], axis=0)


def fold(block):
    return jnp.sum(block.reshape(block.shape[0] // 8, 8, block.shape[1]), axis=0)


def put_lanes(ref, slots, base, row):
    for k in range(row.shape[1] // LANES):
        piece = row[:, k * LANES : (k + 1) * LANES]
        for s in range(slots):
            ref[s, base + k : base + k + 1, :] = piece


def pack(own, width, jsrc, x_ref, gy_ref, f_ref, g_ref, w_ref, ipack_ref, jpack_ref, block_ref, line_ref, vec_ref, in_sem, out_sem):
    copies = [
        pltpu.make_async_copy(f_ref, vec_ref.at[0], in_sem.at[2]),
        pltpu.make_async_copy(w_ref, vec_ref.at[1], in_sem.at[3]),
        pltpu.make_async_copy(g_ref, vec_ref.at[2], in_sem.at[4]),
        pltpu.make_async_copy(x_ref, block_ref.at[pl.ds(0, own)], in_sem.at[0]),
        pltpu.make_async_copy(gy_ref, block_ref.at[pl.ds(own, own)], in_sem.at[1]),
    ]
    for copy in copies:
        copy.start()
    line_ref[...] = jnp.zeros_like(line_ref)
    for copy in copies:
        copy.wait()
    line_ref[0, 0:1, 0:own] = vec_ref[0].astype(F32)
    line_ref[0, 1:2, 0:own] = vec_ref[1].astype(F32)
    line_ref[1, 0:1, 0:own] = vec_ref[2].astype(F32)
    block_ref[2 * own : 2 * own + AUX, :] = line_ref[1].astype(BF16)
    outs = [pltpu.make_async_copy(block_ref, jpack_ref.at[s], out_sem.at[s]) for s in range(jsrc)]
    for copy in outs:
        copy.start()
    ipack_ref[0:own, :] = block_ref[0:own, :]
    ipack_ref[own : own + AUX, :] = line_ref[0].astype(BF16)
    for copy in outs:
        copy.wait()


def stack(own, count, *refs):
    out_ref = refs[count]
    size = own + AUX
    for k in range(count):
        place = behind("row", k, count)
        out_ref[pl.ds(pl.multiple_of(place * size, size), size), :] = refs[k][...]


GROUP = 4
NT = (((1,), (1,)), ((), ()))
TN = (((0,), (0,)), ((), ()))


def behind(axis, k, count):
    return lax.rem(lax.axis_index(axis) + (count - k), count)


def build(own, width, isrc, jsrc, *refs):
    steps = isrc // GROUP
    pi_refs, pj_ref = refs[:steps], refs[steps]
    plan_ref, inner_ref, xi_ref, w_ref, mass_ref, col_ref, bias_ref, xj_ref, gj_ref = refs[steps + 1 :]
    cols = jsrc * own
    size = own + AUX
    scale = 1.0 / (2.0 * width * EPS)
    bias = []
    for k in range(jsrc):
        part = pj_ref[k, 0:own, :]
        xj_ref[k * own : (k + 1) * own, :] = part
        gj_ref[k * own : (k + 1) * own, :] = pj_ref[k, own : 2 * own, :]
        pf = part.astype(F32)
        sq = jnp.sum(pf * pf, axis=1, keepdims=True)
        pot = to_col(pj_ref[k, 2 * own : 2 * own + AUX, :].astype(F32)[0:1, 0:LANES], own)
        bias.append(pot / EPS - sq * scale)
    jbias = lanes_of(jnp.concatenate(bias, axis=0))
    bias_ref[isrc : isrc + 8, :] = jnp.zeros((8, LANES), F32)
    for k in range(cols // LANES):
        bias_ref[isrc + k : isrc + k + 1, :] = jbias[:, k * LANES : (k + 1) * LANES]
    xj = xj_ref[...]
    gj = gj_ref[...]
    span = GROUP * own
    cmass = cph = None
    for m in range(steps):
        src = pi_refs[m]
        t = behind("y", m, steps)
        base = pl.multiple_of(t * span, span)
        first = pl.multiple_of(t * GROUP, GROUP)
        ibias = []
        for k in range(GROUP):
            part = src[k * size : k * size + own, :]
            xi_ref[pl.ds(pl.multiple_of(base + k * own, own), own), :] = part
            aux = src[k * size + own : (k + 1) * size, :].astype(F32)
            w_ref[pl.ds(first + k, 1), :] = aux[1:2, 0:LANES]
            pf = part.astype(F32)
            sq = jnp.sum(pf * pf, axis=1, keepdims=True)
            ibias.append(to_col(aux[0:1, 0:LANES], own) / EPS - sq * scale)
        ibias = jnp.concatenate(ibias, axis=0)
        lines = slots_of(ibias, own, GROUP)
        for k in range(GROUP):
            bias_ref[pl.ds(first + k, 1), :] = lines[k : k + 1]
        part = xi_ref[pl.ds(base, span), :]
        cross = lax.dot_general(part, xj, NT, preferred_element_type=F32)
        plan = jnp.exp(cross * (2.0 * scale) + jbias + ibias)
        plan_ref[pl.ds(base, span), :] = plan
        inner = lax.dot_general(part, gj, NT, preferred_element_type=F32)
        inner_ref[pl.ds(base, span), :] = inner
        weighted = plan * inner
        mass = slots_of(jnp.sum(plan, axis=1, keepdims=True), own, GROUP)
        ph = slots_of(jnp.sum(weighted, axis=1, keepdims=True), own, GROUP)
        for k in range(GROUP):
            mass_ref[0, pl.ds(first + k, 1), :] = mass[k : k + 1]
            mass_ref[0, pl.ds(isrc + first + k, 1), :] = ph[k : k + 1]
        plan, weighted = fold(plan), fold(weighted)
        cmass = plan if cmass is None else cmass + plan
        cph = weighted if cph is None else cph + weighted
    for s in range(1, isrc):
        mass_ref[s] = mass_ref[0]
    col_ref[...] = jnp.zeros_like(col_ref)
    cmass = jnp.sum(cmass, axis=0, keepdims=True)
    cph = jnp.sum(cph, axis=0, keepdims=True)
    for k in range(cols // LANES):
        col_ref[k : k + 1, :] = cmass[:, k * LANES : (k + 1) * LANES]
        col_ref[8 + k : 9 + k, :] = cph[:, k * LANES : (k + 1) * LANES]


def apply_cols(own, isrc, phi, plan_ref):
    span = GROUP * own
    acc = None
    for t in range(isrc // GROUP):
        col = column_of(phi[t * GROUP : (t + 1) * GROUP], own, GROUP)
        part = fold(plan_ref[t * span : (t + 1) * span, :] * col)
        acc = part if acc is None else acc + part
    return jnp.sum(acc, axis=0, keepdims=True)


def valid(own, value):
    lanes = lax.broadcasted_iota(jnp.int32, value.shape, 1)
    return jnp.where(lanes < own, value, 0.0)


def phi_first(own, isrc, jsrc, got_ref, col_ref, plan_ref, mass_ref, send_ref):
    total = jnp.sum(got_ref[...], axis=0)
    mass_ref[...] = total
    phi = valid(own, -total[isrc:] / total[:isrc])
    applied = apply_cols(own, isrc, phi, plan_ref)
    for s in range(jsrc):
        send_ref[s, 0:16, :] = col_ref[...]
        send_ref[s, 16:24, :] = jnp.zeros((8, LANES), F32)
    put_lanes(send_ref, jsrc, 16, applied)


def phi_next(own, isrc, jsrc, got_ref, mass_ref, w_ref, plan_ref, phi_ref, send_ref):
    total = jnp.sum(got_ref[...], axis=0)
    mass = mass_ref[...]
    phi = valid(own, -(mass[isrc:] + total) / mass[:isrc])
    phi_ref[...] = phi
    applied = apply_cols(own, isrc, phi, plan_ref)
    wts = valid(own, w_ref[...])
    wsum = jnp.sum(wts, axis=0, keepdims=True)
    wphi = jnp.sum(wts * phi, axis=0, keepdims=True)
    for s in range(jsrc):
        send_ref[s, 6:7, :] = wsum
        send_ref[s, 7:8, :] = wphi
    put_lanes(send_ref, jsrc, 0, applied)


def row_of(value, count):
    return jnp.concatenate([value[k : k + 1, :] for k in range(count)], axis=1)


def apply_rows(own, isrc, psi, plan_ref, send_ref):
    span = GROUP * own
    for t in range(isrc // GROUP):
        col = jnp.sum(plan_ref[t * span : (t + 1) * span, :] * psi, axis=1, keepdims=True)
        part = slots_of(col, own, GROUP)
        for s in range(isrc):
            send_ref[s, t * GROUP : (t + 1) * GROUP, :] = part


def psi_first(own, isrc, got_ref, plan_ref, col_ref, send_ref):
    total = jnp.sum(got_ref[...], axis=0)
    col_ref[...] = total[:16]
    count = plan_ref.shape[1] // LANES
    psi = row_of(-(total[8:16] + total[16:24]) / total[0:8], count)
    apply_rows(own, isrc, psi, plan_ref, send_ref)


def psi_next(own, isrc, got_ref, col_ref, plan_ref, send_ref, *psi_refs):
    total = jnp.sum(got_ref[...], axis=0)
    count = plan_ref.shape[1] // LANES
    psi = -(col_ref[8:16] + total) / col_ref[0:8]
    for ref in psi_refs:
        ref[...] = psi
    apply_rows(own, isrc, row_of(psi, count), plan_ref, send_ref)


def bit_of(axis, bit):
    return lax.rem(lax.shift_right_logical(lax.axis_index(axis), bit), 2)


def phi_last(own, width, isrc, jsrc, *refs):
    got_ref, mass_ref, w_ref, psi_ref, plan_ref, inner_ref, xi_ref = refs[:7]
    phi_ref, send_hbm, keep_ref, give_ref, send_ref, mixed_ref, acc_ref, sem = refs[7:]
    phi_next(own, isrc, jsrc, got_ref, mass_ref, w_ref, plan_ref, phi_ref, send_ref)
    sent = pltpu.make_async_copy(send_ref, send_hbm, sem)
    sent.start()
    cols = plan_ref.shape[1]
    psi = row_of(psi_ref[...], cols // LANES)
    span = GROUP * own
    for t in range(isrc // GROUP):
        at = slice(t * span, (t + 1) * span)
        col = column_of(phi_ref[t * GROUP : (t + 1) * GROUP, :], own, GROUP)
        plan = plan_ref[at, :]
        mixed_ref[0, at, :] = (plan * (inner_ref[at, :] + (col + psi))).astype(BF16)
        mixed_ref[1, at, :] = plan.astype(BF16)
    part = xi_ref[...]
    for q in range(2):
        term = lax.dot_general(mixed_ref[q], part, TN, preferred_element_type=F32)
        acc_ref[q * cols : (q + 1) * cols, :] = term
    scale = 1.0 / (width * EPS)
    mine = bit_of("z", 0)
    for q in range(2):
        for m in range(jsrc // 2):
            keep = pl.ds(pl.multiple_of(q * cols + (2 * m + mine) * own, own), own)
            give = pl.ds(pl.multiple_of(q * cols + (2 * m + 1 - mine) * own, own), own)
            first = q * (cols // 2) + m * own
            at = slice(first, first + own)
            keep_ref[at, :] = acc_ref[keep, :] * scale
            give_ref[at, :] = (acc_ref[give, :] * scale).astype(BF16)
    sent.wait()


def halve(own, bit, keep_ref, got_ref, next_ref, send_ref):
    mine = bit_of("z", bit)
    size, out = keep_ref.shape[0] // 2, next_ref.shape[0] // 2
    for q in range(2):
        for m in range(out // own):
            keep = pl.ds(pl.multiple_of(q * size + (2 * m + mine) * own, own), own)
            give = pl.ds(pl.multiple_of(q * size + (2 * m + 1 - mine) * own, own), own)
            first = q * out + m * own
            at = slice(first, first + own)
            next_ref[at, :] = keep_ref[keep, :] + got_ref[keep, :].astype(F32)
            send_ref[at, :] = (keep_ref[give, :] + got_ref[give, :].astype(F32)).astype(BF16)


def finish_rows(own, width, isrc, every, *refs):
    got_ref, col_ref, phi_ref, psi_ref, bias_ref, xi_hbm, pj_ref, after_ref = refs[:8]
    row_hbm, gw_ref, delta_ref, row_ref, xi_ref, xj_ref, gj_ref, sem, out_sem = refs[8:]
    jsrc = pj_ref.shape[0]
    span = GROUP * own
    parts = []
    for t in range(isrc // GROUP):
        at = pl.ds(t * span, span)
        parts.append(pltpu.make_async_copy(xi_hbm.at[at], xi_ref.at[at], sem.at[t]))
        parts[t].start()
    for k in range(jsrc):
        xj_ref[k * own : (k + 1) * own, :] = pj_ref[k, 0:own, :]
        gj_ref[k * own : (k + 1) * own, :] = pj_ref[k, own : 2 * own, :]
    total = jnp.sum(got_ref[...], axis=0)
    cols = jsrc * own
    psi = -(col_ref[8:16] + total) / col_ref[0:8]
    delta = row_of(psi - psi_ref[...], cols // LANES)
    psi = row_of(psi, cols // LANES)
    jbias = row_of(bias_ref[isrc:], cols // LANES)
    rows = lax.broadcasted_iota(jnp.int32, (own, cols), 0)
    lanes = lax.broadcasted_iota(jnp.int32, (own, cols), 1)
    first = lax.axis_index("z") * own
    delta_ref[...] = jnp.sum(jnp.where(lanes == rows + first, delta, 0.0), axis=1, keepdims=True)
    wsum = jnp.sum(total[6:7], axis=1, keepdims=True)
    wphi = jnp.sum(total[7:8], axis=1, keepdims=True)
    gw_ref[...] = -(every / wsum) * (phi_ref[...] - wphi / wsum)
    scale = 1.0 / (width * EPS)
    xj = xj_ref[...]
    gj = gj_ref[...]
    outs = []
    for t in range(isrc // GROUP):
        group = slice(t * GROUP, (t + 1) * GROUP)
        col = column_of(phi_ref[group, :], own, GROUP)
        ibias = column_of(bias_ref[group, :], own, GROUP)
        parts[t].wait()
        part = xi_ref[t * span : (t + 1) * span, :]
        cross = lax.dot_general(part, xj, NT, preferred_element_type=F32)
        plan = jnp.exp(cross * scale + jbias + ibias)
        inner = lax.dot_general(part, gj, NT, preferred_element_type=F32)
        mixed = plan * (inner + (col + psi))
        qrow = jnp.sum(mixed, axis=1, keepdims=True)
        base = jnp.dot(plan.astype(BF16), gj, preferred_element_type=F32)
        term = jnp.dot(mixed.astype(BF16), xj, preferred_element_type=F32)
        term = base + (term - qrow * part.astype(F32)) * scale
        term = term.astype(BF16)
        for k in range(GROUP):
            row_ref[t * GROUP + k] = term[k * own : (k + 1) * own]
        group = pl.ds(t * GROUP, GROUP)
        outs.append(pltpu.make_async_copy(row_ref.at[group], row_hbm.at[group], out_sem.at[t]))
        outs[t].start()
    for copy in outs:
        copy.wait()


def total_up(own, rows_ref, keep_ref, got_ref, delta_ref, out_ref):
    acc = jnp.sum(rows_ref[...].astype(F32), axis=0)
    sums = keep_ref[...] + got_ref[...].astype(F32)
    out_ref[...] = (acc + (sums[:own] + delta_ref[...] * sums[own:])).astype(BF16)


def local(particles, cotangent, row_potential, col_potential, weights):
    own, width = particles.shape
    iaxes, jaxes = ("y", "row"), ("z",)
    ysrc, xsrc = lax.axis_size("y"), lax.axis_size("row")
    isrc, jsrc = ysrc * xsrc, lax.axis_size("z")
    rows, cols = isrc * own, jsrc * own

    def swap(value, axes):
        return lax.all_to_all(value, axes, 0, 0, tiled=True)

    def shift(value, axis, k):
        n = lax.axis_size(axis)
        return lax.ppermute(value, axis, [(i, (i + k) % n) for i in range(n)])

    def flip(value, bit):
        return lax.ppermute(value, "z", [(i, i ^ bit) for i in range(jsrc)])

    def call(body, micros, outs, *args, scratch=(), in_specs=None, out_specs=None, mib=12, hbm=()):
        return pl.pallas_call(
            body,
            out_shape=[(pltpu.HBM if n in hbm else jax.ShapeDtypeStruct)(s, d) for n, (s, d) in enumerate(outs)],
            in_specs=in_specs or whole(len(args)),
            out_specs=out_specs or whole(len(outs)),
            scratch_shapes=list(scratch),
            compiler_params=params(mib),
            cost_estimate=pl.CostEstimate(flops=int(micros * 1e9), bytes_accessed=1024, transcendentals=0),
        )(*args)

    anywhere = pl.BlockSpec(memory_space=pltpu.HBM)
    ipack, jpack = call(
        functools.partial(pack, own, width, jsrc),
        2,
        [((own + AUX, width), BF16), ((jsrc, 2 * own + AUX, width), BF16)],
        *[
            pltpu.with_memory_space_constraint(v, pltpu.HBM)
            for v in (
                particles,
                cotangent,
                row_potential.reshape(1, own),
                col_potential.reshape(1, own),
                weights.reshape(1, own),
            )
        ],
        scratch=[
            pltpu.VMEM((2 * own + AUX, width), BF16),
            pltpu.VMEM((2, AUX, width), F32),
            pltpu.VMEM((3, 1, own), BF16),
            pltpu.SemaphoreType.DMA((5,)),
            pltpu.SemaphoreType.DMA((jsrc,)),
        ],
        in_specs=[anywhere] * 5,
        out_specs=whole(1) + [anywhere],
        hbm=(1,),
    )
    jgot = swap(jpack, jaxes)
    near = [shift(ipack, "row", k) for k in range(1, xsrc)]
    (line,) = call(
        functools.partial(stack, own, xsrc), 1, [((xsrc * (own + AUX), width), BF16)], ipack, *near
    )
    igot = [line] + [shift(line, "y", k) for k in range(1, ysrc)]
    plan, inner, xi, wts, send, col_part, bias = call(
        functools.partial(build, own, width, isrc, jsrc),
        5,
        [
            ((rows, cols), F32),
            ((rows, cols), F32),
            ((rows, width), BF16),
            ((isrc, LANES), F32),
            ((isrc, 2 * isrc, LANES), F32),
            ((16, LANES), F32),
            ((isrc + 8, LANES), F32),
        ],
        *igot,
        jgot,
        scratch=[pltpu.VMEM((cols, width), BF16), pltpu.VMEM((cols, width), BF16)],
    )
    got = swap(send, iaxes)
    mass, send = call(
        functools.partial(phi_first, own, isrc, jsrc),
        1,
        [((2 * isrc, LANES), F32), ((jsrc, 24, LANES), F32)],
        got,
        col_part,
        plan,
    )
    got = swap(send, jaxes)
    col, send = call(
        functools.partial(psi_first, own, isrc),
        1,
        [((16, LANES), F32), ((isrc, isrc, LANES), F32)],
        got,
        plan,
    )
    for step in range(1, ITERS):
        got = swap(send, iaxes)
        if step < ITERS - 1:
            phi, send = call(
                functools.partial(phi_next, own, isrc, jsrc),
                1,
                [((isrc, LANES), F32), ((jsrc, 8, LANES), F32)],
                got,
                mass,
                wts,
                plan,
            )
            got = swap(send, jaxes)
            send, *kept = call(
                functools.partial(psi_next, own, isrc),
                1,
                [((isrc, isrc, LANES), F32)] + [((8, LANES), F32)] * (step == ITERS - 2),
                got,
                col,
                plan,
            )
    half = cols
    phi, send, keep, give = call(
        functools.partial(phi_last, own, width, isrc, jsrc),
        4,
        [((isrc, LANES), F32), ((jsrc, 8, LANES), F32), ((half, width), F32), ((half, width), BF16)],
        got,
        mass,
        wts,
        *kept,
        plan,
        inner,
        xi,
        scratch=[
            pltpu.VMEM((jsrc, 8, LANES), F32),
            pltpu.VMEM((2, rows, cols), BF16),
            pltpu.VMEM((2 * cols, width), F32),
            pltpu.SemaphoreType.DMA,
        ],
        out_specs=whole(1) + [anywhere] + whole(2),
        hbm=(1,),
        mib=20,
    )
    send, give = lax.optimization_barrier((send, give))
    taken = flip(give, 1)
    got = swap(send, jaxes)
    half //= 2
    keep, give = call(
        functools.partial(halve, own, 1), 1, [((half, width), F32), ((half, width), BF16)], keep, taken
    )
    taken = flip(give, 2)
    row_send, gw, delta = call(
        functools.partial(finish_rows, own, width, isrc, float(isrc * jsrc * own)),
        4,
        [((isrc, own, width), BF16), ((isrc, LANES), F32), ((own, 1), F32)],
        got,
        col,
        phi,
        *kept,
        bias,
        pltpu.with_memory_space_constraint(xi, pltpu.HBM),
        jgot,
        keep,
        scratch=[
            pltpu.VMEM((isrc, own, width), BF16),
            pltpu.VMEM((rows, width), BF16),
            pltpu.VMEM((cols, width), BF16),
            pltpu.VMEM((cols, width), BF16),
            pltpu.SemaphoreType.DMA((isrc // GROUP,)),
            pltpu.SemaphoreType.DMA((isrc // GROUP,)),
        ],
        in_specs=whole(5) + [anywhere] + whole(2),
        out_specs=[anywhere] + whole(2),
        hbm=(0,),
        mib=24,
    )
    row_send, taken = lax.optimization_barrier((row_send, taken))
    half //= 2
    keep, give = call(
        functools.partial(halve, own, 2), 1, [((half, width), F32), ((half, width), BF16)], keep, taken
    )
    taken = flip(give, 4)
    row_got = swap(row_send, iaxes)
    (grad,) = call(
        functools.partial(total_up, own), 1, [((own, width), BF16)], row_got, keep, taken, delta
    )
    mine = lax.axis_index("y") * xsrc + lax.axis_index("row")
    grad_weights = lax.dynamic_slice(gw, (mine, 0), (1, own)).reshape(own)
    return (grad, grad_weights)


def solution(mesh):
    filt, row, col = mesh.devices.shape
    split = Mesh(mesh.devices.reshape(filt, row, 8, col // 8), ("filt", "row", "z", "y"))
    spec = ("filt", "row", "z", "y")
    return jax.shard_map(
        local,
        mesh=split,
        in_specs=(P(spec, None), P(spec, None), P(spec), P(spec), P(spec)),
        out_specs=(P(spec, None), P(spec)),
        check_vma=False,
    )
```

```python
import functools

import jax
import jax.numpy as jnp
from jax import lax
from jax.experimental import pallas as pl
from jax.experimental.pallas import tpu as pltpu
from jax.sharding import Mesh
from jax.sharding import PartitionSpec as P

ITERS = 4


EPS = 0.09

LANES = 128
AUX = 8
F32 = jnp.float32
BF16 = jnp.bfloat16


def params(mib):
    return pltpu.CompilerParams(vmem_limit_bytes=mib << 20)


def whole(n):
    return [pl.BlockSpec(memory_space=pltpu.VMEM)] * n


def eye(own):
    rows = lax.broadcasted_iota(jnp.int32, (own, LANES), 0)
    lanes = lax.broadcasted_iota(jnp.int32, (own, LANES), 1)
    return rows == lanes


def to_row(col, own):
    return jnp.sum(jnp.where(eye(own), col, 0.0), axis=0, keepdims=True)


def to_col(row, own):
    return jnp.sum(jnp.where(eye(own), row, 0.0), axis=1, keepdims=True)


def lanes_of(col):
    out = []
    for k in range(col.shape[0] // LANES):
        out.append(to_row(col[k * LANES : (k + 1) * LANES], LANES))
    return jnp.concatenate(out, axis=1)


def slots_of(value, own, count):
    return jnp.concatenate([to_row(value[k * own : (k + 1) * own], own) for k in range(count)], axis=0)


def column_of(value, own, count):
    return jnp.concatenate([to_col(value[k : k + 1], own) for k in range(count)], axis=0)


def fold(block):
    return jnp.sum(block.reshape(block.shape[0] // 8, 8, block.shape[1]), axis=0)


def put_lanes(ref, slots, base, row):
    for k in range(row.shape[1] // LANES):
        piece = row[:, k * LANES : (k + 1) * LANES]
        for s in range(slots):
            ref[s, base + k : base + k + 1, :] = piece


def pack(own, width, jsrc, x_ref, gy_ref, f_ref, g_ref, w_ref, ipack_ref, jpack_ref, block_ref, line_ref, vec_ref, in_sem, out_sem):
    copies = [
        pltpu.make_async_copy(f_ref, vec_ref.at[0], in_sem.at[2]),
        pltpu.make_async_copy(w_ref, vec_ref.at[1], in_sem.at[3]),
        pltpu.make_async_copy(g_ref, vec_ref.at[2], in_sem.at[4]),
        pltpu.make_async_copy(x_ref, block_ref.at[pl.ds(0, own)], in_sem.at[0]),
        pltpu.make_async_copy(gy_ref, block_ref.at[pl.ds(own, own)], in_sem.at[1]),
    ]
    for copy in copies:
        copy.start()
    line_ref[...] = jnp.zeros_like(line_ref)
    for copy in copies:
        copy.wait()
    line_ref[0, 0:1, 0:own] = vec_ref[0].astype(F32)
    line_ref[0, 1:2, 0:own] = vec_ref[1].astype(F32)
    line_ref[1, 0:1, 0:own] = vec_ref[2].astype(F32)
    block_ref[2 * own : 2 * own + AUX, :] = line_ref[1].astype(BF16)
    outs = [pltpu.make_async_copy(block_ref, jpack_ref.at[s], out_sem.at[s]) for s in range(jsrc)]
    for copy in outs:
        copy.start()
    ipack_ref[0:own, :] = block_ref[0:own, :]
    ipack_ref[own : own + AUX, :] = line_ref[0].astype(BF16)
    for copy in outs:
        copy.wait()


def stack(own, count, *refs):
    out_ref = refs[count]
    size = own + AUX
    for k in range(count):
        place = behind("row", k, count)
        out_ref[pl.ds(pl.multiple_of(place * size, size), size), :] = refs[k][...]


GROUP = 4
NT = (((1,), (1,)), ((), ()))
TN = (((0,), (0,)), ((), ()))


def behind(axis, k, count):
    return lax.rem(lax.axis_index(axis) + (count - k), count)


def build(own, width, isrc, jsrc, *refs):
    steps = isrc // GROUP
    pi_refs, pj_ref = refs[:steps], refs[steps]
    plan_ref, inner_ref, xi_ref, w_ref, mass_ref, col_ref, bias_ref, xj_ref, gj_ref = refs[steps + 1 :]
    cols = jsrc * own
    size = own + AUX
    scale = 1.0 / (2.0 * width * EPS)
    bias = []
    for k in range(jsrc):
        part = pj_ref[k, 0:own, :]
        xj_ref[k * own : (k + 1) * own, :] = part
        gj_ref[k * own : (k + 1) * own, :] = pj_ref[k, own : 2 * own, :]
        pf = part.astype(F32)
        sq = jnp.sum(pf * pf, axis=1, keepdims=True)
        pot = to_col(pj_ref[k, 2 * own : 2 * own + AUX, :].astype(F32)[0:1, 0:LANES], own)
        bias.append(pot / EPS - sq * scale)
    jbias = lanes_of(jnp.concatenate(bias, axis=0))
    bias_ref[isrc : isrc + 8, :] = jnp.zeros((8, LANES), F32)
    for k in range(cols // LANES):
        bias_ref[isrc + k : isrc + k + 1, :] = jbias[:, k * LANES : (k + 1) * LANES]
    xj = xj_ref[...]
    gj = gj_ref[...]
    span = GROUP * own
    cmass = cph = None
    for m in range(steps):
        src = pi_refs[m]
        t = behind("y", m, steps)
        base = pl.multiple_of(t * span, span)
        first = pl.multiple_of(t * GROUP, GROUP)
        ibias = []
        for k in range(GROUP):
            part = src[k * size : k * size + own, :]
            xi_ref[pl.ds(pl.multiple_of(base + k * own, own), own), :] = part
            aux = src[k * size + own : (k + 1) * size, :].astype(F32)
            w_ref[pl.ds(first + k, 1), :] = aux[1:2, 0:LANES]
            pf = part.astype(F32)
            sq = jnp.sum(pf * pf, axis=1, keepdims=True)
            ibias.append(to_col(aux[0:1, 0:LANES], own) / EPS - sq * scale)
        ibias = jnp.concatenate(ibias, axis=0)
        lines = slots_of(ibias, own, GROUP)
        for k in range(GROUP):
            bias_ref[pl.ds(first + k, 1), :] = lines[k : k + 1]
        part = xi_ref[pl.ds(base, span), :]
        cross = lax.dot_general(part, xj, NT, preferred_element_type=F32)
        plan = jnp.exp(cross * (2.0 * scale) + jbias + ibias)
        plan_ref[pl.ds(base, span), :] = plan
        inner = lax.dot_general(part, gj, NT, preferred_element_type=F32)
        inner_ref[pl.ds(base, span), :] = inner
        weighted = plan * inner
        mass = slots_of(jnp.sum(plan, axis=1, keepdims=True), own, GROUP)
        ph = slots_of(jnp.sum(weighted, axis=1, keepdims=True), own, GROUP)
        for k in range(GROUP):
            mass_ref[0, pl.ds(first + k, 1), :] = mass[k : k + 1]
            mass_ref[0, pl.ds(isrc + first + k, 1), :] = ph[k : k + 1]
        plan, weighted = fold(plan), fold(weighted)
        cmass = plan if cmass is None else cmass + plan
        cph = weighted if cph is None else cph + weighted
    for s in range(1, isrc):
        mass_ref[s] = mass_ref[0]
    col_ref[...] = jnp.zeros_like(col_ref)
    cmass = jnp.sum(cmass, axis=0, keepdims=True)
    cph = jnp.sum(cph, axis=0, keepdims=True)
    for k in range(cols // LANES):
        col_ref[k : k + 1, :] = cmass[:, k * LANES : (k + 1) * LANES]
        col_ref[8 + k : 9 + k, :] = cph[:, k * LANES : (k + 1) * LANES]


def apply_cols(own, isrc, phi, plan_ref):
    span = GROUP * own
    acc = None
    for t in range(isrc // GROUP):
        col = column_of(phi[t * GROUP : (t + 1) * GROUP], own, GROUP)
        part = fold(plan_ref[t * span : (t + 1) * span, :] * col)
        acc = part if acc is None else acc + part
    return jnp.sum(acc, axis=0, keepdims=True)


def valid(own, value):
    lanes = lax.broadcasted_iota(jnp.int32, value.shape, 1)
    return jnp.where(lanes < own, value, 0.0)


def phi_first(own, isrc, jsrc, got_ref, col_ref, plan_ref, mass_ref, send_ref):
    total = jnp.sum(got_ref[...], axis=0)
    mass_ref[...] = total
    phi = valid(own, -total[isrc:] / total[:isrc])
    applied = apply_cols(own, isrc, phi, plan_ref)
    for s in range(jsrc):
        send_ref[s, 0:16, :] = col_ref[...]
        send_ref[s, 16:24, :] = jnp.zeros((8, LANES), F32)
    put_lanes(send_ref, jsrc, 16, applied)


def phi_next(own, isrc, jsrc, got_ref, mass_ref, w_ref, plan_ref, phi_ref, send_ref):
    total = jnp.sum(got_ref[...], axis=0)
    mass = mass_ref[...]
    phi = valid(own, -(mass[isrc:] + total) / mass[:isrc])
    phi_ref[...] = phi
    applied = apply_cols(own, isrc, phi, plan_ref)
    wts = valid(own, w_ref[...])
    wsum = jnp.sum(wts, axis=0, keepdims=True)
    wphi = jnp.sum(wts * phi, axis=0, keepdims=True)
    for s in range(jsrc):
        send_ref[s, 6:7, :] = wsum
        send_ref[s, 7:8, :] = wphi
    put_lanes(send_ref, jsrc, 0, applied)


def row_of(value, count):
    return jnp.concatenate([value[k : k + 1, :] for k in range(count)], axis=1)


def apply_rows(own, isrc, psi, plan_ref, send_ref):
    span = GROUP * own
    for t in range(isrc // GROUP):
        col = jnp.sum(plan_ref[t * span : (t + 1) * span, :] * psi, axis=1, keepdims=True)
        part = slots_of(col, own, GROUP)
        for s in range(isrc):
            send_ref[s, t * GROUP : (t + 1) * GROUP, :] = part


def psi_first(own, isrc, got_ref, plan_ref, col_ref, send_ref):
    total = jnp.sum(got_ref[...], axis=0)
    col_ref[...] = total[:16]
    count = plan_ref.shape[1] // LANES
    psi = row_of(-(total[8:16] + total[16:24]) / total[0:8], count)
    apply_rows(own, isrc, psi, plan_ref, send_ref)


def psi_next(own, isrc, got_ref, col_ref, plan_ref, send_ref, *psi_refs):
    total = jnp.sum(got_ref[...], axis=0)
    count = plan_ref.shape[1] // LANES
    psi = -(col_ref[8:16] + total) / col_ref[0:8]
    for ref in psi_refs:
        ref[...] = psi
    apply_rows(own, isrc, row_of(psi, count), plan_ref, send_ref)


def bit_of(axis, bit):
    return lax.rem(lax.shift_right_logical(lax.axis_index(axis), bit), 2)


def phi_last(own, width, isrc, jsrc, *refs):
    got_ref, mass_ref, w_ref, psi_ref, plan_ref, inner_ref, xi_ref = refs[:7]
    phi_ref, send_hbm, keep_ref, give_ref, send_ref, mixed_ref, acc_ref, sem = refs[7:]
    phi_next(own, isrc, jsrc, got_ref, mass_ref, w_ref, plan_ref, phi_ref, send_ref)
    sent = pltpu.make_async_copy(send_ref, send_hbm, sem)
    sent.start()
    cols = plan_ref.shape[1]
    psi = row_of(psi_ref[...], cols // LANES)
    span = GROUP * own
    for t in range(isrc // GROUP):
        at = slice(t * span, (t + 1) * span)
        col = column_of(phi_ref[t * GROUP : (t + 1) * GROUP, :], own, GROUP)
        plan = plan_ref[at, :]
        mixed_ref[0, at, :] = (plan * (inner_ref[at, :] + (col + psi))).astype(BF16)
        mixed_ref[1, at, :] = plan.astype(BF16)
    part = xi_ref[...]
    for q in range(2):
        term = lax.dot_general(mixed_ref[q], part, TN, preferred_element_type=F32)
        acc_ref[q * cols : (q + 1) * cols, :] = term
    scale = 1.0 / (width * EPS)
    mine = bit_of("z", 0)
    for q in range(2):
        for m in range(jsrc // 2):
            keep = pl.ds(pl.multiple_of(q * cols + (2 * m + mine) * own, own), own)
            give = pl.ds(pl.multiple_of(q * cols + (2 * m + 1 - mine) * own, own), own)
            first = q * (cols // 2) + m * own
            at = slice(first, first + own)
            keep_ref[at, :] = (acc_ref[keep, :] * scale).astype(BF16)
            give_ref[at, :] = (acc_ref[give, :] * scale).astype(BF16)
    sent.wait()


def halve(own, bit, keep_ref, got_ref, next_ref, send_ref):
    mine = bit_of("z", bit)
    size, out = keep_ref.shape[0] // 2, next_ref.shape[0] // 2
    for q in range(2):
        for m in range(out // own):
            keep = pl.ds(pl.multiple_of(q * size + (2 * m + mine) * own, own), own)
            give = pl.ds(pl.multiple_of(q * size + (2 * m + 1 - mine) * own, own), own)
            first = q * out + m * own
            at = slice(first, first + own)
            next_ref[at, :] = keep_ref[keep, :].astype(F32) + got_ref[keep, :].astype(F32)
            send_ref[at, :] = (keep_ref[give, :].astype(F32) + got_ref[give, :].astype(F32)).astype(BF16)


def finish_rows(own, width, isrc, every, *refs):
    got_ref, col_ref, phi_ref, psi_ref, bias_ref, xi_ref, pj_ref, after_ref = refs[:8]
    row_ref, gw_ref, delta_ref, xj_ref, gj_ref = refs[8:]
    jsrc = pj_ref.shape[0]
    span = GROUP * own
    for k in range(jsrc):
        xj_ref[k * own : (k + 1) * own, :] = pj_ref[k, 0:own, :]
        gj_ref[k * own : (k + 1) * own, :] = pj_ref[k, own : 2 * own, :]
    total = jnp.sum(got_ref[...], axis=0)
    cols = jsrc * own
    psi = -(col_ref[8:16] + total) / col_ref[0:8]
    delta = row_of(psi - psi_ref[...], cols // LANES)
    psi = row_of(psi, cols // LANES)
    jbias = row_of(bias_ref[isrc:], cols // LANES)
    rows = lax.broadcasted_iota(jnp.int32, (own, cols), 0)
    lanes = lax.broadcasted_iota(jnp.int32, (own, cols), 1)
    first = lax.axis_index("z") * own
    delta_ref[...] = jnp.sum(jnp.where(lanes == rows + first, delta, 0.0), axis=1, keepdims=True)
    wsum = jnp.sum(total[6:7], axis=1, keepdims=True)
    wphi = jnp.sum(total[7:8], axis=1, keepdims=True)
    gw_ref[...] = -(every / wsum) * (phi_ref[...] - wphi / wsum)
    scale = 1.0 / (width * EPS)
    xj = xj_ref[...]
    gj = gj_ref[...]
    for t in range(isrc // GROUP):
        group = slice(t * GROUP, (t + 1) * GROUP)
        col = column_of(phi_ref[group, :], own, GROUP)
        ibias = column_of(bias_ref[group, :], own, GROUP)
        part = xi_ref[t * span : (t + 1) * span, :]
        cross = lax.dot_general(part, xj, NT, preferred_element_type=F32)
        plan = jnp.exp(cross * scale + jbias + ibias)
        inner = lax.dot_general(part, gj, NT, preferred_element_type=F32)
        mixed = plan * (inner + (col + psi))
        qrow = jnp.sum(mixed, axis=1, keepdims=True)
        base = jnp.dot(plan.astype(BF16), gj, preferred_element_type=F32)
        term = jnp.dot(mixed.astype(BF16), xj, preferred_element_type=F32)
        term = base + (term - qrow * part.astype(F32)) * scale
        term = term.astype(BF16)
        for k in range(GROUP):
            row_ref[t * GROUP + k] = term[k * own : (k + 1) * own]


def total_up(own, rows_ref, keep_ref, got_ref, delta_ref, out_ref):
    acc = jnp.sum(rows_ref[...].astype(F32), axis=0)
    sums = keep_ref[...] + got_ref[...].astype(F32)
    out_ref[...] = (acc + (sums[:own] + delta_ref[...] * sums[own:])).astype(BF16)


def local(particles, cotangent, row_potential, col_potential, weights):
    own, width = particles.shape
    iaxes, jaxes = ("y", "row"), ("z",)
    ysrc, xsrc = lax.axis_size("y"), lax.axis_size("row")
    isrc, jsrc = ysrc * xsrc, lax.axis_size("z")
    rows, cols = isrc * own, jsrc * own

    def swap(value, axes):
        return lax.all_to_all(value, axes, 0, 0, tiled=True)

    def shift(value, axis, k):
        n = lax.axis_size(axis)
        return lax.ppermute(value, axis, [(i, (i + k) % n) for i in range(n)])

    def flip(value, bit):
        return lax.ppermute(value, "z", [(i, i ^ bit) for i in range(jsrc)])

    def call(body, micros, outs, *args, scratch=(), in_specs=None, out_specs=None, mib=12, hbm=()):
        return pl.pallas_call(
            body,
            out_shape=[(pltpu.HBM if n in hbm else jax.ShapeDtypeStruct)(s, d) for n, (s, d) in enumerate(outs)],
            in_specs=in_specs or whole(len(args)),
            out_specs=out_specs or whole(len(outs)),
            scratch_shapes=list(scratch),
            compiler_params=params(mib),
            cost_estimate=pl.CostEstimate(flops=int(micros * 1e9), bytes_accessed=1024, transcendentals=0),
        )(*args)

    anywhere = pl.BlockSpec(memory_space=pltpu.HBM)
    ipack, jpack = call(
        functools.partial(pack, own, width, jsrc),
        2,
        [((own + AUX, width), BF16), ((jsrc, 2 * own + AUX, width), BF16)],
        *[
            pltpu.with_memory_space_constraint(v, pltpu.HBM)
            for v in (
                particles,
                cotangent,
                row_potential.reshape(1, own),
                col_potential.reshape(1, own),
                weights.reshape(1, own),
            )
        ],
        scratch=[
            pltpu.VMEM((2 * own + AUX, width), BF16),
            pltpu.VMEM((2, AUX, width), F32),
            pltpu.VMEM((3, 1, own), BF16),
            pltpu.SemaphoreType.DMA((5,)),
            pltpu.SemaphoreType.DMA((jsrc,)),
        ],
        in_specs=[anywhere] * 5,
        out_specs=whole(1) + [anywhere],
        hbm=(1,),
    )
    jgot = swap(jpack, jaxes)
    near = [shift(ipack, "row", k) for k in range(1, xsrc)]
    (line,) = call(
        functools.partial(stack, own, xsrc), 1, [((xsrc * (own + AUX), width), BF16)], ipack, *near
    )
    igot = [line] + [shift(line, "y", k) for k in range(1, ysrc)]
    plan, inner, xi, wts, send, col_part, bias = call(
        functools.partial(build, own, width, isrc, jsrc),
        5,
        [
            ((rows, cols), F32),
            ((rows, cols), F32),
            ((rows, width), BF16),
            ((isrc, LANES), F32),
            ((isrc, 2 * isrc, LANES), F32),
            ((16, LANES), F32),
            ((isrc + 8, LANES), F32),
        ],
        *igot,
        jgot,
        scratch=[pltpu.VMEM((cols, width), BF16), pltpu.VMEM((cols, width), BF16)],
    )
    got = swap(send, iaxes)
    mass, send = call(
        functools.partial(phi_first, own, isrc, jsrc),
        1,
        [((2 * isrc, LANES), F32), ((jsrc, 24, LANES), F32)],
        got,
        col_part,
        plan,
    )
    got = swap(send, jaxes)
    col, send = call(
        functools.partial(psi_first, own, isrc),
        1,
        [((16, LANES), F32), ((isrc, isrc, LANES), F32)],
        got,
        plan,
    )
    for step in range(1, ITERS):
        got = swap(send, iaxes)
        if step < ITERS - 1:
            phi, send = call(
                functools.partial(phi_next, own, isrc, jsrc),
                1,
                [((isrc, LANES), F32), ((jsrc, 8, LANES), F32)],
                got,
                mass,
                wts,
                plan,
            )
            got = swap(send, jaxes)
            send, *kept = call(
                functools.partial(psi_next, own, isrc),
                1,
                [((isrc, isrc, LANES), F32)] + [((8, LANES), F32)] * (step == ITERS - 2),
                got,
                col,
                plan,
            )
    half = cols
    phi, send, keep, give = call(
        functools.partial(phi_last, own, width, isrc, jsrc),
        4,
        [((isrc, LANES), F32), ((jsrc, 8, LANES), F32), ((half, width), BF16), ((half, width), BF16)],
        got,
        mass,
        wts,
        *kept,
        plan,
        inner,
        xi,
        scratch=[
            pltpu.VMEM((jsrc, 8, LANES), F32),
            pltpu.VMEM((2, rows, cols), BF16),
            pltpu.VMEM((2 * cols, width), F32),
            pltpu.SemaphoreType.DMA,
        ],
        out_specs=whole(1) + [anywhere] + whole(2),
        hbm=(1,),
        mib=20,
    )
    send, give = lax.optimization_barrier((send, give))
    taken = flip(give, 1)
    got = swap(send, jaxes)
    half //= 2
    keep, give = call(
        functools.partial(halve, own, 1), 1, [((half, width), F32), ((half, width), BF16)], keep, taken
    )
    taken = flip(give, 2)
    row_send, gw, delta = call(
        functools.partial(finish_rows, own, width, isrc, float(isrc * jsrc * own)),
        4,
        [((isrc, own, width), BF16), ((isrc, LANES), F32), ((own, 1), F32)],
        got,
        col,
        phi,
        *kept,
        bias,
        xi,
        jgot,
        keep,
        scratch=[
            pltpu.VMEM((cols, width), BF16),
            pltpu.VMEM((cols, width), BF16),
        ],
        mib=24,
    )
    row_send, taken = lax.optimization_barrier((row_send, taken))
    half //= 2
    keep, give = call(
        functools.partial(halve, own, 2), 1, [((half, width), F32), ((half, width), BF16)], keep, taken
    )
    taken = flip(give, 4)
    row_got = swap(row_send, iaxes)
    (grad,) = call(
        functools.partial(total_up, own), 1, [((own, width), BF16)], row_got, keep, taken, delta
    )
    mine = lax.axis_index("y") * xsrc + lax.axis_index("row")
    grad_weights = lax.dynamic_slice(gw, (mine, 0), (1, own)).reshape(own)
    return (grad, grad_weights)


def solution(mesh):
    filt, row, col = mesh.devices.shape
    split = Mesh(mesh.devices.reshape(filt, row, 8, col // 8), ("filt", "row", "z", "y"))
    spec = ("filt", "row", "z", "y")
    return jax.shard_map(
        local,
        mesh=split,
        in_specs=(P(spec, None), P(spec, None), P(spec), P(spec), P(spec)),
        out_specs=(P(spec, None), P(spec)),
        check_vma=False,
    )
```

```python
import functools

import jax
import jax.numpy as jnp
from jax import lax
from jax.experimental import pallas as pl
from jax.experimental.pallas import tpu as pltpu
from jax.sharding import Mesh
from jax.sharding import PartitionSpec as P

ITERS = 4


EPS = 0.09

LANES = 128
AUX = 8
F32 = jnp.float32
BF16 = jnp.bfloat16


def params(mib):
    return pltpu.CompilerParams(vmem_limit_bytes=mib << 20)


def whole(n):
    return [pl.BlockSpec(memory_space=pltpu.VMEM)] * n


def eye(own):
    rows = lax.broadcasted_iota(jnp.int32, (own, LANES), 0)
    lanes = lax.broadcasted_iota(jnp.int32, (own, LANES), 1)
    return rows == lanes


def to_row(col, own):
    return jnp.sum(jnp.where(eye(own), col, 0.0), axis=0, keepdims=True)


def to_col(row, own):
    return jnp.sum(jnp.where(eye(own), row, 0.0), axis=1, keepdims=True)


def lanes_of(col):
    out = []
    for k in range(col.shape[0] // LANES):
        out.append(to_row(col[k * LANES : (k + 1) * LANES], LANES))
    return jnp.concatenate(out, axis=1)


def slots_of(value, own, count):
    return jnp.concatenate([to_row(value[k * own : (k + 1) * own], own) for k in range(count)], axis=0)


def column_of(value, own, count):
    return jnp.concatenate([to_col(value[k : k + 1], own) for k in range(count)], axis=0)


def fold(block):
    return jnp.sum(block.reshape(block.shape[0] // 8, 8, block.shape[1]), axis=0)


def put_lanes(ref, slots, base, row):
    for k in range(row.shape[1] // LANES):
        piece = row[:, k * LANES : (k + 1) * LANES]
        for s in range(slots):
            ref[s, base + k : base + k + 1, :] = piece


def pack(own, width, jsrc, x_ref, gy_ref, f_ref, g_ref, w_ref, ipack_ref, jpack_ref, block_ref, line_ref, vec_ref, in_sem, out_sem):
    copies = [
        pltpu.make_async_copy(f_ref, vec_ref.at[0], in_sem.at[2]),
        pltpu.make_async_copy(w_ref, vec_ref.at[1], in_sem.at[3]),
        pltpu.make_async_copy(g_ref, vec_ref.at[2], in_sem.at[4]),
        pltpu.make_async_copy(x_ref, block_ref.at[pl.ds(0, own)], in_sem.at[0]),
        pltpu.make_async_copy(gy_ref, block_ref.at[pl.ds(own, own)], in_sem.at[1]),
    ]
    for copy in copies:
        copy.start()
    line_ref[...] = jnp.zeros_like(line_ref)
    for copy in copies:
        copy.wait()
    line_ref[0, 0:1, 0:own] = vec_ref[0].astype(F32)
    line_ref[0, 1:2, 0:own] = vec_ref[1].astype(F32)
    line_ref[1, 0:1, 0:own] = vec_ref[2].astype(F32)
    block_ref[2 * own : 2 * own + AUX, :] = line_ref[1].astype(BF16)
    outs = [pltpu.make_async_copy(block_ref, jpack_ref.at[s], out_sem.at[s]) for s in range(jsrc)]
    for copy in outs:
        copy.start()
    ipack_ref[0:own, :] = block_ref[0:own, :]
    ipack_ref[own : own + AUX, :] = line_ref[0].astype(BF16)
    for copy in outs:
        copy.wait()


def stack(own, count, *refs):
    out_ref = refs[count]
    size = own + AUX
    for k in range(count):
        place = behind("row", k, count)
        out_ref[pl.ds(pl.multiple_of(place * size, size), size), :] = refs[k][...]


GROUP = 4
NT = (((1,), (1,)), ((), ()))
TN = (((0,), (0,)), ((), ()))


def behind(axis, k, count):
    return lax.rem(lax.axis_index(axis) + (count - k), count)


def build(own, width, isrc, jsrc, *refs):
    steps = isrc // GROUP
    pi_refs, pj_ref = refs[:steps], refs[steps]
    plan_ref, inner_ref, xi_ref, w_ref, mass_ref, col_ref, bias_ref, xj_ref, gj_ref = refs[steps + 1 :]
    cols = jsrc * own
    size = own + AUX
    scale = 1.0 / (2.0 * width * EPS)
    bias = []
    for k in range(jsrc):
        part = pj_ref[k, 0:own, :]
        xj_ref[k * own : (k + 1) * own, :] = part
        gj_ref[k * own : (k + 1) * own, :] = pj_ref[k, own : 2 * own, :]
        pf = part.astype(F32)
        sq = jnp.sum(pf * pf, axis=1, keepdims=True)
        pot = to_col(pj_ref[k, 2 * own : 2 * own + AUX, :].astype(F32)[0:1, 0:LANES], own)
        bias.append(pot / EPS - sq * scale)
    jbias = lanes_of(jnp.concatenate(bias, axis=0))
    bias_ref[isrc : isrc + 8, :] = jnp.zeros((8, LANES), F32)
    for k in range(cols // LANES):
        bias_ref[isrc + k : isrc + k + 1, :] = jbias[:, k * LANES : (k + 1) * LANES]
    xj = xj_ref[...]
    gj = gj_ref[...]
    span = GROUP * own
    cmass = cph = None
    for m in range(steps):
        src = pi_refs[m]
        t = behind("y", m, steps)
        base = pl.multiple_of(t * span, span)
        first = pl.multiple_of(t * GROUP, GROUP)
        ibias = []
        for k in range(GROUP):
            part = src[k * size : k * size + own, :]
            xi_ref[pl.ds(pl.multiple_of(base + k * own, own), own), :] = part
            aux = src[k * size + own : (k + 1) * size, :].astype(F32)
            w_ref[pl.ds(first + k, 1), :] = aux[1:2, 0:LANES]
            pf = part.astype(F32)
            sq = jnp.sum(pf * pf, axis=1, keepdims=True)
            ibias.append(to_col(aux[0:1, 0:LANES], own) / EPS - sq * scale)
        ibias = jnp.concatenate(ibias, axis=0)
        lines = slots_of(ibias, own, GROUP)
        for k in range(GROUP):
            bias_ref[pl.ds(first + k, 1), :] = lines[k : k + 1]
        part = xi_ref[pl.ds(base, span), :]
        cross = lax.dot_general(part, xj, NT, preferred_element_type=F32)
        plan = jnp.exp(cross * (2.0 * scale) + jbias + ibias)
        plan_ref[pl.ds(base, span), :] = plan
        inner = lax.dot_general(part, gj, NT, preferred_element_type=F32)
        inner_ref[pl.ds(base, span), :] = inner
        weighted = plan * inner
        mass = slots_of(jnp.sum(plan, axis=1, keepdims=True), own, GROUP)
        ph = slots_of(jnp.sum(weighted, axis=1, keepdims=True), own, GROUP)
        for k in range(GROUP):
            mass_ref[0, pl.ds(first + k, 1), :] = mass[k : k + 1]
            mass_ref[0, pl.ds(isrc + first + k, 1), :] = ph[k : k + 1]
        plan, weighted = fold(plan), fold(weighted)
        cmass = plan if cmass is None else cmass + plan
        cph = weighted if cph is None else cph + weighted
    for s in range(1, isrc):
        mass_ref[s] = mass_ref[0]
    col_ref[...] = jnp.zeros_like(col_ref)
    cmass = jnp.sum(cmass, axis=0, keepdims=True)
    cph = jnp.sum(cph, axis=0, keepdims=True)
    for k in range(cols // LANES):
        col_ref[k : k + 1, :] = cmass[:, k * LANES : (k + 1) * LANES]
        col_ref[8 + k : 9 + k, :] = cph[:, k * LANES : (k + 1) * LANES]


def apply_cols(own, isrc, phi, plan_ref):
    span = GROUP * own
    acc = None
    for t in range(isrc // GROUP):
        col = column_of(phi[t * GROUP : (t + 1) * GROUP], own, GROUP)
        part = fold(plan_ref[t * span : (t + 1) * span, :] * col)
        acc = part if acc is None else acc + part
    return jnp.sum(acc, axis=0, keepdims=True)


def valid(own, value):
    lanes = lax.broadcasted_iota(jnp.int32, value.shape, 1)
    return jnp.where(lanes < own, value, 0.0)


def phi_first(own, isrc, jsrc, got_ref, col_ref, plan_ref, mass_ref, send_ref):
    total = jnp.sum(got_ref[...], axis=0)
    mass_ref[...] = total
    phi = valid(own, -total[isrc:] / total[:isrc])
    applied = apply_cols(own, isrc, phi, plan_ref)
    for s in range(jsrc):
        send_ref[s, 0:16, :] = col_ref[...]
        send_ref[s, 16:24, :] = jnp.zeros((8, LANES), F32)
    put_lanes(send_ref, jsrc, 16, applied)


def phi_next(own, isrc, jsrc, got_ref, mass_ref, w_ref, plan_ref, phi_ref, send_ref):
    total = jnp.sum(got_ref[...], axis=0)
    mass = mass_ref[...]
    phi = valid(own, -(mass[isrc:] + total) / mass[:isrc])
    phi_ref[...] = phi
    applied = apply_cols(own, isrc, phi, plan_ref)
    wts = valid(own, w_ref[...])
    wsum = jnp.sum(wts, axis=0, keepdims=True)
    wphi = jnp.sum(wts * phi, axis=0, keepdims=True)
    for s in range(jsrc):
        send_ref[s, 6:7, :] = wsum
        send_ref[s, 7:8, :] = wphi
    put_lanes(send_ref, jsrc, 0, applied)


def row_of(value, count):
    return jnp.concatenate([value[k : k + 1, :] for k in range(count)], axis=1)


def apply_rows(own, isrc, psi, plan_ref, send_ref):
    span = GROUP * own
    for t in range(isrc // GROUP):
        col = jnp.sum(plan_ref[t * span : (t + 1) * span, :] * psi, axis=1, keepdims=True)
        part = slots_of(col, own, GROUP)
        for s in range(isrc):
            send_ref[s, t * GROUP : (t + 1) * GROUP, :] = part


def psi_first(own, isrc, got_ref, plan_ref, col_ref, send_ref):
    total = jnp.sum(got_ref[...], axis=0)
    col_ref[...] = total[:16]
    count = plan_ref.shape[1] // LANES
    psi = row_of(-(total[8:16] + total[16:24]) / total[0:8], count)
    apply_rows(own, isrc, psi, plan_ref, send_ref)


def psi_next(own, isrc, got_ref, col_ref, plan_ref, send_ref, *psi_refs):
    total = jnp.sum(got_ref[...], axis=0)
    count = plan_ref.shape[1] // LANES
    psi = -(col_ref[8:16] + total) / col_ref[0:8]
    for ref in psi_refs:
        ref[...] = psi
    apply_rows(own, isrc, row_of(psi, count), plan_ref, send_ref)


def bit_of(axis, bit):
    return lax.rem(lax.shift_right_logical(lax.axis_index(axis), bit), 2)


def phi_last(own, width, isrc, jsrc, *refs):
    got_ref, mass_ref, w_ref, psi_ref, plan_ref, inner_ref, xi_ref = refs[:7]
    phi_ref, send_hbm, keep_ref, give_ref, send_ref, mixed_ref, acc_ref, sem = refs[7:]
    phi_next(own, isrc, jsrc, got_ref, mass_ref, w_ref, plan_ref, phi_ref, send_ref)
    sent = pltpu.make_async_copy(send_ref, send_hbm, sem)
    sent.start()
    cols = plan_ref.shape[1]
    psi = row_of(psi_ref[...], cols // LANES)
    span = GROUP * own
    for t in range(isrc // GROUP):
        at = slice(t * span, (t + 1) * span)
        col = column_of(phi_ref[t * GROUP : (t + 1) * GROUP, :], own, GROUP)
        plan = plan_ref[at, :]
        mixed_ref[0, at, :] = (plan * (inner_ref[at, :] + (col + psi))).astype(BF16)
        mixed_ref[1, at, :] = plan.astype(BF16)
    part = xi_ref[...]
    for q in range(2):
        term = lax.dot_general(mixed_ref[q], part, TN, preferred_element_type=F32)
        acc_ref[q * cols : (q + 1) * cols, :] = term
    scale = 1.0 / (width * EPS)
    mine = bit_of("z", 0)
    for q in range(2):
        for m in range(jsrc // 2):
            keep = pl.ds(pl.multiple_of(q * cols + (2 * m + mine) * own, own), own)
            give = pl.ds(pl.multiple_of(q * cols + (2 * m + 1 - mine) * own, own), own)
            first = q * (cols // 2) + m * own
            at = slice(first, first + own)
            keep_ref[at, :] = (acc_ref[keep, :] * scale).astype(BF16)
            give_ref[at, :] = (acc_ref[give, :] * scale).astype(BF16)
    sent.wait()


def halve_apart(own, keep_ref, got_ref, next_ref, right_ref, left_ref):
    count = keep_ref.shape[0] // (2 * own)
    mine = lax.shift_right_logical(lax.axis_index("z"), 1)

    def block(q, i):
        place = q * count + lax.rem(mine + i, count)
        at = pl.ds(pl.multiple_of(place * own, own), own)
        return keep_ref[at, :].astype(F32) + got_ref[at, :].astype(F32)

    for m in range(count // 2):
        at = slice(m * own, (m + 1) * own)
        for q in range(2):
            first = (q * (count // 2) + m) * own
            next_ref[first : first + own, :] = block(q, 2 * m)
        right_ref[at, :] = block(0, 2 * m + 1).astype(BF16)
        left_ref[at, :] = block(1, (2 * m + count - 1) % count).astype(BF16)


def halve_across(own, keep_ref, right_ref, left_ref, next_ref, send_ref):
    for q, got_ref in enumerate((right_ref, left_ref)):
        at = slice(q * own, (q + 1) * own)
        for m, ref in enumerate((next_ref, send_ref)):
            first = (2 * q + m) * own
            value = keep_ref[first : first + own, :] + got_ref[m * own : (m + 1) * own, :].astype(F32)
            ref[at, :] = value.astype(ref.dtype)


def finish_rows(own, width, isrc, every, *refs):
    got_ref, col_ref, phi_ref, psi_ref, bias_ref, xi_ref, pj_ref, after_ref = refs[:8]
    row_ref, gw_ref, delta_ref, xj_ref, gj_ref = refs[8:]
    jsrc = pj_ref.shape[0]
    span = GROUP * own
    for k in range(jsrc):
        xj_ref[k * own : (k + 1) * own, :] = pj_ref[k, 0:own, :]
        gj_ref[k * own : (k + 1) * own, :] = pj_ref[k, own : 2 * own, :]
    total = jnp.sum(got_ref[...], axis=0)
    cols = jsrc * own
    psi = -(col_ref[8:16] + total) / col_ref[0:8]
    delta = row_of(psi - psi_ref[...], cols // LANES)
    psi = row_of(psi, cols // LANES)
    jbias = row_of(bias_ref[isrc:], cols // LANES)
    rows = lax.broadcasted_iota(jnp.int32, (own, cols), 0)
    lanes = lax.broadcasted_iota(jnp.int32, (own, cols), 1)
    first = lax.axis_index("z") * own
    delta_ref[...] = jnp.sum(jnp.where(lanes == rows + first, delta, 0.0), axis=1, keepdims=True)
    wsum = jnp.sum(total[6:7], axis=1, keepdims=True)
    wphi = jnp.sum(total[7:8], axis=1, keepdims=True)
    gw_ref[...] = -(every / wsum) * (phi_ref[...] - wphi / wsum)
    scale = 1.0 / (width * EPS)
    xj = xj_ref[...]
    gj = gj_ref[...]
    for t in range(isrc // GROUP):
        group = slice(t * GROUP, (t + 1) * GROUP)
        col = column_of(phi_ref[group, :], own, GROUP)
        ibias = column_of(bias_ref[group, :], own, GROUP)
        part = xi_ref[t * span : (t + 1) * span, :]
        cross = lax.dot_general(part, xj, NT, preferred_element_type=F32)
        plan = jnp.exp(cross * scale + jbias + ibias)
        inner = lax.dot_general(part, gj, NT, preferred_element_type=F32)
        mixed = plan * (inner + (col + psi))
        qrow = jnp.sum(mixed, axis=1, keepdims=True)
        base = jnp.dot(plan.astype(BF16), gj, preferred_element_type=F32)
        term = jnp.dot(mixed.astype(BF16), xj, preferred_element_type=F32)
        term = base + (term - qrow * part.astype(F32)) * scale
        term = term.astype(BF16)
        for k in range(GROUP):
            row_ref[t * GROUP + k] = term[k * own : (k + 1) * own]


def total_up(own, rows_ref, keep_ref, got_ref, delta_ref, out_ref):
    acc = jnp.sum(rows_ref[...].astype(F32), axis=0)
    sums = keep_ref[...] + got_ref[...].astype(F32)
    out_ref[...] = (acc + (sums[:own] + delta_ref[...] * sums[own:])).astype(BF16)


def local(particles, cotangent, row_potential, col_potential, weights):
    own, width = particles.shape
    iaxes, jaxes = ("y", "row"), ("z",)
    ysrc, xsrc = lax.axis_size("y"), lax.axis_size("row")
    isrc, jsrc = ysrc * xsrc, lax.axis_size("z")
    rows, cols = isrc * own, jsrc * own

    def swap(value, axes):
        return lax.all_to_all(value, axes, 0, 0, tiled=True)

    def shift(value, axis, k):
        n = lax.axis_size(axis)
        return lax.ppermute(value, axis, [(i, (i + k) % n) for i in range(n)])

    def flip(value, bit):
        return lax.ppermute(value, "z", [(i, i ^ bit) for i in range(jsrc)])

    def call(body, micros, outs, *args, scratch=(), in_specs=None, out_specs=None, mib=12, hbm=()):
        return pl.pallas_call(
            body,
            out_shape=[(pltpu.HBM if n in hbm else jax.ShapeDtypeStruct)(s, d) for n, (s, d) in enumerate(outs)],
            in_specs=in_specs or whole(len(args)),
            out_specs=out_specs or whole(len(outs)),
            scratch_shapes=list(scratch),
            compiler_params=params(mib),
            cost_estimate=pl.CostEstimate(flops=int(micros * 1e9), bytes_accessed=1024, transcendentals=0),
        )(*args)

    anywhere = pl.BlockSpec(memory_space=pltpu.HBM)
    ipack, jpack = call(
        functools.partial(pack, own, width, jsrc),
        2,
        [((own + AUX, width), BF16), ((jsrc, 2 * own + AUX, width), BF16)],
        *[
            pltpu.with_memory_space_constraint(v, pltpu.HBM)
            for v in (
                particles,
                cotangent,
                row_potential.reshape(1, own),
                col_potential.reshape(1, own),
                weights.reshape(1, own),
            )
        ],
        scratch=[
            pltpu.VMEM((2 * own + AUX, width), BF16),
            pltpu.VMEM((2, AUX, width), F32),
            pltpu.VMEM((3, 1, own), BF16),
            pltpu.SemaphoreType.DMA((5,)),
            pltpu.SemaphoreType.DMA((jsrc,)),
        ],
        in_specs=[anywhere] * 5,
        out_specs=whole(1) + [anywhere],
        hbm=(1,),
    )
    jgot = swap(jpack, jaxes)
    near = [shift(ipack, "row", k) for k in range(1, xsrc)]
    (line,) = call(
        functools.partial(stack, own, xsrc), 1, [((xsrc * (own + AUX), width), BF16)], ipack, *near
    )
    igot = [line] + [shift(line, "y", k) for k in range(1, ysrc)]
    plan, inner, xi, wts, send, col_part, bias = call(
        functools.partial(build, own, width, isrc, jsrc),
        5,
        [
            ((rows, cols), F32),
            ((rows, cols), F32),
            ((rows, width), BF16),
            ((isrc, LANES), F32),
            ((isrc, 2 * isrc, LANES), F32),
            ((16, LANES), F32),
            ((isrc + 8, LANES), F32),
        ],
        *igot,
        jgot,
        scratch=[pltpu.VMEM((cols, width), BF16), pltpu.VMEM((cols, width), BF16)],
    )
    got = swap(send, iaxes)
    mass, send = call(
        functools.partial(phi_first, own, isrc, jsrc),
        1,
        [((2 * isrc, LANES), F32), ((jsrc, 24, LANES), F32)],
        got,
        col_part,
        plan,
    )
    got = swap(send, jaxes)
    col, send = call(
        functools.partial(psi_first, own, isrc),
        1,
        [((16, LANES), F32), ((isrc, isrc, LANES), F32)],
        got,
        plan,
    )
    for step in range(1, ITERS):
        got = swap(send, iaxes)
        if step < ITERS - 1:
            phi, send = call(
                functools.partial(phi_next, own, isrc, jsrc),
                1,
                [((isrc, LANES), F32), ((jsrc, 8, LANES), F32)],
                got,
                mass,
                wts,
                plan,
            )
            got = swap(send, jaxes)
            send, *kept = call(
                functools.partial(psi_next, own, isrc),
                1,
                [((isrc, isrc, LANES), F32)] + [((8, LANES), F32)] * (step == ITERS - 2),
                got,
                col,
                plan,
            )
    half = cols
    phi, send, keep, give = call(
        functools.partial(phi_last, own, width, isrc, jsrc),
        4,
        [((isrc, LANES), F32), ((jsrc, 8, LANES), F32), ((half, width), BF16), ((half, width), BF16)],
        got,
        mass,
        wts,
        *kept,
        plan,
        inner,
        xi,
        scratch=[
            pltpu.VMEM((jsrc, 8, LANES), F32),
            pltpu.VMEM((2, rows, cols), BF16),
            pltpu.VMEM((2 * cols, width), F32),
            pltpu.SemaphoreType.DMA,
        ],
        out_specs=whole(1) + [anywhere] + whole(2),
        hbm=(1,),
        mib=20,
    )
    send, give = lax.optimization_barrier((send, give))
    taken = flip(give, 1)
    got = swap(send, jaxes)
    keep, right, left = call(
        functools.partial(halve_apart, own),
        1,
        [((half // 2, width), F32), ((half // 4, width), BF16), ((half // 4, width), BF16)],
        keep,
        taken,
    )
    right, left = shift(right, "z", 2), shift(left, "z", jsrc - 2)
    row_send, gw, delta = call(
        functools.partial(finish_rows, own, width, isrc, float(isrc * jsrc * own)),
        4,
        [((isrc, own, width), BF16), ((isrc, LANES), F32), ((own, 1), F32)],
        got,
        col,
        phi,
        *kept,
        bias,
        xi,
        jgot,
        keep,
        scratch=[
            pltpu.VMEM((cols, width), BF16),
            pltpu.VMEM((cols, width), BF16),
        ],
        mib=24,
    )
    row_send, right, left = lax.optimization_barrier((row_send, right, left))
    keep, give = call(
        functools.partial(halve_across, own),
        1,
        [((half // 4, width), F32), ((half // 4, width), BF16)],
        keep,
        right,
        left,
    )
    taken = flip(give, 4)
    row_got = swap(row_send, iaxes)
    (grad,) = call(
        functools.partial(total_up, own), 1, [((own, width), BF16)], row_got, keep, taken, delta
    )
    mine = lax.axis_index("y") * xsrc + lax.axis_index("row")
    grad_weights = lax.dynamic_slice(gw, (mine, 0), (1, own)).reshape(own)
    return (grad, grad_weights)


def solution(mesh):
    filt, row, col = mesh.devices.shape
    split = Mesh(mesh.devices.reshape(filt, row, 8, col // 8), ("filt", "row", "z", "y"))
    spec = ("filt", "row", "z", "y")
    return jax.shard_map(
        local,
        mesh=split,
        in_specs=(P(spec, None), P(spec, None), P(spec), P(spec), P(spec)),
        out_specs=(P(spec, None), P(spec)),
        check_vma=False,
    )
```

```python
import functools

import jax
import jax.numpy as jnp
from jax import lax
from jax.experimental import pallas as pl
from jax.experimental.pallas import tpu as pltpu
from jax.sharding import Mesh
from jax.sharding import PartitionSpec as P

ITERS = 4


EPS = 0.09

LANES = 128
AUX = 8
F32 = jnp.float32
BF16 = jnp.bfloat16


def params(mib):
    return pltpu.CompilerParams(vmem_limit_bytes=mib << 20)


def whole(n):
    return [pl.BlockSpec(memory_space=pltpu.VMEM)] * n


def eye(own):
    rows = lax.broadcasted_iota(jnp.int32, (own, LANES), 0)
    lanes = lax.broadcasted_iota(jnp.int32, (own, LANES), 1)
    return rows == lanes


def to_row(col, own):
    return jnp.sum(jnp.where(eye(own), col, 0.0), axis=0, keepdims=True)


def to_col(row, own):
    return jnp.sum(jnp.where(eye(own), row, 0.0), axis=1, keepdims=True)


def lanes_of(col):
    out = []
    for k in range(col.shape[0] // LANES):
        out.append(to_row(col[k * LANES : (k + 1) * LANES], LANES))
    return jnp.concatenate(out, axis=1)


def slots_of(value, own, count):
    return jnp.concatenate([to_row(value[k * own : (k + 1) * own], own) for k in range(count)], axis=0)


def column_of(value, own, count):
    return jnp.concatenate([to_col(value[k : k + 1], own) for k in range(count)], axis=0)


def fold(block):
    return jnp.sum(block.reshape(block.shape[0] // 8, 8, block.shape[1]), axis=0)


def put_lanes(ref, slots, base, row):
    for k in range(row.shape[1] // LANES):
        piece = row[:, k * LANES : (k + 1) * LANES]
        for s in range(slots):
            ref[s, base + k : base + k + 1, :] = piece


def pack(own, width, jsrc, x_ref, gy_ref, f_ref, g_ref, w_ref, ipack_ref, jpack_ref, block_ref, line_ref, vec_ref, in_sem, out_sem):
    copies = [
        pltpu.make_async_copy(f_ref, vec_ref.at[0], in_sem.at[2]),
        pltpu.make_async_copy(w_ref, vec_ref.at[1], in_sem.at[3]),
        pltpu.make_async_copy(g_ref, vec_ref.at[2], in_sem.at[4]),
        pltpu.make_async_copy(x_ref, block_ref.at[pl.ds(0, own)], in_sem.at[0]),
        pltpu.make_async_copy(gy_ref, block_ref.at[pl.ds(own, own)], in_sem.at[1]),
    ]
    for copy in copies:
        copy.start()
    line_ref[...] = jnp.zeros_like(line_ref)
    for copy in copies:
        copy.wait()
    line_ref[0, 0:1, 0:own] = vec_ref[0].astype(F32)
    line_ref[0, 1:2, 0:own] = vec_ref[1].astype(F32)
    line_ref[1, 0:1, 0:own] = vec_ref[2].astype(F32)
    block_ref[2 * own : 2 * own + AUX, :] = line_ref[1].astype(BF16)
    outs = [pltpu.make_async_copy(block_ref, jpack_ref.at[s], out_sem.at[s]) for s in range(jsrc)]
    for copy in outs:
        copy.start()
    ipack_ref[0:own, :] = block_ref[0:own, :]
    ipack_ref[own : own + AUX, :] = line_ref[0].astype(BF16)
    for copy in outs:
        copy.wait()


def stack(own, count, *refs):
    out_ref = refs[count]
    size = own + AUX
    for k in range(count):
        place = behind("row", k, count)
        out_ref[pl.ds(pl.multiple_of(place * size, size), size), :] = refs[k][...]


GROUP = 4
NT = (((1,), (1,)), ((), ()))
TN = (((0,), (0,)), ((), ()))


def behind(axis, k, count):
    return lax.rem(lax.axis_index(axis) + (count - k), count)


def build(own, width, isrc, jsrc, *refs):
    steps = isrc // GROUP
    pi_refs, pj_ref = refs[:steps], refs[steps]
    plan_ref, inner_ref, xi_ref, w_ref, mass_ref, col_ref, bias_ref, xj_ref, gj_ref = refs[steps + 1 :]
    cols = jsrc * own
    size = own + AUX
    scale = 1.0 / (2.0 * width * EPS)
    bias = []
    for k in range(jsrc):
        part = pj_ref[k, 0:own, :]
        xj_ref[k * own : (k + 1) * own, :] = part
        gj_ref[k * own : (k + 1) * own, :] = pj_ref[k, own : 2 * own, :]
        pf = part.astype(F32)
        sq = jnp.sum(pf * pf, axis=1, keepdims=True)
        pot = to_col(pj_ref[k, 2 * own : 2 * own + AUX, :].astype(F32)[0:1, 0:LANES], own)
        bias.append(pot / EPS - sq * scale)
    jbias = lanes_of(jnp.concatenate(bias, axis=0))
    bias_ref[isrc : isrc + 8, :] = jnp.zeros((8, LANES), F32)
    for k in range(cols // LANES):
        bias_ref[isrc + k : isrc + k + 1, :] = jbias[:, k * LANES : (k + 1) * LANES]
    xj = xj_ref[...]
    gj = gj_ref[...]
    span = GROUP * own
    cmass = cph = None
    for m in range(steps):
        src = pi_refs[m]
        t = behind("y", m, steps)
        base = pl.multiple_of(t * span, span)
        first = pl.multiple_of(t * GROUP, GROUP)
        ibias = []
        for k in range(GROUP):
            part = src[k * size : k * size + own, :]
            xi_ref[pl.ds(pl.multiple_of(base + k * own, own), own), :] = part
            aux = src[k * size + own : (k + 1) * size, :].astype(F32)
            w_ref[pl.ds(first + k, 1), :] = aux[1:2, 0:LANES]
            pf = part.astype(F32)
            sq = jnp.sum(pf * pf, axis=1, keepdims=True)
            ibias.append(to_col(aux[0:1, 0:LANES], own) / EPS - sq * scale)
        ibias = jnp.concatenate(ibias, axis=0)
        lines = slots_of(ibias, own, GROUP)
        for k in range(GROUP):
            bias_ref[pl.ds(first + k, 1), :] = lines[k : k + 1]
        part = xi_ref[pl.ds(base, span), :]
        cross = lax.dot_general(part, xj, NT, preferred_element_type=F32)
        plan = jnp.exp(cross * (2.0 * scale) + jbias + ibias)
        plan_ref[pl.ds(base, span), :] = plan
        inner = lax.dot_general(part, gj, NT, preferred_element_type=F32)
        inner_ref[pl.ds(base, span), :] = inner
        weighted = plan * inner
        mass = slots_of(jnp.sum(plan, axis=1, keepdims=True), own, GROUP)
        ph = slots_of(jnp.sum(weighted, axis=1, keepdims=True), own, GROUP)
        for k in range(GROUP):
            mass_ref[0, pl.ds(first + k, 1), :] = mass[k : k + 1]
            mass_ref[0, pl.ds(isrc + first + k, 1), :] = ph[k : k + 1]
        plan, weighted = fold(plan), fold(weighted)
        cmass = plan if cmass is None else cmass + plan
        cph = weighted if cph is None else cph + weighted
    for s in range(1, isrc):
        mass_ref[s] = mass_ref[0]
    col_ref[...] = jnp.zeros_like(col_ref)
    cmass = jnp.sum(cmass, axis=0, keepdims=True)
    cph = jnp.sum(cph, axis=0, keepdims=True)
    for k in range(cols // LANES):
        col_ref[k : k + 1, :] = cmass[:, k * LANES : (k + 1) * LANES]
        col_ref[8 + k : 9 + k, :] = cph[:, k * LANES : (k + 1) * LANES]


def apply_cols(own, isrc, phi, plan_ref):
    span = GROUP * own
    acc = None
    for t in range(isrc // GROUP):
        col = column_of(phi[t * GROUP : (t + 1) * GROUP], own, GROUP)
        part = fold(plan_ref[t * span : (t + 1) * span, :] * col)
        acc = part if acc is None else acc + part
    return jnp.sum(acc, axis=0, keepdims=True)


def valid(own, value):
    lanes = lax.broadcasted_iota(jnp.int32, value.shape, 1)
    return jnp.where(lanes < own, value, 0.0)


def phi_first(own, isrc, jsrc, got_ref, col_ref, plan_ref, mass_ref, send_ref):
    total = jnp.sum(got_ref[...], axis=0)
    mass_ref[...] = total
    phi = valid(own, -total[isrc:] / total[:isrc])
    applied = apply_cols(own, isrc, phi, plan_ref)
    for s in range(jsrc):
        send_ref[s, 0:16, :] = col_ref[...]
        send_ref[s, 16:24, :] = jnp.zeros((8, LANES), F32)
    put_lanes(send_ref, jsrc, 16, applied)


def phi_next(own, isrc, jsrc, got_ref, mass_ref, w_ref, plan_ref, phi_ref, send_ref):
    total = jnp.sum(got_ref[...], axis=0)
    mass = mass_ref[...]
    phi = valid(own, -(mass[isrc:] + total) / mass[:isrc])
    phi_ref[...] = phi
    applied = apply_cols(own, isrc, phi, plan_ref)
    wts = valid(own, w_ref[...])
    wsum = jnp.sum(wts, axis=0, keepdims=True)
    wphi = jnp.sum(wts * phi, axis=0, keepdims=True)
    for s in range(jsrc):
        send_ref[s, 6:7, :] = wsum
        send_ref[s, 7:8, :] = wphi
    put_lanes(send_ref, jsrc, 0, applied)


def row_of(value, count):
    return jnp.concatenate([value[k : k + 1, :] for k in range(count)], axis=1)


def apply_rows(own, isrc, psi, plan_ref, send_ref):
    span = GROUP * own
    for t in range(isrc // GROUP):
        col = jnp.sum(plan_ref[t * span : (t + 1) * span, :] * psi, axis=1, keepdims=True)
        part = slots_of(col, own, GROUP)
        for s in range(isrc):
            send_ref[s, t * GROUP : (t + 1) * GROUP, :] = part


def psi_first(own, isrc, got_ref, plan_ref, col_ref, send_ref):
    total = jnp.sum(got_ref[...], axis=0)
    col_ref[...] = total[:16]
    count = plan_ref.shape[1] // LANES
    psi = row_of(-(total[8:16] + total[16:24]) / total[0:8], count)
    apply_rows(own, isrc, psi, plan_ref, send_ref)


def psi_next(own, isrc, got_ref, col_ref, plan_ref, send_ref, *psi_refs):
    total = jnp.sum(got_ref[...], axis=0)
    count = plan_ref.shape[1] // LANES
    psi = -(col_ref[8:16] + total) / col_ref[0:8]
    for ref in psi_refs:
        ref[...] = psi
    apply_rows(own, isrc, row_of(psi, count), plan_ref, send_ref)


def bit_of(axis, bit):
    return lax.rem(lax.shift_right_logical(lax.axis_index(axis), bit), 2)


def phi_last(own, width, isrc, jsrc, *refs):
    got_ref, mass_ref, w_ref, psi_ref, plan_ref, inner_ref, xi_ref = refs[:7]
    phi_ref, send_hbm, keep_ref, give_ref, send_ref, mixed_ref, acc_ref, sem = refs[7:]
    phi_next(own, isrc, jsrc, got_ref, mass_ref, w_ref, plan_ref, phi_ref, send_ref)
    sent = pltpu.make_async_copy(send_ref, send_hbm, sem)
    sent.start()
    cols = plan_ref.shape[1]
    psi = row_of(psi_ref[...], cols // LANES)
    span = GROUP * own
    for t in range(isrc // GROUP):
        at = slice(t * span, (t + 1) * span)
        col = column_of(phi_ref[t * GROUP : (t + 1) * GROUP, :], own, GROUP)
        plan = plan_ref[at, :]
        mixed_ref[0, at, :] = (plan * (inner_ref[at, :] + (col + psi))).astype(BF16)
        mixed_ref[1, at, :] = plan.astype(BF16)
    part = xi_ref[...]
    for q in range(2):
        term = lax.dot_general(mixed_ref[q], part, TN, preferred_element_type=F32)
        acc_ref[q * cols : (q + 1) * cols, :] = term
    scale = 1.0 / (width * EPS)
    mine = bit_of("z", 0)
    for q in range(2):
        for m in range(jsrc // 2):
            keep = pl.ds(pl.multiple_of(q * cols + (2 * m + mine) * own, own), own)
            give = pl.ds(pl.multiple_of(q * cols + (2 * m + 1 - mine) * own, own), own)
            first = q * (cols // 2) + m * own
            at = slice(first, first + own)
            keep_ref[at, :] = (acc_ref[keep, :] * scale).astype(BF16)
            give_ref[at, :] = (acc_ref[give, :] * scale).astype(BF16)
    sent.wait()


def halve_apart(own, keep_ref, got_ref, next_ref, right_ref, left_ref):
    count = keep_ref.shape[0] // (2 * own)
    mine = lax.shift_right_logical(lax.axis_index("z"), 1)

    def block(q, i):
        place = q * count + lax.rem(mine + i, count)
        at = pl.ds(pl.multiple_of(place * own, own), own)
        return keep_ref[at, :].astype(F32) + got_ref[at, :].astype(F32)

    for m in range(count // 2):
        at = slice(m * own, (m + 1) * own)
        for q in range(2):
            first = (q * (count // 2) + m) * own
            next_ref[first : first + own, :] = block(q, 2 * m)
        right_ref[at, :] = block(0, 2 * m + 1).astype(BF16)
        left_ref[at, :] = block(1, (2 * m + count - 1) % count).astype(BF16)


def halve_across(own, keep_ref, right_ref, left_ref, delta_ref, next_ref, send_ref):
    for m, ref in enumerate((next_ref, send_ref)):
        at = slice(m * own, (m + 1) * own)
        sums = keep_ref[at, :] + right_ref[at, :].astype(F32)
        fix = keep_ref[(2 + m) * own : (3 + m) * own, :] + left_ref[at, :].astype(F32)
        ref[...] = (sums + delta_ref[at, :] * fix).astype(ref.dtype)


def finish_rows(own, width, isrc, every, *refs):
    got_ref, col_ref, phi_ref, psi_ref, bias_ref, xi_ref, pj_ref, after_ref = refs[:8]
    row_ref, gw_ref, delta_ref, xj_ref, gj_ref = refs[8:]
    jsrc = pj_ref.shape[0]
    span = GROUP * own
    for k in range(jsrc):
        xj_ref[k * own : (k + 1) * own, :] = pj_ref[k, 0:own, :]
        gj_ref[k * own : (k + 1) * own, :] = pj_ref[k, own : 2 * own, :]
    total = jnp.sum(got_ref[...], axis=0)
    cols = jsrc * own
    psi = -(col_ref[8:16] + total) / col_ref[0:8]
    delta = row_of(psi - psi_ref[...], cols // LANES)
    psi = row_of(psi, cols // LANES)
    jbias = row_of(bias_ref[isrc:], cols // LANES)
    rows = lax.broadcasted_iota(jnp.int32, (own, cols), 0)
    lanes = lax.broadcasted_iota(jnp.int32, (own, cols), 1)
    for m in range(2):
        first = lax.rem(lax.axis_index("z") + m * (jsrc // 2), jsrc) * own
        column = jnp.sum(jnp.where(lanes == rows + first, delta, 0.0), axis=1, keepdims=True)
        delta_ref[m * own : (m + 1) * own, :] = column
    wsum = jnp.sum(total[6:7], axis=1, keepdims=True)
    wphi = jnp.sum(total[7:8], axis=1, keepdims=True)
    gw_ref[...] = -(every / wsum) * (phi_ref[...] - wphi / wsum)
    scale = 1.0 / (width * EPS)
    xj = xj_ref[...]
    gj = gj_ref[...]
    for t in range(isrc // GROUP):
        group = slice(t * GROUP, (t + 1) * GROUP)
        col = column_of(phi_ref[group, :], own, GROUP)
        ibias = column_of(bias_ref[group, :], own, GROUP)
        part = xi_ref[t * span : (t + 1) * span, :]
        cross = lax.dot_general(part, xj, NT, preferred_element_type=F32)
        plan = jnp.exp(cross * scale + jbias + ibias)
        inner = lax.dot_general(part, gj, NT, preferred_element_type=F32)
        mixed = plan * (inner + (col + psi))
        qrow = jnp.sum(mixed, axis=1, keepdims=True)
        base = jnp.dot(plan.astype(BF16), gj, preferred_element_type=F32)
        term = jnp.dot(mixed.astype(BF16), xj, preferred_element_type=F32)
        term = base + (term - qrow * part.astype(F32)) * scale
        term = term.astype(BF16)
        for k in range(GROUP):
            row_ref[t * GROUP + k] = term[k * own : (k + 1) * own]


def total_up(rows_ref, keep_ref, got_ref, out_ref):
    acc = jnp.sum(rows_ref[...].astype(F32), axis=0)
    out_ref[...] = (acc + (keep_ref[...] + got_ref[...].astype(F32))).astype(BF16)


def local(particles, cotangent, row_potential, col_potential, weights):
    own, width = particles.shape
    iaxes, jaxes = ("y", "row"), ("z",)
    ysrc, xsrc = lax.axis_size("y"), lax.axis_size("row")
    isrc, jsrc = ysrc * xsrc, lax.axis_size("z")
    rows, cols = isrc * own, jsrc * own

    def swap(value, axes):
        return lax.all_to_all(value, axes, 0, 0, tiled=True)

    def shift(value, axis, k):
        n = lax.axis_size(axis)
        return lax.ppermute(value, axis, [(i, (i + k) % n) for i in range(n)])

    def flip(value, bit):
        return lax.ppermute(value, "z", [(i, i ^ bit) for i in range(jsrc)])

    def call(body, micros, outs, *args, scratch=(), in_specs=None, out_specs=None, mib=12, hbm=()):
        return pl.pallas_call(
            body,
            out_shape=[(pltpu.HBM if n in hbm else jax.ShapeDtypeStruct)(s, d) for n, (s, d) in enumerate(outs)],
            in_specs=in_specs or whole(len(args)),
            out_specs=out_specs or whole(len(outs)),
            scratch_shapes=list(scratch),
            compiler_params=params(mib),
            cost_estimate=pl.CostEstimate(flops=int(micros * 1e9), bytes_accessed=1024, transcendentals=0),
        )(*args)

    anywhere = pl.BlockSpec(memory_space=pltpu.HBM)
    ipack, jpack = call(
        functools.partial(pack, own, width, jsrc),
        2,
        [((own + AUX, width), BF16), ((jsrc, 2 * own + AUX, width), BF16)],
        *[
            pltpu.with_memory_space_constraint(v, pltpu.HBM)
            for v in (
                particles,
                cotangent,
                row_potential.reshape(1, own),
                col_potential.reshape(1, own),
                weights.reshape(1, own),
            )
        ],
        scratch=[
            pltpu.VMEM((2 * own + AUX, width), BF16),
            pltpu.VMEM((2, AUX, width), F32),
            pltpu.VMEM((3, 1, own), BF16),
            pltpu.SemaphoreType.DMA((5,)),
            pltpu.SemaphoreType.DMA((jsrc,)),
        ],
        in_specs=[anywhere] * 5,
        out_specs=whole(1) + [anywhere],
        hbm=(1,),
    )
    jgot = swap(jpack, jaxes)
    near = [shift(ipack, "row", k) for k in range(1, xsrc)]
    (line,) = call(
        functools.partial(stack, own, xsrc), 1, [((xsrc * (own + AUX), width), BF16)], ipack, *near
    )
    igot = [line] + [shift(line, "y", k) for k in range(1, ysrc)]
    plan, inner, xi, wts, send, col_part, bias = call(
        functools.partial(build, own, width, isrc, jsrc),
        5,
        [
            ((rows, cols), F32),
            ((rows, cols), F32),
            ((rows, width), BF16),
            ((isrc, LANES), F32),
            ((isrc, 2 * isrc, LANES), F32),
            ((16, LANES), F32),
            ((isrc + 8, LANES), F32),
        ],
        *igot,
        jgot,
        scratch=[pltpu.VMEM((cols, width), BF16), pltpu.VMEM((cols, width), BF16)],
    )
    got = swap(send, iaxes)
    mass, send = call(
        functools.partial(phi_first, own, isrc, jsrc),
        1,
        [((2 * isrc, LANES), F32), ((jsrc, 24, LANES), F32)],
        got,
        col_part,
        plan,
    )
    got = swap(send, jaxes)
    col, send = call(
        functools.partial(psi_first, own, isrc),
        1,
        [((16, LANES), F32), ((isrc, isrc, LANES), F32)],
        got,
        plan,
    )
    for step in range(1, ITERS):
        got = swap(send, iaxes)
        if step < ITERS - 1:
            phi, send = call(
                functools.partial(phi_next, own, isrc, jsrc),
                1,
                [((isrc, LANES), F32), ((jsrc, 8, LANES), F32)],
                got,
                mass,
                wts,
                plan,
            )
            got = swap(send, jaxes)
            send, *kept = call(
                functools.partial(psi_next, own, isrc),
                1,
                [((isrc, isrc, LANES), F32)] + [((8, LANES), F32)] * (step == ITERS - 2),
                got,
                col,
                plan,
            )
    half = cols
    phi, send, keep, give = call(
        functools.partial(phi_last, own, width, isrc, jsrc),
        4,
        [((isrc, LANES), F32), ((jsrc, 8, LANES), F32), ((half, width), BF16), ((half, width), BF16)],
        got,
        mass,
        wts,
        *kept,
        plan,
        inner,
        xi,
        scratch=[
            pltpu.VMEM((jsrc, 8, LANES), F32),
            pltpu.VMEM((2, rows, cols), BF16),
            pltpu.VMEM((2 * cols, width), F32),
            pltpu.SemaphoreType.DMA,
        ],
        out_specs=whole(1) + [anywhere] + whole(2),
        hbm=(1,),
        mib=20,
    )
    send, give = lax.optimization_barrier((send, give))
    taken = flip(give, 1)
    got = swap(send, jaxes)
    keep, right, left = call(
        functools.partial(halve_apart, own),
        1,
        [((half // 2, width), F32), ((half // 4, width), BF16), ((half // 4, width), BF16)],
        keep,
        taken,
    )
    right, left = shift(right, "z", 2), shift(left, "z", jsrc - 2)
    row_send, gw, delta = call(
        functools.partial(finish_rows, own, width, isrc, float(isrc * jsrc * own)),
        4,
        [((isrc, own, width), BF16), ((isrc, LANES), F32), ((2 * own, 1), F32)],
        got,
        col,
        phi,
        *kept,
        bias,
        xi,
        jgot,
        keep,
        scratch=[
            pltpu.VMEM((cols, width), BF16),
            pltpu.VMEM((cols, width), BF16),
        ],
        mib=24,
    )
    row_send, right, left = lax.optimization_barrier((row_send, right, left))
    keep, give = call(
        functools.partial(halve_across, own),
        1,
        [((own, width), F32), ((own, width), BF16)],
        keep,
        right,
        left,
        delta,
    )
    taken = flip(give, 4)
    row_got = swap(row_send, iaxes)
    (grad,) = call(total_up, 1, [((own, width), BF16)], row_got, keep, taken)
    mine = lax.axis_index("y") * xsrc + lax.axis_index("row")
    grad_weights = lax.dynamic_slice(gw, (mine, 0), (1, own)).reshape(own)
    return (grad, grad_weights)


def solution(mesh):
    filt, row, col = mesh.devices.shape
    split = Mesh(mesh.devices.reshape(filt, row, 8, col // 8), ("filt", "row", "z", "y"))
    spec = ("filt", "row", "z", "y")
    return jax.shard_map(
        local,
        mesh=split,
        in_specs=(P(spec, None), P(spec, None), P(spec), P(spec), P(spec)),
        out_specs=(P(spec, None), P(spec)),
        check_vma=False,
    )
```

```python
import functools

import jax
import jax.numpy as jnp
from jax import lax
from jax.experimental import pallas as pl
from jax.experimental.pallas import tpu as pltpu
from jax.sharding import Mesh
from jax.sharding import PartitionSpec as P

ITERS = 4


EPS = 0.09

LANES = 128
AUX = 8
F32 = jnp.float32
BF16 = jnp.bfloat16


def params(mib):
    return pltpu.CompilerParams(vmem_limit_bytes=mib << 20)


def whole(n):
    return [pl.BlockSpec(memory_space=pltpu.VMEM)] * n


def eye(own):
    rows = lax.broadcasted_iota(jnp.int32, (own, LANES), 0)
    lanes = lax.broadcasted_iota(jnp.int32, (own, LANES), 1)
    return rows == lanes


def to_row(col, own):
    return jnp.sum(jnp.where(eye(own), col, 0.0), axis=0, keepdims=True)


def to_col(row, own):
    return jnp.sum(jnp.where(eye(own), row, 0.0), axis=1, keepdims=True)


def lanes_of(col):
    out = []
    for k in range(col.shape[0] // LANES):
        out.append(to_row(col[k * LANES : (k + 1) * LANES], LANES))
    return jnp.concatenate(out, axis=1)


def slots_of(value, own, count):
    return jnp.concatenate([to_row(value[k * own : (k + 1) * own], own) for k in range(count)], axis=0)


def column_of(value, own, count):
    return jnp.concatenate([to_col(value[k : k + 1], own) for k in range(count)], axis=0)


def fold(block):
    return jnp.sum(block.reshape(block.shape[0] // 8, 8, block.shape[1]), axis=0)


def put_lanes(ref, slots, base, row):
    for k in range(row.shape[1] // LANES):
        piece = row[:, k * LANES : (k + 1) * LANES]
        for s in range(slots):
            ref[s, base + k : base + k + 1, :] = piece


def pack(own, width, jsrc, x_ref, gy_ref, f_ref, g_ref, w_ref, ipack_ref, jpack_ref, line_ref, vec_ref, aux_ref, in_sem, out_sem):
    vectors = [pltpu.make_async_copy(ref, vec_ref.at[n], in_sem.at[n]) for n, ref in enumerate((g_ref, f_ref, w_ref))]
    mine = pltpu.make_async_copy(x_ref, ipack_ref.at[pl.ds(0, own)], in_sem.at[3])
    for copy in vectors:
        copy.start()
    outs = []
    for s in range(jsrc):
        for n, ref in enumerate((x_ref, gy_ref)):
            outs.append(pltpu.make_async_copy(ref, jpack_ref.at[s, pl.ds(n * own, own)], out_sem.at[3 * s + n]))
            outs[-1].start()
    mine.start()
    line_ref[...] = jnp.zeros_like(line_ref)
    for copy in vectors:
        copy.wait()
    line_ref[0, 0:1, 0:own] = vec_ref[0].astype(F32)
    aux_ref[...] = line_ref[0].astype(BF16)
    for s in range(jsrc):
        outs.append(pltpu.make_async_copy(aux_ref, jpack_ref.at[s, pl.ds(2 * own, AUX)], out_sem.at[3 * s + 2]))
        outs[-1].start()
    line_ref[1, 0:1, 0:own] = vec_ref[1].astype(F32)
    line_ref[1, 1:2, 0:own] = vec_ref[2].astype(F32)
    ipack_ref[own : own + AUX, :] = line_ref[1].astype(BF16)
    mine.wait()
    for copy in outs:
        copy.wait()


def stack(own, count, *refs):
    out_ref = refs[count]
    size = own + AUX
    for k in range(count):
        place = behind("row", k, count)
        out_ref[pl.ds(pl.multiple_of(place * size, size), size), :] = refs[k][...]


GROUP = 4
NT = (((1,), (1,)), ((), ()))
TN = (((0,), (0,)), ((), ()))


def behind(axis, k, count):
    return lax.rem(lax.axis_index(axis) + (count - k), count)


def build(own, width, isrc, jsrc, *refs):
    steps = isrc // GROUP
    pi_refs, pj_ref = refs[:steps], refs[steps]
    plan_ref, inner_ref, xi_ref, w_ref, mass_ref, col_ref, bias_ref, xj_ref, gj_ref = refs[steps + 1 :]
    cols = jsrc * own
    size = own + AUX
    scale = 1.0 / (2.0 * width * EPS)
    bias = []
    for k in range(jsrc):
        part = pj_ref[k, 0:own, :]
        xj_ref[k * own : (k + 1) * own, :] = part
        gj_ref[k * own : (k + 1) * own, :] = pj_ref[k, own : 2 * own, :]
        pf = part.astype(F32)
        sq = jnp.sum(pf * pf, axis=1, keepdims=True)
        pot = to_col(pj_ref[k, 2 * own : 2 * own + AUX, :].astype(F32)[0:1, 0:LANES], own)
        bias.append(pot / EPS - sq * scale)
    jbias = lanes_of(jnp.concatenate(bias, axis=0))
    bias_ref[isrc : isrc + 8, :] = jnp.zeros((8, LANES), F32)
    for k in range(cols // LANES):
        bias_ref[isrc + k : isrc + k + 1, :] = jbias[:, k * LANES : (k + 1) * LANES]
    xj = xj_ref[...]
    gj = gj_ref[...]
    span = GROUP * own
    cmass = cph = None
    for m in range(steps):
        src = pi_refs[m]
        t = behind("y", m, steps)
        base = pl.multiple_of(t * span, span)
        first = pl.multiple_of(t * GROUP, GROUP)
        ibias = []
        for k in range(GROUP):
            part = src[k * size : k * size + own, :]
            xi_ref[pl.ds(pl.multiple_of(base + k * own, own), own), :] = part
            aux = src[k * size + own : (k + 1) * size, :].astype(F32)
            w_ref[pl.ds(first + k, 1), :] = aux[1:2, 0:LANES]
            pf = part.astype(F32)
            sq = jnp.sum(pf * pf, axis=1, keepdims=True)
            ibias.append(to_col(aux[0:1, 0:LANES], own) / EPS - sq * scale)
        ibias = jnp.concatenate(ibias, axis=0)
        lines = slots_of(ibias, own, GROUP)
        for k in range(GROUP):
            bias_ref[pl.ds(first + k, 1), :] = lines[k : k + 1]
        part = xi_ref[pl.ds(base, span), :]
        cross = lax.dot_general(part, xj, NT, preferred_element_type=F32)
        plan = jnp.exp(cross * (2.0 * scale) + jbias + ibias)
        plan_ref[pl.ds(base, span), :] = plan
        inner = lax.dot_general(part, gj, NT, preferred_element_type=F32)
        inner_ref[pl.ds(base, span), :] = inner
        weighted = plan * inner
        mass = slots_of(jnp.sum(plan, axis=1, keepdims=True), own, GROUP)
        ph = slots_of(jnp.sum(weighted, axis=1, keepdims=True), own, GROUP)
        for k in range(GROUP):
            mass_ref[0, pl.ds(first + k, 1), :] = mass[k : k + 1]
            mass_ref[0, pl.ds(isrc + first + k, 1), :] = ph[k : k + 1]
        plan, weighted = fold(plan), fold(weighted)
        cmass = plan if cmass is None else cmass + plan
        cph = weighted if cph is None else cph + weighted
    for s in range(1, isrc):
        mass_ref[s] = mass_ref[0]
    col_ref[...] = jnp.zeros_like(col_ref)
    cmass = jnp.sum(cmass, axis=0, keepdims=True)
    cph = jnp.sum(cph, axis=0, keepdims=True)
    for k in range(cols // LANES):
        col_ref[k : k + 1, :] = cmass[:, k * LANES : (k + 1) * LANES]
        col_ref[8 + k : 9 + k, :] = cph[:, k * LANES : (k + 1) * LANES]


def apply_cols(own, isrc, phi, plan_ref):
    span = GROUP * own
    acc = None
    for t in range(isrc // GROUP):
        col = column_of(phi[t * GROUP : (t + 1) * GROUP], own, GROUP)
        part = fold(plan_ref[t * span : (t + 1) * span, :] * col)
        acc = part if acc is None else acc + part
    return jnp.sum(acc, axis=0, keepdims=True)


def valid(own, value):
    lanes = lax.broadcasted_iota(jnp.int32, value.shape, 1)
    return jnp.where(lanes < own, value, 0.0)


def phi_first(own, isrc, jsrc, got_ref, col_ref, plan_ref, mass_ref, send_ref):
    total = jnp.sum(got_ref[...], axis=0)
    mass_ref[...] = total
    phi = valid(own, -total[isrc:] / total[:isrc])
    applied = apply_cols(own, isrc, phi, plan_ref)
    for s in range(jsrc):
        send_ref[s, 0:16, :] = col_ref[...]
        send_ref[s, 16:24, :] = jnp.zeros((8, LANES), F32)
    put_lanes(send_ref, jsrc, 16, applied)


def phi_next(own, isrc, jsrc, got_ref, mass_ref, w_ref, plan_ref, phi_ref, send_ref):
    total = jnp.sum(got_ref[...], axis=0)
    mass = mass_ref[...]
    phi = valid(own, -(mass[isrc:] + total) / mass[:isrc])
    phi_ref[...] = phi
    applied = apply_cols(own, isrc, phi, plan_ref)
    wts = valid(own, w_ref[...])
    wsum = jnp.sum(wts, axis=0, keepdims=True)
    wphi = jnp.sum(wts * phi, axis=0, keepdims=True)
    for s in range(jsrc):
        send_ref[s, 6:7, :] = wsum
        send_ref[s, 7:8, :] = wphi
    put_lanes(send_ref, jsrc, 0, applied)


def row_of(value, count):
    return jnp.concatenate([value[k : k + 1, :] for k in range(count)], axis=1)


def apply_rows(own, isrc, psi, plan_ref, send_ref):
    span = GROUP * own
    for t in range(isrc // GROUP):
        col = jnp.sum(plan_ref[t * span : (t + 1) * span, :] * psi, axis=1, keepdims=True)
        part = slots_of(col, own, GROUP)
        for s in range(isrc):
            send_ref[s, t * GROUP : (t + 1) * GROUP, :] = part


def psi_first(own, isrc, got_ref, plan_ref, col_ref, send_ref):
    total = jnp.sum(got_ref[...], axis=0)
    col_ref[...] = total[:16]
    count = plan_ref.shape[1] // LANES
    psi = row_of(-(total[8:16] + total[16:24]) / total[0:8], count)
    apply_rows(own, isrc, psi, plan_ref, send_ref)


def psi_next(own, isrc, got_ref, col_ref, plan_ref, send_ref, *psi_refs):
    total = jnp.sum(got_ref[...], axis=0)
    count = plan_ref.shape[1] // LANES
    psi = -(col_ref[8:16] + total) / col_ref[0:8]
    for ref in psi_refs:
        ref[...] = psi
    apply_rows(own, isrc, row_of(psi, count), plan_ref, send_ref)


def bit_of(axis, bit):
    return lax.rem(lax.shift_right_logical(lax.axis_index(axis), bit), 2)


def phi_last(own, width, isrc, jsrc, *refs):
    got_ref, mass_ref, w_ref, psi_ref, plan_ref, inner_ref, xi_ref = refs[:7]
    phi_ref, send_hbm, keep_ref, give_ref, send_ref, mixed_ref, acc_ref, sem = refs[7:]
    phi_next(own, isrc, jsrc, got_ref, mass_ref, w_ref, plan_ref, phi_ref, send_ref)
    sent = pltpu.make_async_copy(send_ref, send_hbm, sem)
    sent.start()
    cols = plan_ref.shape[1]
    psi = row_of(psi_ref[...], cols // LANES)
    span = GROUP * own
    for t in range(isrc // GROUP):
        at = slice(t * span, (t + 1) * span)
        col = column_of(phi_ref[t * GROUP : (t + 1) * GROUP, :], own, GROUP)
        plan = plan_ref[at, :]
        mixed_ref[0, at, :] = (plan * (inner_ref[at, :] + (col + psi))).astype(BF16)
        mixed_ref[1, at, :] = plan.astype(BF16)
    part = xi_ref[...]
    for q in range(2):
        term = lax.dot_general(mixed_ref[q], part, TN, preferred_element_type=F32)
        acc_ref[q * cols : (q + 1) * cols, :] = term
    scale = 1.0 / (width * EPS)
    mine = bit_of("z", 0)
    for q in range(2):
        for m in range(jsrc // 2):
            keep = pl.ds(pl.multiple_of(q * cols + (2 * m + mine) * own, own), own)
            give = pl.ds(pl.multiple_of(q * cols + (2 * m + 1 - mine) * own, own), own)
            first = q * (cols // 2) + m * own
            at = slice(first, first + own)
            keep_ref[at, :] = (acc_ref[keep, :] * scale).astype(BF16)
            give_ref[at, :] = (acc_ref[give, :] * scale).astype(BF16)
    sent.wait()


def halve_apart(own, keep_ref, got_ref, next_ref, right_ref, left_ref):
    count = keep_ref.shape[0] // (2 * own)
    mine = lax.shift_right_logical(lax.axis_index("z"), 1)

    def block(q, i):
        place = q * count + lax.rem(mine + i, count)
        at = pl.ds(pl.multiple_of(place * own, own), own)
        return keep_ref[at, :].astype(F32) + got_ref[at, :].astype(F32)

    for m in range(count // 2):
        at = slice(m * own, (m + 1) * own)
        for q in range(2):
            first = (q * (count // 2) + m) * own
            next_ref[first : first + own, :] = block(q, 2 * m)
        right_ref[at, :] = block(0, 2 * m + 1).astype(BF16)
        left_ref[at, :] = block(1, (2 * m + count - 1) % count).astype(BF16)


def halve_across(own, keep_ref, right_ref, left_ref, delta_ref, next_ref, send_ref):
    for m, ref in enumerate((next_ref, send_ref)):
        at = slice(m * own, (m + 1) * own)
        sums = keep_ref[at, :] + right_ref[at, :].astype(F32)
        fix = keep_ref[(2 + m) * own : (3 + m) * own, :] + left_ref[at, :].astype(F32)
        ref[...] = (sums + delta_ref[at, :] * fix).astype(ref.dtype)


def finish_rows(own, width, isrc, every, *refs):
    got_ref, col_ref, phi_ref, psi_ref, bias_ref, xi_ref, pj_ref, after_ref = refs[:8]
    row_ref, gw_ref, delta_ref, xj_ref, gj_ref = refs[8:]
    jsrc = pj_ref.shape[0]
    span = GROUP * own
    for k in range(jsrc):
        xj_ref[k * own : (k + 1) * own, :] = pj_ref[k, 0:own, :]
        gj_ref[k * own : (k + 1) * own, :] = pj_ref[k, own : 2 * own, :]
    total = jnp.sum(got_ref[...], axis=0)
    cols = jsrc * own
    psi = -(col_ref[8:16] + total) / col_ref[0:8]
    delta = row_of(psi - psi_ref[...], cols // LANES)
    psi = row_of(psi, cols // LANES)
    jbias = row_of(bias_ref[isrc:], cols // LANES)
    rows = lax.broadcasted_iota(jnp.int32, (own, cols), 0)
    lanes = lax.broadcasted_iota(jnp.int32, (own, cols), 1)
    for m in range(2):
        first = lax.rem(lax.axis_index("z") + m * (jsrc // 2), jsrc) * own
        column = jnp.sum(jnp.where(lanes == rows + first, delta, 0.0), axis=1, keepdims=True)
        delta_ref[m * own : (m + 1) * own, :] = column
    wsum = jnp.sum(total[6:7], axis=1, keepdims=True)
    wphi = jnp.sum(total[7:8], axis=1, keepdims=True)
    gw_ref[...] = -(every / wsum) * (phi_ref[...] - wphi / wsum)
    scale = 1.0 / (width * EPS)
    xj = xj_ref[...]
    gj = gj_ref[...]
    for t in range(isrc // GROUP):
        group = slice(t * GROUP, (t + 1) * GROUP)
        col = column_of(phi_ref[group, :], own, GROUP)
        ibias = column_of(bias_ref[group, :], own, GROUP)
        part = xi_ref[t * span : (t + 1) * span, :]
        cross = lax.dot_general(part, xj, NT, preferred_element_type=F32)
        plan = jnp.exp(cross * scale + jbias + ibias)
        inner = lax.dot_general(part, gj, NT, preferred_element_type=F32)
        mixed = plan * (inner + (col + psi))
        qrow = jnp.sum(mixed, axis=1, keepdims=True)
        base = jnp.dot(plan.astype(BF16), gj, preferred_element_type=F32)
        term = jnp.dot(mixed.astype(BF16), xj, preferred_element_type=F32)
        term = base + (term - qrow * part.astype(F32)) * scale
        term = term.astype(BF16)
        for k in range(GROUP):
            row_ref[t * GROUP + k] = term[k * own : (k + 1) * own]


def total_up(rows_ref, keep_ref, got_ref, out_ref):
    acc = jnp.sum(rows_ref[...].astype(F32), axis=0)
    out_ref[...] = (acc + (keep_ref[...] + got_ref[...].astype(F32))).astype(BF16)


def local(particles, cotangent, row_potential, col_potential, weights):
    own, width = particles.shape
    iaxes, jaxes = ("y", "row"), ("z",)
    ysrc, xsrc = lax.axis_size("y"), lax.axis_size("row")
    isrc, jsrc = ysrc * xsrc, lax.axis_size("z")
    rows, cols = isrc * own, jsrc * own

    def swap(value, axes):
        return lax.all_to_all(value, axes, 0, 0, tiled=True)

    def shift(value, axis, k):
        n = lax.axis_size(axis)
        return lax.ppermute(value, axis, [(i, (i + k) % n) for i in range(n)])

    def flip(value, bit):
        return lax.ppermute(value, "z", [(i, i ^ bit) for i in range(jsrc)])

    def call(body, micros, outs, *args, scratch=(), in_specs=None, out_specs=None, mib=12, hbm=()):
        return pl.pallas_call(
            body,
            out_shape=[(pltpu.HBM if n in hbm else jax.ShapeDtypeStruct)(s, d) for n, (s, d) in enumerate(outs)],
            in_specs=in_specs or whole(len(args)),
            out_specs=out_specs or whole(len(outs)),
            scratch_shapes=list(scratch),
            compiler_params=params(mib),
            cost_estimate=pl.CostEstimate(flops=int(micros * 1e9), bytes_accessed=1024, transcendentals=0),
        )(*args)

    anywhere = pl.BlockSpec(memory_space=pltpu.HBM)
    ipack, jpack = call(
        functools.partial(pack, own, width, jsrc),
        2,
        [((own + AUX, width), BF16), ((jsrc, 2 * own + AUX, width), BF16)],
        *[
            pltpu.with_memory_space_constraint(v, pltpu.HBM)
            for v in (
                particles,
                cotangent,
                row_potential.reshape(1, own),
                col_potential.reshape(1, own),
                weights.reshape(1, own),
            )
        ],
        scratch=[
            pltpu.VMEM((2, AUX, width), F32),
            pltpu.VMEM((3, 1, own), BF16),
            pltpu.VMEM((AUX, width), BF16),
            pltpu.SemaphoreType.DMA((4,)),
            pltpu.SemaphoreType.DMA((3 * jsrc,)),
        ],
        in_specs=[anywhere] * 5,
        out_specs=whole(1) + [anywhere],
        hbm=(1,),
    )
    jgot = swap(jpack, jaxes)
    near = [shift(ipack, "row", k) for k in range(1, xsrc)]
    (line,) = call(
        functools.partial(stack, own, xsrc), 1, [((xsrc * (own + AUX), width), BF16)], ipack, *near
    )
    igot = [line] + [shift(line, "y", k) for k in range(1, ysrc)]
    plan, inner, xi, wts, send, col_part, bias = call(
        functools.partial(build, own, width, isrc, jsrc),
        5,
        [
            ((rows, cols), F32),
            ((rows, cols), F32),
            ((rows, width), BF16),
            ((isrc, LANES), F32),
            ((isrc, 2 * isrc, LANES), F32),
            ((16, LANES), F32),
            ((isrc + 8, LANES), F32),
        ],
        *igot,
        jgot,
        scratch=[pltpu.VMEM((cols, width), BF16), pltpu.VMEM((cols, width), BF16)],
    )
    got = swap(send, iaxes)
    mass, send = call(
        functools.partial(phi_first, own, isrc, jsrc),
        1,
        [((2 * isrc, LANES), F32), ((jsrc, 24, LANES), F32)],
        got,
        col_part,
        plan,
    )
    got = swap(send, jaxes)
    col, send = call(
        functools.partial(psi_first, own, isrc),
        1,
        [((16, LANES), F32), ((isrc, isrc, LANES), F32)],
        got,
        plan,
    )
    for step in range(1, ITERS):
        got = swap(send, iaxes)
        if step < ITERS - 1:
            phi, send = call(
                functools.partial(phi_next, own, isrc, jsrc),
                1,
                [((isrc, LANES), F32), ((jsrc, 8, LANES), F32)],
                got,
                mass,
                wts,
                plan,
            )
            got = swap(send, jaxes)
            send, *kept = call(
                functools.partial(psi_next, own, isrc),
                1,
                [((isrc, isrc, LANES), F32)] + [((8, LANES), F32)] * (step == ITERS - 2),
                got,
                col,
                plan,
            )
    half = cols
    phi, send, keep, give = call(
        functools.partial(phi_last, own, width, isrc, jsrc),
        4,
        [((isrc, LANES), F32), ((jsrc, 8, LANES), F32), ((half, width), BF16), ((half, width), BF16)],
        got,
        mass,
        wts,
        *kept,
        plan,
        inner,
        xi,
        scratch=[
            pltpu.VMEM((jsrc, 8, LANES), F32),
            pltpu.VMEM((2, rows, cols), BF16),
            pltpu.VMEM((2 * cols, width), F32),
            pltpu.SemaphoreType.DMA,
        ],
        out_specs=whole(1) + [anywhere] + whole(2),
        hbm=(1,),
        mib=20,
    )
    send, give = lax.optimization_barrier((send, give))
    taken = flip(give, 1)
    got = swap(send, jaxes)
    keep, right, left = call(
        functools.partial(halve_apart, own),
        1,
        [((half // 2, width), F32), ((half // 4, width), BF16), ((half // 4, width), BF16)],
        keep,
        taken,
    )
    right, left = shift(right, "z", 2), shift(left, "z", jsrc - 2)
    row_send, gw, delta = call(
        functools.partial(finish_rows, own, width, isrc, float(isrc * jsrc * own)),
        4,
        [((isrc, own, width), BF16), ((isrc, LANES), F32), ((2 * own, 1), F32)],
        got,
        col,
        phi,
        *kept,
        bias,
        xi,
        jgot,
        keep,
        scratch=[
            pltpu.VMEM((cols, width), BF16),
            pltpu.VMEM((cols, width), BF16),
        ],
        mib=24,
    )
    row_send, right, left = lax.optimization_barrier((row_send, right, left))
    keep, give = call(
        functools.partial(halve_across, own),
        1,
        [((own, width), F32), ((own, width), BF16)],
        keep,
        right,
        left,
        delta,
    )
    taken = flip(give, 4)
    row_got = swap(row_send, iaxes)
    (grad,) = call(total_up, 1, [((own, width), BF16)], row_got, keep, taken)
    mine = lax.axis_index("y") * xsrc + lax.axis_index("row")
    grad_weights = lax.dynamic_slice(gw, (mine, 0), (1, own)).reshape(own)
    return (grad, grad_weights)


def solution(mesh):
    filt, row, col = mesh.devices.shape
    split = Mesh(mesh.devices.reshape(filt, row, 8, col // 8), ("filt", "row", "z", "y"))
    spec = ("filt", "row", "z", "y")
    return jax.shard_map(
        local,
        mesh=split,
        in_specs=(P(spec, None), P(spec, None), P(spec), P(spec), P(spec)),
        out_specs=(P(spec, None), P(spec)),
        check_vma=False,
    )
```

```python
import functools

import jax
import jax.numpy as jnp
from jax import lax
from jax.experimental import pallas as pl
from jax.experimental.pallas import tpu as pltpu
from jax.sharding import Mesh
from jax.sharding import PartitionSpec as P

ITERS = 4


EPS = 0.09

LANES = 128
AUX = 8
F32 = jnp.float32
BF16 = jnp.bfloat16


def params(mib):
    return pltpu.CompilerParams(vmem_limit_bytes=mib << 20)


def whole(n):
    return [pl.BlockSpec(memory_space=pltpu.VMEM)] * n


def eye(own):
    rows = lax.broadcasted_iota(jnp.int32, (own, LANES), 0)
    lanes = lax.broadcasted_iota(jnp.int32, (own, LANES), 1)
    return rows == lanes


def to_row(col, own):
    return jnp.sum(jnp.where(eye(own), col, 0.0), axis=0, keepdims=True)


def to_col(row, own):
    return jnp.sum(jnp.where(eye(own), row, 0.0), axis=1, keepdims=True)


def lanes_of(col):
    out = []
    for k in range(col.shape[0] // LANES):
        out.append(to_row(col[k * LANES : (k + 1) * LANES], LANES))
    return jnp.concatenate(out, axis=1)


def slots_of(value, own, count):
    return jnp.concatenate([to_row(value[k * own : (k + 1) * own], own) for k in range(count)], axis=0)


def column_of(value, own, count):
    return jnp.concatenate([to_col(value[k : k + 1], own) for k in range(count)], axis=0)


def fold(block):
    return jnp.sum(block.reshape(block.shape[0] // 8, 8, block.shape[1]), axis=0)


def put_lanes(ref, slots, base, row):
    for k in range(row.shape[1] // LANES):
        piece = row[:, k * LANES : (k + 1) * LANES]
        for s in range(slots):
            ref[s, base + k : base + k + 1, :] = piece


def pack(own, width, jsrc, x_ref, gy_ref, f_ref, g_ref, w_ref, ipack_ref, jpack_ref, block_ref, line_ref, vec_ref, in_sem, out_sem):
    copies = [
        pltpu.make_async_copy(f_ref, vec_ref.at[0], in_sem.at[2]),
        pltpu.make_async_copy(w_ref, vec_ref.at[1], in_sem.at[3]),
        pltpu.make_async_copy(g_ref, vec_ref.at[2], in_sem.at[4]),
        pltpu.make_async_copy(x_ref, block_ref.at[pl.ds(0, own)], in_sem.at[0]),
        pltpu.make_async_copy(gy_ref, block_ref.at[pl.ds(own, own)], in_sem.at[1]),
    ]
    for copy in copies:
        copy.start()
    line_ref[...] = jnp.zeros_like(line_ref)
    for copy in copies:
        copy.wait()
    line_ref[0, 0:1, 0:own] = vec_ref[0].astype(F32)
    line_ref[0, 1:2, 0:own] = vec_ref[1].astype(F32)
    line_ref[1, 0:1, 0:own] = vec_ref[2].astype(F32)
    block_ref[2 * own : 2 * own + AUX, :] = line_ref[1].astype(BF16)
    outs = [pltpu.make_async_copy(block_ref, jpack_ref.at[s], out_sem.at[s]) for s in range(jsrc)]
    for copy in outs:
        copy.start()
    ipack_ref[0:own, :] = block_ref[0:own, :]
    ipack_ref[own : own + AUX, :] = line_ref[0].astype(BF16)
    for copy in outs:
        copy.wait()


def reach(count):
    return [0] + sorted(range(1, count), key=lambda k: -min(k, count - k))


def stack(own, count, *refs):
    out_ref = refs[count]
    size = own + AUX
    for k in range(count):
        place = behind("row", reach(count)[k], count)
        out_ref[pl.ds(pl.multiple_of(place * size, size), size), :] = refs[k][...]


GROUP = 4
NT = (((1,), (1,)), ((), ()))
TN = (((0,), (0,)), ((), ()))


def behind(axis, k, count):
    return lax.rem(lax.axis_index(axis) + (count - k), count)


def build(own, width, isrc, jsrc, *refs):
    steps = isrc // GROUP
    pi_refs, pj_ref = refs[:steps], refs[steps]
    plan_ref, inner_ref, xi_ref, w_ref, mass_ref, col_ref, bias_ref, xj_ref, gj_ref = refs[steps + 1 :]
    cols = jsrc * own
    size = own + AUX
    scale = 1.0 / (2.0 * width * EPS)
    bias = []
    for k in range(jsrc):
        part = pj_ref[k, 0:own, :]
        xj_ref[k * own : (k + 1) * own, :] = part
        gj_ref[k * own : (k + 1) * own, :] = pj_ref[k, own : 2 * own, :]
        pf = part.astype(F32)
        sq = jnp.sum(pf * pf, axis=1, keepdims=True)
        pot = to_col(pj_ref[k, 2 * own : 2 * own + AUX, :].astype(F32)[0:1, 0:LANES], own)
        bias.append(pot / EPS - sq * scale)
    jbias = lanes_of(jnp.concatenate(bias, axis=0))
    bias_ref[isrc : isrc + 8, :] = jnp.zeros((8, LANES), F32)
    for k in range(cols // LANES):
        bias_ref[isrc + k : isrc + k + 1, :] = jbias[:, k * LANES : (k + 1) * LANES]
    xj = xj_ref[...]
    gj = gj_ref[...]
    span = GROUP * own
    cmass = cph = None
    for m in range(steps):
        src = pi_refs[m]
        t = behind("y", reach(steps)[m], steps)
        base = pl.multiple_of(t * span, span)
        first = pl.multiple_of(t * GROUP, GROUP)
        ibias = []
        for k in range(GROUP):
            part = src[k * size : k * size + own, :]
            xi_ref[pl.ds(pl.multiple_of(base + k * own, own), own), :] = part
            aux = src[k * size + own : (k + 1) * size, :].astype(F32)
            w_ref[pl.ds(first + k, 1), :] = aux[1:2, 0:LANES]
            pf = part.astype(F32)
            sq = jnp.sum(pf * pf, axis=1, keepdims=True)
            ibias.append(to_col(aux[0:1, 0:LANES], own) / EPS - sq * scale)
        ibias = jnp.concatenate(ibias, axis=0)
        lines = slots_of(ibias, own, GROUP)
        for k in range(GROUP):
            bias_ref[pl.ds(first + k, 1), :] = lines[k : k + 1]
        part = xi_ref[pl.ds(base, span), :]
        cross = lax.dot_general(part, xj, NT, preferred_element_type=F32)
        plan = jnp.exp(cross * (2.0 * scale) + jbias + ibias)
        plan_ref[pl.ds(base, span), :] = plan
        inner = lax.dot_general(part, gj, NT, preferred_element_type=F32)
        inner_ref[pl.ds(base, span), :] = inner
        weighted = plan * inner
        mass = slots_of(jnp.sum(plan, axis=1, keepdims=True), own, GROUP)
        ph = slots_of(jnp.sum(weighted, axis=1, keepdims=True), own, GROUP)
        for k in range(GROUP):
            mass_ref[0, pl.ds(first + k, 1), :] = mass[k : k + 1]
            mass_ref[0, pl.ds(isrc + first + k, 1), :] = ph[k : k + 1]
        plan, weighted = fold(plan), fold(weighted)
        cmass = plan if cmass is None else cmass + plan
        cph = weighted if cph is None else cph + weighted
    for s in range(1, isrc):
        mass_ref[s] = mass_ref[0]
    col_ref[...] = jnp.zeros_like(col_ref)
    cmass = jnp.sum(cmass, axis=0, keepdims=True)
    cph = jnp.sum(cph, axis=0, keepdims=True)
    for k in range(cols // LANES):
        col_ref[k : k + 1, :] = cmass[:, k * LANES : (k + 1) * LANES]
        col_ref[8 + k : 9 + k, :] = cph[:, k * LANES : (k + 1) * LANES]


def apply_cols(own, isrc, phi, plan_ref):
    span = GROUP * own
    acc = None
    for t in range(isrc // GROUP):
        col = column_of(phi[t * GROUP : (t + 1) * GROUP], own, GROUP)
        part = fold(plan_ref[t * span : (t + 1) * span, :] * col)
        acc = part if acc is None else acc + part
    return jnp.sum(acc, axis=0, keepdims=True)


def valid(own, value):
    lanes = lax.broadcasted_iota(jnp.int32, value.shape, 1)
    return jnp.where(lanes < own, value, 0.0)


def phi_first(own, isrc, jsrc, got_ref, col_ref, plan_ref, mass_ref, send_ref):
    total = jnp.sum(got_ref[...], axis=0)
    mass_ref[...] = total
    phi = valid(own, -total[isrc:] / total[:isrc])
    applied = apply_cols(own, isrc, phi, plan_ref)
    for s in range(jsrc):
        send_ref[s, 0:16, :] = col_ref[...]
        send_ref[s, 16:24, :] = jnp.zeros((8, LANES), F32)
    put_lanes(send_ref, jsrc, 16, applied)


def phi_next(own, isrc, jsrc, got_ref, mass_ref, w_ref, plan_ref, phi_ref, send_ref):
    total = jnp.sum(got_ref[...], axis=0)
    mass = mass_ref[...]
    phi = valid(own, -(mass[isrc:] + total) / mass[:isrc])
    phi_ref[...] = phi
    applied = apply_cols(own, isrc, phi, plan_ref)
    wts = valid(own, w_ref[...])
    wsum = jnp.sum(wts, axis=0, keepdims=True)
    wphi = jnp.sum(wts * phi, axis=0, keepdims=True)
    for s in range(jsrc):
        send_ref[s, 6:7, :] = wsum
        send_ref[s, 7:8, :] = wphi
    put_lanes(send_ref, jsrc, 0, applied)


def row_of(value, count):
    return jnp.concatenate([value[k : k + 1, :] for k in range(count)], axis=1)


def apply_rows(own, isrc, psi, plan_ref, send_ref):
    span = GROUP * own
    for t in range(isrc // GROUP):
        col = jnp.sum(plan_ref[t * span : (t + 1) * span, :] * psi, axis=1, keepdims=True)
        part = slots_of(col, own, GROUP)
        for s in range(isrc):
            send_ref[s, t * GROUP : (t + 1) * GROUP, :] = part


def psi_first(own, isrc, got_ref, plan_ref, col_ref, send_ref):
    total = jnp.sum(got_ref[...], axis=0)
    col_ref[...] = total[:16]
    count = plan_ref.shape[1] // LANES
    psi = row_of(-(total[8:16] + total[16:24]) / total[0:8], count)
    apply_rows(own, isrc, psi, plan_ref, send_ref)


def psi_next(own, isrc, got_ref, col_ref, plan_ref, send_ref, *psi_refs):
    total = jnp.sum(got_ref[...], axis=0)
    count = plan_ref.shape[1] // LANES
    psi = -(col_ref[8:16] + total) / col_ref[0:8]
    for ref in psi_refs:
        ref[...] = psi
    apply_rows(own, isrc, row_of(psi, count), plan_ref, send_ref)


def bit_of(axis, bit):
    return lax.rem(lax.shift_right_logical(lax.axis_index(axis), bit), 2)


def phi_last(own, width, isrc, jsrc, *refs):
    got_ref, mass_ref, w_ref, psi_ref, plan_ref, inner_ref, xi_ref = refs[:7]
    phi_ref, send_hbm, keep_ref, give_ref, send_ref, mixed_ref, acc_ref, sem = refs[7:]
    phi_next(own, isrc, jsrc, got_ref, mass_ref, w_ref, plan_ref, phi_ref, send_ref)
    sent = pltpu.make_async_copy(send_ref, send_hbm, sem)
    sent.start()
    cols = plan_ref.shape[1]
    psi = row_of(psi_ref[...], cols // LANES)
    span = GROUP * own
    for t in range(isrc // GROUP):
        at = slice(t * span, (t + 1) * span)
        col = column_of(phi_ref[t * GROUP : (t + 1) * GROUP, :], own, GROUP)
        plan = plan_ref[at, :]
        mixed_ref[0, at, :] = (plan * (inner_ref[at, :] + (col + psi))).astype(BF16)
        mixed_ref[1, at, :] = plan.astype(BF16)
    part = xi_ref[...]
    for q in range(2):
        term = lax.dot_general(mixed_ref[q], part, TN, preferred_element_type=F32)
        acc_ref[q * cols : (q + 1) * cols, :] = term
    scale = 1.0 / (width * EPS)
    mine = bit_of("z", 0)
    for q in range(2):
        for m in range(jsrc // 2):
            keep = pl.ds(pl.multiple_of(q * cols + (2 * m + mine) * own, own), own)
            give = pl.ds(pl.multiple_of(q * cols + (2 * m + 1 - mine) * own, own), own)
            first = q * (cols // 2) + m * own
            at = slice(first, first + own)
            keep_ref[at, :] = (acc_ref[keep, :] * scale).astype(BF16)
            give_ref[at, :] = (acc_ref[give, :] * scale).astype(BF16)
    sent.wait()


def halve_apart(own, keep_ref, got_ref, next_ref, right_ref, left_ref):
    count = keep_ref.shape[0] // (2 * own)
    mine = lax.shift_right_logical(lax.axis_index("z"), 1)

    def block(q, i):
        place = q * count + lax.rem(mine + i, count)
        at = pl.ds(pl.multiple_of(place * own, own), own)
        return keep_ref[at, :].astype(F32) + got_ref[at, :].astype(F32)

    for m in range(count // 2):
        at = slice(m * own, (m + 1) * own)
        for q in range(2):
            first = (q * (count // 2) + m) * own
            next_ref[first : first + own, :] = block(q, 2 * m)
        right_ref[at, :] = block(0, 2 * m + 1).astype(BF16)
        left_ref[at, :] = block(1, (2 * m + count - 1) % count).astype(BF16)


def halve_across(own, keep_ref, right_ref, left_ref, delta_ref, next_ref, send_ref):
    for m, ref in enumerate((next_ref, send_ref)):
        at = slice(m * own, (m + 1) * own)
        sums = keep_ref[at, :] + right_ref[at, :].astype(F32)
        fix = keep_ref[(2 + m) * own : (3 + m) * own, :] + left_ref[at, :].astype(F32)
        ref[...] = (sums + delta_ref[at, :] * fix).astype(ref.dtype)


def finish_rows(own, width, isrc, every, *refs):
    got_ref, col_ref, phi_ref, psi_ref, bias_ref, xi_ref, pj_ref, after_ref = refs[:8]
    row_ref, gw_ref, delta_ref, xj_ref, gj_ref = refs[8:]
    jsrc = pj_ref.shape[0]
    span = GROUP * own
    for k in range(jsrc):
        xj_ref[k * own : (k + 1) * own, :] = pj_ref[k, 0:own, :]
        gj_ref[k * own : (k + 1) * own, :] = pj_ref[k, own : 2 * own, :]
    total = jnp.sum(got_ref[...], axis=0)
    cols = jsrc * own
    psi = -(col_ref[8:16] + total) / col_ref[0:8]
    delta = row_of(psi - psi_ref[...], cols // LANES)
    psi = row_of(psi, cols // LANES)
    jbias = row_of(bias_ref[isrc:], cols // LANES)
    rows = lax.broadcasted_iota(jnp.int32, (own, cols), 0)
    lanes = lax.broadcasted_iota(jnp.int32, (own, cols), 1)
    for m in range(2):
        first = lax.rem(lax.axis_index("z") + m * (jsrc // 2), jsrc) * own
        column = jnp.sum(jnp.where(lanes == rows + first, delta, 0.0), axis=1, keepdims=True)
        delta_ref[m * own : (m + 1) * own, :] = column
    wsum = jnp.sum(total[6:7], axis=1, keepdims=True)
    wphi = jnp.sum(total[7:8], axis=1, keepdims=True)
    gw_ref[...] = -(every / wsum) * (phi_ref[...] - wphi / wsum)
    scale = 1.0 / (width * EPS)
    xj = xj_ref[...]
    gj = gj_ref[...]
    for t in range(isrc // GROUP):
        group = slice(t * GROUP, (t + 1) * GROUP)
        col = column_of(phi_ref[group, :], own, GROUP)
        ibias = column_of(bias_ref[group, :], own, GROUP)
        part = xi_ref[t * span : (t + 1) * span, :]
        cross = lax.dot_general(part, xj, NT, preferred_element_type=F32)
        plan = jnp.exp(cross * scale + jbias + ibias)
        inner = lax.dot_general(part, gj, NT, preferred_element_type=F32)
        mixed = plan * (inner + (col + psi))
        qrow = jnp.sum(mixed, axis=1, keepdims=True)
        base = jnp.dot(plan.astype(BF16), gj, preferred_element_type=F32)
        term = jnp.dot(mixed.astype(BF16), xj, preferred_element_type=F32)
        term = base + (term - qrow * part.astype(F32)) * scale
        term = term.astype(BF16)
        for k in range(GROUP):
            row_ref[t * GROUP + k] = term[k * own : (k + 1) * own]


def total_up(rows_ref, keep_ref, got_ref, out_ref):
    acc = jnp.sum(rows_ref[...].astype(F32), axis=0)
    out_ref[...] = (acc + (keep_ref[...] + got_ref[...].astype(F32))).astype(BF16)


def local(particles, cotangent, row_potential, col_potential, weights):
    own, width = particles.shape
    iaxes, jaxes = ("y", "row"), ("z",)
    ysrc, xsrc = lax.axis_size("y"), lax.axis_size("row")
    isrc, jsrc = ysrc * xsrc, lax.axis_size("z")
    rows, cols = isrc * own, jsrc * own

    def swap(value, axes):
        return lax.all_to_all(value, axes, 0, 0, tiled=True)

    def shift(value, axis, k):
        n = lax.axis_size(axis)
        return lax.ppermute(value, axis, [(i, (i + k) % n) for i in range(n)])

    def flip(value, bit):
        return lax.ppermute(value, "z", [(i, i ^ bit) for i in range(jsrc)])

    def call(body, micros, outs, *args, scratch=(), in_specs=None, out_specs=None, mib=12, hbm=()):
        return pl.pallas_call(
            body,
            out_shape=[(pltpu.HBM if n in hbm else jax.ShapeDtypeStruct)(s, d) for n, (s, d) in enumerate(outs)],
            in_specs=in_specs or whole(len(args)),
            out_specs=out_specs or whole(len(outs)),
            scratch_shapes=list(scratch),
            compiler_params=params(mib),
            cost_estimate=pl.CostEstimate(flops=int(micros * 1e9), bytes_accessed=1024, transcendentals=0),
        )(*args)

    anywhere = pl.BlockSpec(memory_space=pltpu.HBM)
    ipack, jpack = call(
        functools.partial(pack, own, width, jsrc),
        2,
        [((own + AUX, width), BF16), ((jsrc, 2 * own + AUX, width), BF16)],
        *[
            pltpu.with_memory_space_constraint(v, pltpu.HBM)
            for v in (
                particles,
                cotangent,
                row_potential.reshape(1, own),
                col_potential.reshape(1, own),
                weights.reshape(1, own),
            )
        ],
        scratch=[
            pltpu.VMEM((2 * own + AUX, width), BF16),
            pltpu.VMEM((2, AUX, width), F32),
            pltpu.VMEM((3, 1, own), BF16),
            pltpu.SemaphoreType.DMA((5,)),
            pltpu.SemaphoreType.DMA((jsrc,)),
        ],
        in_specs=[anywhere] * 5,
        out_specs=whole(1) + [anywhere],
        hbm=(1,),
    )
    jgot = swap(jpack, jaxes)
    near = [shift(ipack, "row", k) for k in reach(xsrc)[1:]]
    (line,) = call(
        functools.partial(stack, own, xsrc), 1, [((xsrc * (own + AUX), width), BF16)], ipack, *near
    )
    igot = [line] + [shift(line, "y", k) for k in reach(ysrc)[1:]]
    plan, inner, xi, wts, send, col_part, bias = call(
        functools.partial(build, own, width, isrc, jsrc),
        5,
        [
            ((rows, cols), F32),
            ((rows, cols), F32),
            ((rows, width), BF16),
            ((isrc, LANES), F32),
            ((isrc, 2 * isrc, LANES), F32),
            ((16, LANES), F32),
            ((isrc + 8, LANES), F32),
        ],
        *igot,
        jgot,
        scratch=[pltpu.VMEM((cols, width), BF16), pltpu.VMEM((cols, width), BF16)],
    )
    got = swap(send, iaxes)
    mass, send = call(
        functools.partial(phi_first, own, isrc, jsrc),
        1,
        [((2 * isrc, LANES), F32), ((jsrc, 24, LANES), F32)],
        got,
        col_part,
        plan,
    )
    got = swap(send, jaxes)
    col, send = call(
        functools.partial(psi_first, own, isrc),
        1,
        [((16, LANES), F32), ((isrc, isrc, LANES), F32)],
        got,
        plan,
    )
    for step in range(1, ITERS):
        got = swap(send, iaxes)
        if step < ITERS - 1:
            phi, send = call(
                functools.partial(phi_next, own, isrc, jsrc),
                1,
                [((isrc, LANES), F32), ((jsrc, 8, LANES), F32)],
                got,
                mass,
                wts,
                plan,
            )
            got = swap(send, jaxes)
            send, *kept = call(
                functools.partial(psi_next, own, isrc),
                1,
                [((isrc, isrc, LANES), F32)] + [((8, LANES), F32)] * (step == ITERS - 2),
                got,
                col,
                plan,
            )
    half = cols
    phi, send, keep, give = call(
        functools.partial(phi_last, own, width, isrc, jsrc),
        4,
        [((isrc, LANES), F32), ((jsrc, 8, LANES), F32), ((half, width), BF16), ((half, width), BF16)],
        got,
        mass,
        wts,
        *kept,
        plan,
        inner,
        xi,
        scratch=[
            pltpu.VMEM((jsrc, 8, LANES), F32),
            pltpu.VMEM((2, rows, cols), BF16),
            pltpu.VMEM((2 * cols, width), F32),
            pltpu.SemaphoreType.DMA,
        ],
        out_specs=whole(1) + [anywhere] + whole(2),
        hbm=(1,),
        mib=20,
    )
    send, give = lax.optimization_barrier((send, give))
    taken = flip(give, 1)
    got = swap(send, jaxes)
    keep, right, left = call(
        functools.partial(halve_apart, own),
        1,
        [((half // 2, width), F32), ((half // 4, width), BF16), ((half // 4, width), BF16)],
        keep,
        taken,
    )
    right, left = shift(right, "z", 2), shift(left, "z", jsrc - 2)
    row_send, gw, delta = call(
        functools.partial(finish_rows, own, width, isrc, float(isrc * jsrc * own)),
        4,
        [((isrc, own, width), BF16), ((isrc, LANES), F32), ((2 * own, 1), F32)],
        got,
        col,
        phi,
        *kept,
        bias,
        xi,
        jgot,
        keep,
        scratch=[
            pltpu.VMEM((cols, width), BF16),
            pltpu.VMEM((cols, width), BF16),
        ],
        mib=24,
    )
    row_send, right, left = lax.optimization_barrier((row_send, right, left))
    keep, give = call(
        functools.partial(halve_across, own),
        1,
        [((own, width), F32), ((own, width), BF16)],
        keep,
        right,
        left,
        delta,
    )
    taken = flip(give, 4)
    row_got = swap(row_send, iaxes)
    (grad,) = call(total_up, 1, [((own, width), BF16)], row_got, keep, taken)
    mine = lax.axis_index("y") * xsrc + lax.axis_index("row")
    grad_weights = lax.dynamic_slice(gw, (mine, 0), (1, own)).reshape(own)
    return (grad, grad_weights)


def solution(mesh):
    filt, row, col = mesh.devices.shape
    split = Mesh(mesh.devices.reshape(filt, row, 8, col // 8), ("filt", "row", "z", "y"))
    spec = ("filt", "row", "z", "y")
    return jax.shard_map(
        local,
        mesh=split,
        in_specs=(P(spec, None), P(spec, None), P(spec), P(spec), P(spec)),
        out_specs=(P(spec, None), P(spec)),
        check_vma=False,
    )
```
